512 devices in a mesh: ctx: 64 (over z, y_hi, core), head: 8 (over x, y_lo).
Axes of the slice: x: 4, y: 8 (y_hi: 4, y_lo: 2; y = y_hi * 2 + y_lo), z: 8, core: 2. Of those that a mesh axis runs over, the one named last changes fastest.
Arguments:
- queries: bfloat16 [65536, 4096], P(('ctx', 'head')), may hold values from -5 to 5
- keys: bfloat16 [65536, 1024], P(('ctx', 'head')), may hold values from -5 to 5
- values: bfloat16 [65536, 1024], P(('ctx', 'head')), may hold values from -5 to 5
- grad_out: bfloat16 [65536, 4096], P(('ctx', 'head')), may hold values from -5 to 5
- delta: float32 [32, 65536], P(None, ('ctx', 'head')), may hold values from -10 to 10
- doc_lengths: int32 [256], replicated, may hold values from 1 to 2048, as said below
Outputs:
- grad_queries: bfloat16 [65536, 4096], P(('ctx', 'head'))
- grad_keys: bfloat16 [65536, 1024], P(('ctx', 'head'))
- grad_values: bfloat16 [65536, 1024], P(('ctx', 'head'))
The draws below stay inside these ranges and needn't reach their ends.
Inputs may be any that keep to these rules, and one draw needn't show every extreme that they name: `doc_lengths`: the lengths are positive and sum to 65536; no document is longer than 2048. Exactly five are 2048 long. With shards of 1024 tokens and c the shard count, they begin in the second half of shard 0, of shard c / 2 - 3, of shard c / 2 - 1, of shard c / 2 + 1, and of shard c - 3.
All inputs are finite; a program needn't handle non-finite values.
Results may differ from the reference program's by a relative error of at most 0.005.
Values may be sent and summed in bfloat16 or wider, within the bound.
A program may use at most 64 MiB of HBM per device.

```python
import jax
import jax.numpy as jnp
from jax import lax

HEADS = 32
KV_HEADS = 8
HEAD_DIM = 128
QBLK = 256
ROWS_CTX = 1024
TOKENS = 65536
MOST = 2048
DOCS = 256


def draw_pair(key):
    base_key = jax.random.fold_in(key, 11)
    key_query, key_key = jax.random.split(base_key, 2)
    query_vals = jnp.clip(jax.random.normal(key_query, (TOKENS, HEADS * HEAD_DIM)), -4.0, 4.0)
    key_vals = jnp.clip(jax.random.normal(key_key, (TOKENS, KV_HEADS * HEAD_DIM)), -4.0, 4.0)
    return (query_vals.astype(jnp.float32), key_vals.astype(jnp.float32))


def draw_queries(key, part):
    return draw_pair(key)[0].astype(jnp.bfloat16)


def draw_keys(key, part):
    return draw_pair(key)[1].astype(jnp.bfloat16)


def fill_lengths(key, total, count):
    weights = jax.random.randint(key, (count,), 48, 65).astype(jnp.int32)
    weight_sum = jnp.sum(weights).astype(jnp.int32)
    extra = (total - count).astype(jnp.int32)
    shares = extra * weights // weight_sum
    leftover = extra - jnp.sum(shares).astype(jnp.int32)
    slots = jnp.arange(count, dtype=jnp.int32)
    return (1 + shares + (slots < leftover).astype(jnp.int32)).astype(jnp.int32)


def draw_doc_lengths(key, part):
    base_key = jax.random.fold_in(key, 23)
    key_first, key_alpha, key_beta, key_gamma, key_fourth, key_left, key_right = jax.random.split(base_key, 7)
    shard_rows = ROWS_CTX
    shard_count = TOKENS // ROWS_CTX
    middle = shard_count // 2
    first_off = jax.random.randint(key_first, (), shard_rows // 2, shard_rows).astype(jnp.int32)
    alpha_off = jax.random.randint(key_alpha, (), shard_rows // 2, shard_rows * 5 // 8).astype(jnp.int32)
    beta_off = jax.random.randint(key_beta, (), shard_rows * 5 // 8, shard_rows * 3 // 4).astype(jnp.int32)
    gamma_off = jax.random.randint(key_gamma, (), shard_rows * 3 // 4, shard_rows).astype(jnp.int32)
    fourth_off = jax.random.randint(key_fourth, (), shard_rows // 2, shard_rows).astype(jnp.int32)
    left_total = (middle - 3) * shard_rows + alpha_off - (2 * shard_rows + first_off)
    gap_one = beta_off - alpha_off
    gap_two = gamma_off - beta_off
    right_total = (shard_count - 3) * shard_rows + fourth_off - ((middle + 3) * shard_rows + gamma_off)
    tail = shard_rows - fourth_off
    spare = DOCS - 9
    left_count = max(1, spare * (middle - 5) // (shard_count - 11))
    right_count = spare - left_count
    left_docs = fill_lengths(key_left, left_total, left_count)
    right_docs = fill_lengths(key_right, right_total, right_count)
    longest = jnp.full((1,), MOST, jnp.int32)
    return jnp.concatenate([first_off[None], longest, left_docs, longest, gap_one[None], longest, gap_two[None], longest, right_docs, longest, tail[None]]).astype(jnp.int32)


def shard_levels(stream_key, shape, cuts, least, largest):
    factor_of = 1.0
    for dim, parts in cuts:
        heights = jax.random.uniform(jax.random.fold_in(jax.random.fold_in(stream_key, 6), dim), (parts,), jnp.float32, least / len(cuts), largest / len(cuts))
        factor_of = factor_of * jnp.repeat(jnp.exp(heights), shape[dim] // parts).reshape((-1,) + (1,) * (len(shape) - 1 - dim))
    return factor_of


def centred(own_key, shape, width, limit, shards=(), kind=jnp.bfloat16):
    entries = jax.random.normal(own_key, shape, jnp.float32) * width
    if len(shards) > 0:
        entries = shard_levels(own_key, shape, shards, -0.22, 0.18) * entries
    return jnp.clip(entries, min=-limit, max=limit).astype(kind)


def setup_inputs(seed: int = 0) -> dict:
    arg_keys = jax.random.split(jax.random.key(seed), 7)
    return {
        "queries": draw_queries(jax.random.fold_in(arg_keys[6], 71), 0),
        "keys": draw_keys(jax.random.fold_in(arg_keys[6], 71), 0),
        "values": centred(arg_keys[2], (TOKENS, KV_HEADS * HEAD_DIM), 1.0, 5.0, ((0, 512),)),
        "grad_out": centred(arg_keys[3], (TOKENS, HEADS * HEAD_DIM), 1.0, 5.0, ((0, 512),)),
        "delta": centred(arg_keys[4], (HEADS, TOKENS), 2.0, 10.0, ((1, 512),), jnp.float32),
        "doc_lengths": draw_doc_lengths(jax.random.fold_in(arg_keys[6], 71), 0),
    }


NEG_FILL = -1e30


def reference(queries, keys, values, grad_out, delta, doc_lengths):
    att_scale = HEAD_DIM ** -0.5
    group_size = HEADS // KV_HEADS
    window = MOST + QBLK
    doc_ends = jnp.cumsum(doc_lengths).astype(jnp.int32)
    positions = jnp.arange(TOKENS, dtype=jnp.int32)
    doc_ids = jnp.sum((doc_ends[None, :] <= positions[:, None]).astype(jnp.int32), axis=1).astype(jnp.int32)
    pad_keys = jnp.concatenate([jnp.zeros((MOST, KV_HEADS * HEAD_DIM), keys.dtype), keys], axis=0)
    pad_vals = jnp.concatenate([jnp.zeros((MOST, KV_HEADS * HEAD_DIM), values.dtype), values], axis=0)
    pad_docs = jnp.concatenate([jnp.full((MOST,), -1, jnp.int32), doc_ids], axis=0)
    pad_pos = jnp.arange(TOKENS + MOST, dtype=jnp.int32) - MOST

    def per_block(carry, block):
        acc_keys, acc_vals = carry
        start = (block * QBLK).astype(jnp.int32)
        q_rows = lax.dynamic_slice_in_dim(queries, start, QBLK, 0).astype(jnp.float32).reshape(QBLK, KV_HEADS, group_size, HEAD_DIM)
        g_rows = lax.dynamic_slice_in_dim(grad_out, start, QBLK, 0).astype(jnp.float32).reshape(QBLK, KV_HEADS, group_size, HEAD_DIM)
        d_rows = lax.dynamic_slice_in_dim(delta, start, QBLK, 1).reshape(KV_HEADS, group_size, QBLK)
        key_win = lax.dynamic_slice_in_dim(pad_keys, start, window, 0).astype(jnp.float32).reshape(window, KV_HEADS, HEAD_DIM)
        val_win = lax.dynamic_slice_in_dim(pad_vals, start, window, 0).astype(jnp.float32).reshape(window, KV_HEADS, HEAD_DIM)
        q_pos = lax.dynamic_slice_in_dim(positions, start, QBLK, 0)
        q_doc = lax.dynamic_slice_in_dim(doc_ids, start, QBLK, 0)
        k_pos = lax.dynamic_slice_in_dim(pad_pos, start, window, 0)
        k_doc = lax.dynamic_slice_in_dim(pad_docs, start, window, 0)
        allowed = (k_doc[None, :] == q_doc[:, None]) & (k_pos[None, :] <= q_pos[:, None]) & (k_pos[None, :] >= 0)
        scores = jnp.einsum('qkgd,wkd->kgqw', q_rows, key_win) * att_scale
        scores = jnp.where(allowed[None, None], scores, NEG_FILL)
        row_max = jnp.max(scores, axis=3, keepdims=True)
        log_total = row_max + jnp.log(jnp.sum(jnp.exp(scores - row_max), axis=3, keepdims=True))
        probs = jnp.where(allowed[None, None], jnp.exp(scores - log_total), 0.0)
        probs_low = lax.optimization_barrier(probs.astype(jnp.bfloat16)).astype(jnp.float32)
        grad_probs = jnp.einsum('qkgd,wkd->kgqw', g_rows, val_win)
        grad_scores = probs * (grad_probs - d_rows[:, :, :, None])
        grad_scores = lax.optimization_barrier(grad_scores.astype(jnp.bfloat16)).astype(jnp.float32)
        dq_rows = jnp.einsum('kgqw,wkd->qkgd', grad_scores, key_win).reshape(QBLK, HEADS * HEAD_DIM)
        key_part = jnp.einsum('kgqw,qkgd->wkd', grad_scores, q_rows).reshape(window, KV_HEADS * HEAD_DIM)
        val_part = jnp.einsum('kgqw,qkgd->wkd', probs_low, g_rows).reshape(window, KV_HEADS * HEAD_DIM)
        acc_keys = lax.dynamic_update_slice_in_dim(acc_keys, lax.dynamic_slice_in_dim(acc_keys, start, window, 0) + key_part, start, 0)
        acc_vals = lax.dynamic_update_slice_in_dim(acc_vals, lax.dynamic_slice_in_dim(acc_vals, start, window, 0) + val_part, start, 0)
        return (acc_keys, acc_vals), (dq_rows * att_scale).astype(jnp.bfloat16)

    zero_acc = jnp.zeros((TOKENS + MOST, KV_HEADS * HEAD_DIM), jnp.float32)
    (acc_keys, acc_vals), dq_blocks = lax.scan(per_block, (zero_acc, zero_acc), jnp.arange(TOKENS // QBLK, dtype=jnp.int32))
    grad_queries = dq_blocks.reshape(TOKENS, HEADS * HEAD_DIM)
    grad_keys = (acc_keys[MOST:] * att_scale).astype(jnp.bfloat16)
    grad_values = acc_vals[MOST:].astype(jnp.bfloat16)
    return (grad_queries, grad_keys, grad_values)
```

```python
import jax
import jax.numpy as jnp
from jax import lax
from jax.sharding import PartitionSpec as P

HEAD_DIM = 128
QBLK = 256
KBLK = 256


NEG_FILL = -1e30


def passed_along(block, axis, distance):
    devices = range(lax.axis_size(axis))
    route = [(i - distance, i) for i in devices if i - distance in devices]
    return lax.ppermute(block, axis, route)


def doc_index(positions, doc_ends):
    return jnp.sum((doc_ends[None, :] <= positions[:, None]).astype(jnp.int32), axis=1)


def contract_first(left, right):
    return lax.dot_general(
        left, right, (((0,), (0,)), ((), ())), preferred_element_type=jnp.float32
    )


def contract_last(left, right):
    return lax.dot_general(
        left, right, (((1,), (1,)), ((), ())), preferred_element_type=jnp.float32
    )


def block_grads(
    q_rows,
    g_rows,
    d_rows,
    q_position,
    q_doc,
    first_start,
    win_keys,
    win_vals,
    win_pos,
    win_doc,
    acc_keys,
    acc_vals,
):
    n_tiles = win_keys.shape[0] // KBLK
    q_last = jnp.max(q_position)
    att_scale = HEAD_DIM ** (-0.5)
    row_count = q_rows.shape[0]

    def tile_live(tile_index):
        k_first = win_pos[0] + tile_index * KBLK
        return (k_first <= q_last) & (k_first + KBLK - 1 >= first_start)

    def tile_scores(tile_index):
        start = tile_index * KBLK
        key_tile = lax.dynamic_slice_in_dim(win_keys, start, KBLK, 0)
        k_position = lax.dynamic_slice_in_dim(win_pos, start, KBLK, 0)
        k_doc = lax.dynamic_slice_in_dim(win_doc, start, KBLK, 0)
        scores = contract_last(q_rows, key_tile) * att_scale
        allowed = (
            (k_doc[None, :] == q_doc[:, None])
            & (k_position[None, :] <= q_position[:, None])
            & (k_position[None, :] >= 0)
        )
        return (jnp.where(allowed, scores, NEG_FILL), allowed, key_tile, start)

    def stats_step(tile_index, carry):

        def stats_update(state):
            row_max, row_sum = state
            scores = tile_scores(tile_index)[0]
            new_max = jnp.maximum(row_max, jnp.max(scores, axis=1))
            row_sum = row_sum * jnp.exp(row_max - new_max) + jnp.sum(
                jnp.exp(scores - new_max[:, None]), axis=1
            )
            return (new_max, row_sum)

        return lax.cond(tile_live(tile_index), stats_update, lambda state: state, carry)

    start_stats = (
        jnp.full((row_count,), NEG_FILL, jnp.float32),
        jnp.zeros((row_count,), jnp.float32),
    )
    row_max, row_sum = lax.fori_loop(0, n_tiles, stats_step, start_stats)
    log_total = row_max + jnp.log(row_sum)

    def grad_step(tile_index, carry):

        def grad_update(state):
            dq_acc, key_acc, val_acc = state
            scores, allowed, key_tile, start = tile_scores(tile_index)
            val_tile = lax.dynamic_slice_in_dim(win_vals, start, KBLK, 0)
            probs = jnp.where(allowed, jnp.exp(scores - log_total[:, None]), 0.0)
            probs_low = probs.astype(jnp.bfloat16)
            grad_probs = contract_last(g_rows, val_tile)
            grad_scores = (probs * (grad_probs - d_rows[:, None])).astype(jnp.bfloat16)
            dq_acc = dq_acc + jnp.dot(grad_scores, key_tile, preferred_element_type=jnp.float32)
            key_part = contract_first(grad_scores, q_rows)
            val_part = contract_first(probs_low, g_rows)
            key_acc = lax.dynamic_update_slice_in_dim(
                key_acc, lax.dynamic_slice_in_dim(key_acc, start, KBLK, 0) + key_part, start, 0
            )
            val_acc = lax.dynamic_update_slice_in_dim(
                val_acc, lax.dynamic_slice_in_dim(val_acc, start, KBLK, 0) + val_part, start, 0
            )
            return (dq_acc, key_acc, val_acc)

        return lax.cond(tile_live(tile_index), grad_update, lambda state: state, carry)

    start_grads = (jnp.zeros((row_count, HEAD_DIM), jnp.float32), acc_keys, acc_vals)
    return lax.fori_loop(0, n_tiles, grad_step, start_grads)


def on_device(queries, keys, values, grad_out, delta, doc_lengths):
    q_local, k_local, v_local, g_local = (
        lax.all_to_all(queries, "head", split_axis=1, concat_axis=0, tiled=True),
        lax.all_to_all(keys, "head", split_axis=1, concat_axis=0, tiled=True),
        lax.all_to_all(values, "head", split_axis=1, concat_axis=0, tiled=True),
        lax.all_to_all(grad_out, "head", split_axis=1, concat_axis=0, tiled=True),
    )
    d_local = lax.all_to_all(delta, "head", split_axis=0, concat_axis=1, tiled=True)
    ctx_rows = q_local.shape[0]
    kv_local = k_local.shape[1] // HEAD_DIM
    heads_local = q_local.shape[1] // HEAD_DIM
    group_size = heads_local // kv_local
    near_keys, near_vals = passed_along((k_local, v_local), "ctx", 1)
    far_keys, far_vals = passed_along((k_local, v_local), "ctx", 2)
    win_keys = jnp.concatenate([far_keys, near_keys, k_local], axis=0)
    win_vals = jnp.concatenate([far_vals, near_vals, v_local], axis=0)
    base_pos = lax.axis_index("ctx") * ctx_rows
    win_pos = base_pos - 2 * ctx_rows + jnp.arange(3 * ctx_rows, dtype=jnp.int32)
    slots = jnp.arange(doc_lengths.shape[0], dtype=jnp.int32)
    doc_ends = jnp.sum(jnp.where(slots[:, None] <= slots[None, :], doc_lengths[:, None], 0), axis=0)
    doc_starts = doc_ends - doc_lengths
    win_doc = doc_index(win_pos, doc_ends)
    q_pos_all = base_pos + jnp.arange(ctx_rows, dtype=jnp.int32)
    q_doc_all = doc_index(q_pos_all, doc_ends)
    block_count = ctx_rows // QBLK
    q_four = q_local.reshape(ctx_rows, kv_local, group_size, HEAD_DIM)
    g_four = g_local.reshape(ctx_rows, kv_local, group_size, HEAD_DIM)
    d_three = d_local.reshape(kv_local, group_size, ctx_rows)
    q_head = q_four[:, 0]
    g_head = g_four[:, 0]
    d_head = d_three[0]

    def per_block(carry, block):
        acc_keys, acc_vals = carry
        block_first = block * QBLK
        q_rows = jnp.swapaxes(lax.dynamic_slice_in_dim(q_head, block_first, QBLK, 0), 0, 1).reshape(
            group_size * QBLK, HEAD_DIM
        )
        g_rows = jnp.swapaxes(lax.dynamic_slice_in_dim(g_head, block_first, QBLK, 0), 0, 1).reshape(
            group_size * QBLK, HEAD_DIM
        )
        d_rows = lax.dynamic_slice_in_dim(d_head, block_first, QBLK, 1).reshape(group_size * QBLK)
        q_position = jnp.tile(lax.dynamic_slice_in_dim(q_pos_all, block_first, QBLK, 0), group_size)
        q_doc = jnp.tile(lax.dynamic_slice_in_dim(q_doc_all, block_first, QBLK, 0), group_size)
        q_first = base_pos + block_first
        first_start = jnp.max(jnp.where(doc_starts <= q_first, doc_starts, 0))
        dq_rows, acc_keys, acc_vals = block_grads(
            q_rows,
            g_rows,
            d_rows,
            q_position,
            q_doc,
            first_start,
            win_keys,
            win_vals,
            win_pos,
            win_doc,
            acc_keys,
            acc_vals,
        )
        return ((acc_keys, acc_vals), dq_rows)

    zero_acc = jnp.zeros((3 * ctx_rows, HEAD_DIM), jnp.float32)
    (acc_keys, acc_vals), dq_blocks = lax.scan(
        per_block, (zero_acc, zero_acc), jnp.arange(block_count, dtype=jnp.int32)
    )
    dq_blocks = dq_blocks.reshape(block_count, group_size, QBLK, HEAD_DIM).transpose(0, 2, 1, 3)
    dq_heads = dq_blocks.reshape(ctx_rows, group_size * HEAD_DIM)
    far_part_keys = acc_keys[:ctx_rows]
    far_part_vals = acc_vals[:ctx_rows]
    near_part_keys = acc_keys[ctx_rows : 2 * ctx_rows]
    near_part_vals = acc_vals[ctx_rows : 2 * ctx_rows]
    total_keys = acc_keys[2 * ctx_rows :]
    total_vals = acc_vals[2 * ctx_rows :]
    got_keys, got_vals = passed_along((near_part_keys, near_part_vals), "ctx", -1)
    far_got_keys, far_got_vals = passed_along((far_part_keys, far_part_vals), "ctx", -2)
    total_keys = total_keys + got_keys + far_got_keys
    total_vals = total_vals + got_vals + far_got_vals
    att_scale = HEAD_DIM ** (-0.5)
    dq_low = (dq_heads * att_scale).astype(jnp.bfloat16)
    dk_low = (total_keys * att_scale).astype(jnp.bfloat16)
    dv_low = total_vals.astype(jnp.bfloat16)
    grad_queries, grad_keys, grad_values = (
        lax.all_to_all(dq_low, "head", split_axis=0, concat_axis=1, tiled=True),
        lax.all_to_all(dk_low, "head", split_axis=0, concat_axis=1, tiled=True),
        lax.all_to_all(dv_low, "head", split_axis=0, concat_axis=1, tiled=True),
    )
    return (grad_queries, grad_keys, grad_values)


def solution(mesh):
    placed = (
        P(("ctx", "head"), None),
        P(("ctx", "head"), None),
        P(("ctx", "head"), None),
        P(("ctx", "head"), None),
        P(None, ("ctx", "head")),
        P(),
    )
    return jax.shard_map(
        on_device,
        mesh=mesh,
        in_specs=placed,
        out_specs=(P(("ctx", "head"), None), P(("ctx", "head"), None), P(("ctx", "head"), None)),
        check_vma=False,
    )
```

```python
import jax
import jax.numpy as jnp
from jax import lax
from jax.experimental import pallas as pl
from jax.experimental.pallas import tpu as pltpu
from jax.sharding import PartitionSpec as P

HEAD_DIM = 128
TILE = 256
NEG_FILL = -1e30
ATT_SCALE = HEAD_DIM ** (-0.5)
LOG2E = 1.4426950408889634


def passed_along(block, axis, distance):
    devices = range(lax.axis_size(axis))
    route = [(i - distance, i) for i in devices if i - distance in devices]
    return lax.ppermute(block, axis, route)


def contract_last(left, right):
    return lax.dot_general(
        left, right, (((1,), (1,)), ((), ())), preferred_element_type=jnp.float32
    )


def contract_inner(left, right):
    return jnp.dot(left, right, preferred_element_type=jnp.float32)


def attention_kernel(
    first_tile,
    q_ref,
    g_ref,
    k_ref,
    v_ref,
    delta_ref,
    start_ref,
    dq_ref,
    dk_ref,
    dv_ref,
    kt_ref,
    score_ref,
):
    rows = q_ref.shape[0]
    heads = q_ref.shape[1] // HEAD_DIM
    halo_tiles = (k_ref.shape[0] - rows) // TILE
    dk_ref[...] = jnp.zeros_like(dk_ref)
    dv_ref[...] = jnp.zeros_like(dv_ref)
    key_offset = lax.broadcasted_iota(jnp.int32, (TILE, TILE), 0)
    query_offset = lax.broadcasted_iota(jnp.int32, (1, TILE), 1)

    def turn(tile, carry):
        at = pl.ds(pl.multiple_of(tile * TILE, TILE), TILE)
        kt_ref[:, at] = k_ref[at, :].T
        return carry

    lax.fori_loop(first_tile[0], k_ref.shape[0] // TILE, turn, 0)

    def query_block(block, carry):
        q_at = pl.ds(pl.multiple_of(block * TILE, TILE), TILE)
        low = first_tile[block]
        high = halo_tiles + block + 1
        start = start_ref[:, q_at]
        last = query_offset + (halo_tiles + block) * TILE
        for head in range(heads):
            cols = slice(head * HEAD_DIM, (head + 1) * HEAD_DIM)
            q = q_ref[q_at, cols]
            g = g_ref[q_at, cols]
            delta = delta_ref[head : head + 1, q_at]

            def score_step(tile, top):
                at = pl.ds(pl.multiple_of(tile * TILE, TILE), TILE)
                scores = contract_last(k_ref[at, :], q) * (ATT_SCALE * LOG2E)
                place = key_offset + tile * TILE
                scores = jnp.where((place >= start) & (place <= last), scores, NEG_FILL)
                score_ref[at, :] = scores
                return jnp.maximum(top, jnp.max(scores.reshape(TILE // 8, 8, TILE), axis=0))

            top = lax.fori_loop(low, high, score_step, jnp.full((8, TILE), NEG_FILL, jnp.float32))
            top = jnp.max(top, axis=0, keepdims=True)

            def sum_step(tile, total):
                at = pl.ds(pl.multiple_of(tile * TILE, TILE), TILE)
                powers = jnp.exp2(score_ref[at, :] - top)
                return total + jnp.sum(powers.reshape(TILE // 8, 8, TILE), axis=0)

            total = lax.fori_loop(low, high, sum_step, jnp.zeros((8, TILE), jnp.float32))
            log_total = top + jnp.log2(jnp.sum(total, axis=0, keepdims=True))

            def grad_step(tile, dq_turned):
                at = pl.ds(pl.multiple_of(tile * TILE, TILE), TILE)
                probs = jnp.exp2(score_ref[at, :] - log_total)
                grad_probs = contract_last(v_ref[at, :], g)
                grad_scores = (probs * (grad_probs - delta)).astype(jnp.bfloat16)
                dv_ref[at, :] += contract_inner(probs.astype(jnp.bfloat16), g)
                dk_ref[at, :] += contract_inner(grad_scores, q)
                return dq_turned + contract_inner(kt_ref[:, at], grad_scores)

            dq_turned = lax.fori_loop(
                low, high, grad_step, jnp.zeros((HEAD_DIM, TILE), jnp.float32)
            )
            dq_ref[q_at, cols] = (dq_turned.T * ATT_SCALE).astype(jnp.bfloat16)
        return carry

    lax.fori_loop(0, rows // TILE, query_block, 0)


def attention(first_tile, q, g, keys, vals, delta, starts):
    rows, window = q.shape[0], keys.shape[0]
    vmem = pl.BlockSpec(memory_space=pltpu.VMEM)
    return pl.pallas_call(
        attention_kernel,
        out_shape=(
            jax.ShapeDtypeStruct(q.shape, jnp.bfloat16),
            jax.ShapeDtypeStruct(keys.shape, jnp.float32),
            jax.ShapeDtypeStruct(keys.shape, jnp.float32),
        ),
        in_specs=[pl.BlockSpec(memory_space=pltpu.SMEM)] + [vmem] * 6,
        out_specs=(vmem, vmem, vmem),
        scratch_shapes=[
            pltpu.VMEM((HEAD_DIM, window), jnp.bfloat16),
            pltpu.VMEM((window, TILE), jnp.float32),
        ],
        compiler_params=pltpu.CompilerParams(vmem_limit_bytes=40 * 1024 * 1024),
        name="attention",
    )(first_tile, q, g, keys, vals, delta, starts)


def on_device(queries, keys, values, grad_out, delta, doc_lengths):
    q_local, k_local, v_local, g_local = (
        lax.all_to_all(queries, "head", split_axis=1, concat_axis=0, tiled=True),
        lax.all_to_all(keys, "head", split_axis=1, concat_axis=0, tiled=True),
        lax.all_to_all(values, "head", split_axis=1, concat_axis=0, tiled=True),
        lax.all_to_all(grad_out, "head", split_axis=1, concat_axis=0, tiled=True),
    )
    d_local = lax.all_to_all(delta, "head", split_axis=0, concat_axis=1, tiled=True)
    rows = q_local.shape[0]
    near_keys, near_vals = passed_along((k_local, v_local), "ctx", 1)
    far_keys, far_vals = passed_along((k_local, v_local), "ctx", 2)
    win_keys = jnp.concatenate([far_keys, near_keys, k_local], axis=0)
    win_vals = jnp.concatenate([far_vals, near_vals, v_local], axis=0)
    base = lax.axis_index("ctx") * rows
    slots = jnp.arange(doc_lengths.shape[0], dtype=jnp.int32)
    doc_starts = jnp.sum(jnp.where(slots[:, None] < slots[None, :], doc_lengths[:, None], 0), axis=0)
    places = base + jnp.arange(rows, dtype=jnp.int32)
    starts = jnp.max(jnp.where(doc_starts[:, None] <= places[None, :], doc_starts[:, None], 0), axis=0)
    starts = starts - (base - 2 * rows)
    first_tile = starts[::TILE] // TILE
    dq, dk, dv = attention(first_tile, q_local, g_local, win_keys, win_vals, d_local, starts[None])
    got_keys, got_vals = passed_along((dk[rows : 2 * rows], dv[rows : 2 * rows]), "ctx", -1)
    far_got_keys, far_got_vals = passed_along((dk[:rows], dv[:rows]), "ctx", -2)
    dk_low = ((dk[2 * rows :] + got_keys + far_got_keys) * ATT_SCALE).astype(jnp.bfloat16)
    dv_low = (dv[2 * rows :] + got_vals + far_got_vals).astype(jnp.bfloat16)
    return (
        lax.all_to_all(dq, "head", split_axis=0, concat_axis=1, tiled=True),
        lax.all_to_all(dk_low, "head", split_axis=0, concat_axis=1, tiled=True),
        lax.all_to_all(dv_low, "head", split_axis=0, concat_axis=1, tiled=True),
    )


def solution(mesh):
    rows = P(("ctx", "head"), None)
    return jax.shard_map(
        on_device,
        mesh=mesh,
        in_specs=(rows, rows, rows, rows, P(None, ("ctx", "head")), P()),
        out_specs=(rows, rows, rows),
        check_vma=False,
    )
```

```python
import functools

import jax
import jax.numpy as jnp
from jax import lax
from jax.experimental import pallas as pl
from jax.experimental.pallas import tpu as pltpu
from jax.sharding import PartitionSpec as P

HEAD_DIM = 128
TILE = 256
STEP = 512
REACH = 2
NEG_FILL = -1e30
ATT_SCALE = HEAD_DIM ** (-0.5)
LOG2E = 1.4426950408889634
MESH = pl.DeviceIdType.MESH
VMEM = pl.BlockSpec(memory_space=pltpu.VMEM)
ANYWHERE = pl.BlockSpec(memory_space=pl.ANY)


def long_firsts(shards):
    middle = shards // 2
    return (0, middle - 3, middle - 1, middle + 1, shards - 3)


def halo_plan(shards, rows, short):
    near = tuple(range(shards - 1))
    far = tuple(range(shards - 2))
    if not short:
        return ((1, 0, rows, near), (2, 0, rows, far))
    firsts = long_firsts(shards)
    seconds = tuple(first + 1 for first in firsts)
    half = rows // 2
    return (
        (1, rows - TILE, rows, near),
        (1, half, rows - TILE, tuple(sorted(set(firsts + seconds)))),
        (1, 0, half, seconds),
        (2, half, rows, firsts),
    )


def halo_reach(shards, rows):
    half = rows // 2
    reach = [TILE] * shards
    for first in long_firsts(shards):
        reach[first + 1] = max(reach[first + 1], half)
        reach[first + 2] = max(reach[first + 2], rows + half)
    return reach


def is_one_of(index, members, shards):
    if members == tuple(range(len(members))):
        return index < len(members)
    return functools.reduce(jnp.logical_or, [index == member for member in members])


def contract_last(left, right):
    return lax.dot_general(
        left, right, (((1,), (1,)), ((), ())), preferred_element_type=jnp.float32
    )


def contract_inner(left, right):
    return jnp.dot(left, right, preferred_element_type=jnp.float32)


def meet(shards, peers, upward):
    ctx, head = lax.axis_index("ctx"), lax.axis_index("head")
    barrier = pltpu.get_barrier_semaphore()
    for step in range(1, peers):
        pl.semaphore_signal(
            barrier, inc=1, device_id=(ctx, lax.rem(head + step, peers)), device_id_type=MESH
        )
    for distance in (1, 2):
        other = ctx - distance if upward else ctx + distance
        there = ctx >= distance if upward else ctx < shards - distance

        @pl.when(there)
        def _():
            pl.semaphore_signal(barrier, inc=1, device_id=(other, head), device_id_type=MESH)

    beyond = shards - 1 - ctx if upward else ctx
    pl.semaphore_wait(barrier, peers - 1 + jnp.minimum(beyond, REACH))


def gather_kernel(
    shards,
    plan,
    q_in,
    k_in,
    v_in,
    g_in,
    d_in,
    q_out,
    k_out,
    v_out,
    g_out,
    d_out,
    send_sem,
    recv_sem,
    local_sem,
    halo_send,
    halo_recv,
):
    ctx, head = lax.axis_index("ctx"), lax.axis_index("head")
    part = q_in.shape[0]
    rows = q_out.shape[0]
    peers = rows // part
    halo = k_out.shape[0] - rows
    k_out[:halo, :] = jnp.zeros((halo, HEAD_DIM), k_out.dtype)
    v_out[:halo, :] = jnp.zeros((halo, HEAD_DIM), v_out.dtype)
    meet(shards, peers, True)

    def columns(ref, owner):
        width = ref.shape[1] // peers
        return ref.at[:, pl.ds(pl.multiple_of(owner * width, width), width)]

    def own_rows(ref, owner, first):
        return ref.at[pl.ds(pl.multiple_of(first + owner * part, part), part), :]

    pairs = (
        (lambda to: columns(k_in, to), lambda of: own_rows(k_out, of, halo)),
        (lambda to: columns(v_in, to), lambda of: own_rows(v_out, of, halo)),
        (lambda to: d_in.at[to], lambda of: d_out.at[of]),
        (lambda to: columns(q_in, to), lambda of: own_rows(q_out, of, 0)),
        (lambda to: columns(g_in, to), lambda of: own_rows(g_out, of, 0)),
    )

    def exchange(index, step):
        to = lax.rem(head + step, peers)
        source, target = pairs[index]
        return pltpu.make_async_remote_copy(
            src_ref=source(to),
            dst_ref=target(head),
            send_sem=send_sem.at[index, step],
            recv_sem=recv_sem.at[index, step],
            device_id=(ctx, to),
            device_id_type=MESH,
        )

    def keep(index):
        source, target = pairs[index]
        return pltpu.make_async_copy(source(head), target(head), local_sem.at[index])

    def arrived(index, step):
        source, target = pairs[index]
        of = lax.rem(head + peers - step, peers)
        pltpu.make_async_remote_copy(
            src_ref=source(head),
            dst_ref=target(of),
            send_sem=send_sem.at[index, step],
            recv_sem=recv_sem.at[index, step],
            device_id=(ctx, of),
            device_id_type=MESH,
        ).wait_recv()

    for index in range(5):
        keep(index).start()
        for step in range(1, peers):
            exchange(index, step).start()
    for index in range(2):
        keep(index).wait()
        for step in range(1, peers):
            arrived(index, step)

    def halo_copy(run, which):
        distance, first, end, _ = plan[run]
        ref = (k_out, v_out)[which]
        return pltpu.make_async_remote_copy(
            src_ref=ref.at[halo + first : halo + end, :],
            dst_ref=ref.at[halo - distance * rows + first : halo - distance * rows + end, :],
            send_sem=halo_send.at[run, which],
            recv_sem=halo_recv.at[run, which],
            device_id=(ctx + distance, head),
            device_id_type=MESH,
        )

    for run, (distance, first, end, senders) in enumerate(plan):

        @pl.when(is_one_of(ctx, senders, shards))
        def _():
            for which in range(2):
                halo_copy(run, which).start()

    for index in range(2, 5):
        keep(index).wait()
        for step in range(1, peers):
            arrived(index, step)
    for run, (distance, first, end, senders) in enumerate(plan):

        @pl.when(is_one_of(ctx, senders, shards))
        def _():
            for which in range(2):
                halo_copy(run, which).wait_send()

        @pl.when(is_one_of(ctx - distance, senders, shards) & (ctx >= distance))
        def _():
            for which in range(2):
                halo_copy(run, which).wait_recv()

    for index in range(5):
        for step in range(1, peers):
            exchange(index, step).wait_send()


def gather(shards, plan, short, queries, keys, values, grad_out, delta):
    peers = delta.shape[0]
    rows = queries.shape[0] * peers
    window = (REACH + 1) * rows + TILE
    width = queries.shape[1] // peers
    low = jnp.bfloat16
    return pl.pallas_call(
        functools.partial(gather_kernel, shards, plan),
        out_shape=(
            jax.ShapeDtypeStruct((rows, width), low),
            jax.ShapeDtypeStruct((window, HEAD_DIM), low),
            jax.ShapeDtypeStruct((window, HEAD_DIM), low),
            jax.ShapeDtypeStruct((rows, width), low),
            jax.ShapeDtypeStruct(delta.shape, jnp.float32),
        ),
        in_specs=[ANYWHERE] * 4 + [VMEM],
        out_specs=(VMEM,) * 5,
        scratch_shapes=[
            pltpu.SemaphoreType.DMA((5, peers)),
            pltpu.SemaphoreType.DMA((5, peers)),
            pltpu.SemaphoreType.DMA((5,)),
            pltpu.SemaphoreType.DMA((len(plan), 2)),
            pltpu.SemaphoreType.DMA((len(plan), 2)),
        ],
        compiler_params=pltpu.CompilerParams(
            collective_id=0 if short else 1,
            has_side_effects=True,
            vmem_limit_bytes=32 * 1024 * 1024,
        ),
        name="gather_short" if short else "gather_full",
    )(queries, keys, values, grad_out, delta)


def attention_kernel(
    first_row,
    q_ref,
    g_ref,
    k_ref,
    v_ref,
    delta_ref,
    start_ref,
    dq_ref,
    dk_ref,
    dv_ref,
    kt_ref,
    score_ref,
    turned_ref,
):
    rows = q_ref.shape[0]
    heads = range(q_ref.shape[1] // HEAD_DIM)
    halo = k_ref.shape[0] - rows
    parts = TILE // delta_ref.shape[2]
    columns = [slice(head * HEAD_DIM, (head + 1) * HEAD_DIM) for head in heads]
    dk_ref[...] = jnp.zeros_like(dk_ref)
    dv_ref[...] = jnp.zeros_like(dv_ref)
    key_offset = lax.broadcasted_iota(jnp.int32, (STEP, TILE), 0)
    query_offset = lax.broadcasted_iota(jnp.int32, (1, TILE), 1)

    def turn(tile, carry):
        at = pl.ds(pl.multiple_of(tile * TILE, TILE), TILE)
        kt_ref[:, at] = k_ref[at, :].T
        return carry

    lax.fori_loop(jnp.maximum(first_row[0] // TILE - 1, 0), k_ref.shape[0] // TILE, turn, 0)

    def query_block(block, carry):
        q_at = pl.ds(pl.multiple_of(block * TILE, TILE), TILE)
        end = halo + (block + 1) * TILE
        count = (end - first_row[block] + STEP - 1) // STEP
        start = start_ref[:, q_at]
        last = query_offset + (end - TILE)
        deltas = [
            jnp.concatenate(
                [delta_ref[block * parts + part, head : head + 1, :] for part in range(parts)],
                axis=1,
            )
            for head in heads
        ]

        def key_rows(step):
            return pl.multiple_of(end - (step + 1) * STEP, TILE)

        def score_step(step, tops):
            first = key_rows(step)
            at = pl.ds(first, STEP)
            keys = k_ref[at, :]
            place = key_offset + first
            allowed = (place >= start) & (place <= last)
            new_tops = []
            for head in heads:
                scores = contract_last(keys, q_ref[q_at, columns[head]]) * (ATT_SCALE * LOG2E)
                scores = jnp.where(allowed, scores, NEG_FILL)
                score_ref[head, at, :] = scores
                tall = jnp.max(scores.reshape(STEP // 8, 8, TILE), axis=0)
                new_tops.append(jnp.maximum(tops[head], tall))
            return tuple(new_tops)

        none = jnp.full((8, TILE), NEG_FILL, jnp.float32)
        tops = lax.fori_loop(0, count, score_step, tuple(none for _ in heads))
        tops = [jnp.max(top, axis=0, keepdims=True) for top in tops]

        def sum_step(step, totals):
            at = pl.ds(key_rows(step), STEP)
            new_totals = []
            for head in heads:
                powers = jnp.exp2(score_ref[head, at, :] - tops[head])
                new_totals.append(
                    totals[head] + jnp.sum(powers.reshape(STEP // 8, 8, TILE), axis=0)
                )
            return tuple(new_totals)

        zero = jnp.zeros((8, TILE), jnp.float32)
        totals = lax.fori_loop(0, count, sum_step, tuple(zero for _ in heads))
        log_totals = [
            tops[head] + jnp.log2(jnp.sum(totals[head], axis=0, keepdims=True)) for head in heads
        ]
        turned_ref[...] = jnp.zeros_like(turned_ref)

        def grad_step(step, carry):
            at = pl.ds(key_rows(step), STEP)
            vals = v_ref[at, :]
            keys_turned = kt_ref[:, at]
            val_parts, key_parts = [], []
            for head in heads:
                q = q_ref[q_at, columns[head]]
                g = g_ref[q_at, columns[head]]
                probs = jnp.exp2(score_ref[head, at, :] - log_totals[head])
                grad_probs = contract_last(vals, g)
                grad_scores = (probs * (grad_probs - deltas[head])).astype(jnp.bfloat16)
                val_parts.append(contract_inner(probs.astype(jnp.bfloat16), g))
                key_parts.append(contract_inner(grad_scores, q))
                turned_ref[head] += contract_inner(keys_turned, grad_scores)
            dv_ref[at, :] += sum(val_parts[1:], val_parts[0])
            dk_ref[at, :] += sum(key_parts[1:], key_parts[0])
            return carry

        lax.fori_loop(0, count, grad_step, 0)
        for head in heads:
            dq_ref[q_at, columns[head]] = (turned_ref[head].T * ATT_SCALE).astype(jnp.bfloat16)
        return carry

    lax.fori_loop(0, rows // TILE, query_block, 0)


def attention(first_row, q, g, keys, vals, delta, starts):
    window = keys.shape[0]
    heads = q.shape[1] // HEAD_DIM
    return pl.pallas_call(
        attention_kernel,
        out_shape=(
            jax.ShapeDtypeStruct(q.shape, jnp.bfloat16),
            jax.ShapeDtypeStruct(keys.shape, jnp.float32),
            jax.ShapeDtypeStruct(keys.shape, jnp.float32),
        ),
        in_specs=[pl.BlockSpec(memory_space=pltpu.SMEM)] + [VMEM] * 6,
        out_specs=(VMEM,) * 3,
        scratch_shapes=[
            pltpu.VMEM((HEAD_DIM, window), jnp.bfloat16),
            pltpu.VMEM((heads, window, TILE), jnp.float32),
            pltpu.VMEM((heads, HEAD_DIM, TILE), jnp.float32),
        ],
        compiler_params=pltpu.CompilerParams(vmem_limit_bytes=44 * 1024 * 1024),
        name="attention",
    )(first_row, q, g, keys, vals, delta, starts)


def scatter_kernel(
    shards,
    plan,
    dq_in,
    dk_in,
    dv_in,
    dq_out,
    dk_out,
    dv_out,
    low_ref,
    got_ref,
    total_ref,
    sum_ref,
    send_sem,
    recv_sem,
    local_sem,
    halo_send,
    halo_recv,
):
    ctx, head = lax.axis_index("ctx"), lax.axis_index("head")
    part = dq_out.shape[0]
    rows = dq_in.shape[0]
    peers = rows // part
    halo = dk_in.shape[0] - rows
    meet(shards, peers, False)

    def columns(ref, owner):
        width = ref.shape[1] // peers
        return ref.at[:, pl.ds(pl.multiple_of(owner * width, width), width)]

    def row_part(ref, owner):
        return ref.at[pl.ds(pl.multiple_of(owner * part, part), part), :]

    pairs = (
        (lambda to: row_part(dq_in, to), lambda of: columns(dq_out, of)),
        (lambda to: row_part(sum_ref.at[0], to), lambda of: columns(dk_out, of)),
        (lambda to: row_part(sum_ref.at[1], to), lambda of: columns(dv_out, of)),
    )

    def exchange(index, step):
        to = lax.rem(head + step, peers)
        source, target = pairs[index]
        return pltpu.make_async_remote_copy(
            src_ref=source(to),
            dst_ref=target(head),
            send_sem=send_sem.at[index, step],
            recv_sem=recv_sem.at[index, step],
            device_id=(ctx, to),
            device_id_type=MESH,
        )

    def keep(index):
        source, target = pairs[index]
        return pltpu.make_async_copy(source(head), target(head), local_sem.at[index])

    def arrived(index, step):
        source, target = pairs[index]
        of = lax.rem(head + peers - step, peers)
        pltpu.make_async_remote_copy(
            src_ref=source(head),
            dst_ref=target(of),
            send_sem=send_sem.at[index, step],
            recv_sem=recv_sem.at[index, step],
            device_id=(ctx, of),
            device_id_type=MESH,
        ).wait_recv()

    def halo_copy(run, which):
        distance, first, end, _ = plan[run]
        base = halo - distance * rows
        return pltpu.make_async_remote_copy(
            src_ref=low_ref.at[which, base + first : base + end, :],
            dst_ref=got_ref.at[which, base + first : base + end, :],
            send_sem=halo_send.at[run, which],
            recv_sem=halo_recv.at[run, which],
            device_id=(ctx - distance, head),
            device_id_type=MESH,
        )

    for run, (distance, first, end, senders) in enumerate(plan):

        @pl.when(is_one_of(ctx - distance, senders, shards) & (ctx >= distance))
        def _():
            at = slice(halo - distance * rows + first, halo - distance * rows + end)
            low_ref[0, at, :] = (dk_in[at, :] * ATT_SCALE).astype(jnp.bfloat16)
            low_ref[1, at, :] = dv_in[at, :].astype(jnp.bfloat16)
            for which in range(2):
                halo_copy(run, which).start()

    keep(0).start()
    for step in range(1, peers):
        exchange(0, step).start()
    total_ref[0] = dk_in[halo:, :] * ATT_SCALE
    total_ref[1] = dv_in[halo:, :]

    for run, (distance, first, end, senders) in enumerate(plan):

        @pl.when(is_one_of(ctx, senders, shards))
        def _():
            got = slice(halo - distance * rows + first, halo - distance * rows + end)
            own = slice(first, end)
            for which in range(2):
                halo_copy(run, which).wait_recv()
                total_ref[which, own, :] += got_ref[which, got, :].astype(jnp.float32)

    sum_ref[...] = total_ref[...].astype(jnp.bfloat16)
    for index in (1, 2):
        keep(index).start()
        for step in range(1, peers):
            exchange(index, step).start()
    for run, (distance, first, end, senders) in enumerate(plan):

        @pl.when(is_one_of(ctx - distance, senders, shards) & (ctx >= distance))
        def _():
            for which in range(2):
                halo_copy(run, which).wait_send()

    for index in range(3):
        keep(index).wait()
        for step in range(1, peers):
            arrived(index, step)
            exchange(index, step).wait_send()


def scatter(shards, plan, short, peers, dq, dk, dv):
    rows, width = dq.shape
    window = dk.shape[0]
    low = jnp.bfloat16
    return pl.pallas_call(
        functools.partial(scatter_kernel, shards, plan),
        out_shape=(
            jax.ShapeDtypeStruct((rows // peers, width * peers), low),
            jax.ShapeDtypeStruct((rows // peers, HEAD_DIM * peers), low),
            jax.ShapeDtypeStruct((rows // peers, HEAD_DIM * peers), low),
        ),
        in_specs=[VMEM] * 3,
        out_specs=(ANYWHERE,) * 3,
        scratch_shapes=[
            pltpu.VMEM((2, window - rows, HEAD_DIM), low),
            pltpu.VMEM((2, window - rows, HEAD_DIM), low),
            pltpu.VMEM((2, rows, HEAD_DIM), jnp.float32),
            pltpu.VMEM((2, rows, HEAD_DIM), low),
            pltpu.SemaphoreType.DMA((3, peers)),
            pltpu.SemaphoreType.DMA((3, peers)),
            pltpu.SemaphoreType.DMA((3,)),
            pltpu.SemaphoreType.DMA((len(plan), 2)),
            pltpu.SemaphoreType.DMA((len(plan), 2)),
        ],
        compiler_params=pltpu.CompilerParams(
            collective_id=2 if short else 3,
            has_side_effects=True,
            vmem_limit_bytes=32 * 1024 * 1024,
        ),
        name="scatter_short" if short else "scatter_full",
    )(dq, dk, dv)


def on_device(queries, keys, values, grad_out, delta, doc_lengths):
    shards, peers = lax.axis_size("ctx"), lax.axis_size("head")
    rows = queries.shape[0] * peers
    delta = delta.reshape(peers, delta.shape[0] // peers, delta.shape[1])
    slots = jnp.arange(doc_lengths.shape[0], dtype=jnp.int32)
    doc_starts = jnp.sum(jnp.where(slots[:, None] < slots[None, :], doc_lengths[:, None], 0), axis=0)

    def start_at(places):
        return jnp.max(
            jnp.where(doc_starts[:, None] <= places[None, :], doc_starts[:, None], 0), axis=0
        )

    base = lax.axis_index("ctx") * rows
    starts = start_at(base + jnp.arange(rows, dtype=jnp.int32)) - (base - REACH * rows - TILE)
    first_row = starts[::TILE]
    edges = jnp.arange(shards, dtype=jnp.int32) * rows
    reach = jnp.array(halo_reach(shards, rows), jnp.int32)
    fits = jnp.all(start_at(edges) >= edges - reach)

    def run(short, *operands):
        plan = halo_plan(shards, rows, short)
        q, k, v, g, d = gather(shards, plan, short, *operands)
        dq, dk, dv = attention(first_row, q, g, k, v, d, starts[None])
        return scatter(shards, plan, short, peers, dq, dk, dv)

    return lax.cond(
        fits,
        functools.partial(run, True),
        functools.partial(run, False),
        queries,
        keys,
        values,
        grad_out,
        delta,
    )


def solution(mesh):
    rows = P(("ctx", "head"), None)
    return jax.shard_map(
        on_device,
        mesh=mesh,
        in_specs=(rows, rows, rows, rows, P(None, ("ctx", "head")), P()),
        out_specs=(rows, rows, rows),
        check_vma=False,
    )
```

```python
import functools

import jax
import jax.numpy as jnp
import numpy as np
from jax import lax
from jax.experimental import pallas as pl
from jax.experimental.pallas import tpu as pltpu
from jax.sharding import PartitionSpec as P

HEAD_DIM = 128
TILE = 256
STEP = 512
REACH = 2
NEG_FILL = -1e30
ATT_SCALE = HEAD_DIM ** (-0.5)
LOG2E = 1.4426950408889634
MESH = pl.DeviceIdType.MESH
VMEM = pl.BlockSpec(memory_space=pltpu.VMEM)
ANYWHERE = pl.BlockSpec(memory_space=pl.ANY)


def long_firsts(shards):
    middle = shards // 2
    return (0, middle - 3, middle - 1, middle + 1, shards - 3)


def halo_plan(shards, rows, short):
    near = tuple(range(shards - 1))
    far = tuple(range(shards - 2))
    if not short:
        return ((1, 0, rows, near), (2, 0, rows, far))
    firsts = long_firsts(shards)
    seconds = tuple(first + 1 for first in firsts)
    half = rows // 2
    return (
        (1, rows - TILE, rows, near),
        (1, half, rows - TILE, tuple(sorted(set(firsts + seconds)))),
        (1, 0, half, seconds),
        (2, half, rows, firsts),
    )


def short_reach(blocks, shards, rows):
    shard = blocks * TILE // rows
    reach = (blocks - 1) * TILE
    for first in long_firsts(shards):
        opening = first * rows + rows // 2
        for other in (first + 1, first + 2):
            reach = np.where(shard == other, np.minimum(reach, opening), reach)
    return reach


def is_one_of(index, members, shards):
    if members == tuple(range(len(members))):
        return index < len(members)
    return functools.reduce(jnp.logical_or, [index == member for member in members])


def contract_last(left, right):
    return lax.dot_general(
        left, right, (((1,), (1,)), ((), ())), preferred_element_type=jnp.float32
    )


def contract_inner(left, right):
    return jnp.dot(left, right, preferred_element_type=jnp.float32)


def meet(shards, peers, upward):
    ctx, head = lax.axis_index("ctx"), lax.axis_index("head")
    barrier = pltpu.get_barrier_semaphore()
    for step in range(1, peers):
        pl.semaphore_signal(
            barrier, inc=1, device_id=(ctx, lax.rem(head + step, peers)), device_id_type=MESH
        )
    for distance in (1, 2):
        other = ctx - distance if upward else ctx + distance
        there = ctx >= distance if upward else ctx < shards - distance

        @pl.when(there)
        def _():
            pl.semaphore_signal(barrier, inc=1, device_id=(other, head), device_id_type=MESH)

    beyond = shards - 1 - ctx if upward else ctx
    pl.semaphore_wait(barrier, peers - 1 + jnp.minimum(beyond, REACH))


def gather_kernel(
    shards,
    plan,
    q_in,
    k_in,
    v_in,
    g_in,
    d_in,
    q_out,
    k_out,
    v_out,
    g_out,
    d_out,
    send_sem,
    recv_sem,
    local_sem,
    halo_send,
    halo_recv,
):
    ctx, head = lax.axis_index("ctx"), lax.axis_index("head")
    part = q_in.shape[0]
    rows = q_out.shape[0]
    peers = rows // part
    halo = k_out.shape[0] - rows
    k_out[:halo, :] = jnp.zeros((halo, HEAD_DIM), k_out.dtype)
    v_out[:halo, :] = jnp.zeros((halo, HEAD_DIM), v_out.dtype)
    meet(shards, peers, True)

    def columns(ref, owner):
        width = ref.shape[1] // peers
        return ref.at[:, pl.ds(pl.multiple_of(owner * width, width), width)]

    def own_rows(ref, owner, first):
        return ref.at[pl.ds(pl.multiple_of(first + owner * part, part), part), :]

    pairs = (
        (lambda to: columns(k_in, to), lambda of: own_rows(k_out, of, halo)),
        (lambda to: columns(v_in, to), lambda of: own_rows(v_out, of, halo)),
        (lambda to: d_in.at[to], lambda of: d_out.at[of]),
        (lambda to: columns(q_in, to), lambda of: own_rows(q_out, of, 0)),
        (lambda to: columns(g_in, to), lambda of: own_rows(g_out, of, 0)),
    )

    def exchange(index, step):
        to = lax.rem(head + step, peers)
        source, target = pairs[index]
        return pltpu.make_async_remote_copy(
            src_ref=source(to),
            dst_ref=target(head),
            send_sem=send_sem.at[index, step],
            recv_sem=recv_sem.at[index, step],
            device_id=(ctx, to),
            device_id_type=MESH,
        )

    def keep(index):
        source, target = pairs[index]
        return pltpu.make_async_copy(source(head), target(head), local_sem.at[index])

    def arrived(index, step):
        source, target = pairs[index]
        of = lax.rem(head + peers - step, peers)
        pltpu.make_async_remote_copy(
            src_ref=source(head),
            dst_ref=target(of),
            send_sem=send_sem.at[index, step],
            recv_sem=recv_sem.at[index, step],
            device_id=(ctx, of),
            device_id_type=MESH,
        ).wait_recv()

    for index in range(5):
        keep(index).start()
        for step in range(1, peers):
            exchange(index, step).start()
    for index in range(2):
        keep(index).wait()
        for step in range(1, peers):
            arrived(index, step)

    def halo_copy(run, which):
        distance, first, end, _ = plan[run]
        ref = (k_out, v_out)[which]
        return pltpu.make_async_remote_copy(
            src_ref=ref.at[halo + first : halo + end, :],
            dst_ref=ref.at[halo - distance * rows + first : halo - distance * rows + end, :],
            send_sem=halo_send.at[run, which],
            recv_sem=halo_recv.at[run, which],
            device_id=(ctx + distance, head),
            device_id_type=MESH,
        )

    for run, (distance, first, end, senders) in enumerate(plan):

        @pl.when(is_one_of(ctx, senders, shards))
        def _():
            for which in range(2):
                halo_copy(run, which).start()

    for index in range(2, 5):
        keep(index).wait()
        for step in range(1, peers):
            arrived(index, step)
    for run, (distance, first, end, senders) in enumerate(plan):

        @pl.when(is_one_of(ctx, senders, shards))
        def _():
            for which in range(2):
                halo_copy(run, which).wait_send()

        @pl.when(is_one_of(ctx - distance, senders, shards) & (ctx >= distance))
        def _():
            for which in range(2):
                halo_copy(run, which).wait_recv()

    for index in range(5):
        for step in range(1, peers):
            exchange(index, step).wait_send()


def gather(shards, plan, queries, keys, values, grad_out, delta):
    peers = delta.shape[0]
    rows = queries.shape[0] * peers
    window = (REACH + 1) * rows + TILE
    width = queries.shape[1] // peers
    low = jnp.bfloat16
    return pl.pallas_call(
        functools.partial(gather_kernel, shards, plan),
        out_shape=(
            jax.ShapeDtypeStruct((rows, width), low),
            jax.ShapeDtypeStruct((window, HEAD_DIM), low),
            jax.ShapeDtypeStruct((window, HEAD_DIM), low),
            jax.ShapeDtypeStruct((rows, width), low),
            jax.ShapeDtypeStruct(delta.shape, jnp.float32),
        ),
        in_specs=[ANYWHERE] * 4 + [VMEM],
        out_specs=(VMEM,) * 5,
        scratch_shapes=[
            pltpu.SemaphoreType.DMA((5, peers)),
            pltpu.SemaphoreType.DMA((5, peers)),
            pltpu.SemaphoreType.DMA((5,)),
            pltpu.SemaphoreType.DMA((len(plan), 2)),
            pltpu.SemaphoreType.DMA((len(plan), 2)),
        ],
        compiler_params=pltpu.CompilerParams(
            collective_id=1,
            has_side_effects=True,
            vmem_limit_bytes=32 * 1024 * 1024,
        ),
        name="gather",
    )(queries, keys, values, grad_out, delta)


def attention_kernel(
    first_row,
    q_ref,
    g_ref,
    k_ref,
    v_ref,
    delta_ref,
    start_ref,
    dq_ref,
    dk_ref,
    dv_ref,
    kt_ref,
    score_ref,
    turned_ref,
):
    rows = q_ref.shape[0]
    heads = range(q_ref.shape[1] // HEAD_DIM)
    halo = k_ref.shape[0] - rows
    parts = TILE // delta_ref.shape[2]
    columns = [slice(head * HEAD_DIM, (head + 1) * HEAD_DIM) for head in heads]
    dk_ref[...] = jnp.zeros_like(dk_ref)
    dv_ref[...] = jnp.zeros_like(dv_ref)
    key_offset = lax.broadcasted_iota(jnp.int32, (STEP, TILE), 0)
    query_offset = lax.broadcasted_iota(jnp.int32, (1, TILE), 1)

    def turn(tile, carry):
        at = pl.ds(pl.multiple_of(tile * TILE, TILE), TILE)
        kt_ref[:, at] = k_ref[at, :].T
        return carry

    lax.fori_loop(jnp.maximum(first_row[0] // TILE - 1, 0), k_ref.shape[0] // TILE, turn, 0)

    def query_block(block, carry):
        q_at = pl.ds(pl.multiple_of(block * TILE, TILE), TILE)
        end = halo + (block + 1) * TILE
        count = (end - first_row[block] + STEP - 1) // STEP
        start = start_ref[:, q_at]
        last = query_offset + (end - TILE)
        deltas = [
            jnp.concatenate(
                [delta_ref[block * parts + part, head : head + 1, :] for part in range(parts)],
                axis=1,
            )
            for head in heads
        ]

        def key_rows(step):
            return pl.multiple_of(end - (step + 1) * STEP, TILE)

        def score_step(step, tops):
            first = key_rows(step)
            at = pl.ds(first, STEP)
            keys = k_ref[at, :]
            place = key_offset + first
            allowed = (place >= start) & (place <= last)
            new_tops = []
            for head in heads:
                scores = contract_last(keys, q_ref[q_at, columns[head]]) * (ATT_SCALE * LOG2E)
                scores = jnp.where(allowed, scores, NEG_FILL)
                score_ref[head, at, :] = scores
                tall = jnp.max(scores.reshape(STEP // 8, 8, TILE), axis=0)
                new_tops.append(jnp.maximum(tops[head], tall))
            return tuple(new_tops)

        none = jnp.full((8, TILE), NEG_FILL, jnp.float32)
        tops = lax.fori_loop(0, count, score_step, tuple(none for _ in heads))
        tops = [jnp.max(top, axis=0, keepdims=True) for top in tops]

        def sum_step(step, totals):
            at = pl.ds(key_rows(step), STEP)
            new_totals = []
            for head in heads:
                powers = jnp.exp2(score_ref[head, at, :] - tops[head])
                new_totals.append(
                    totals[head] + jnp.sum(powers.reshape(STEP // 8, 8, TILE), axis=0)
                )
            return tuple(new_totals)

        zero = jnp.zeros((8, TILE), jnp.float32)
        totals = lax.fori_loop(0, count, sum_step, tuple(zero for _ in heads))
        log_totals = [
            tops[head] + jnp.log2(jnp.sum(totals[head], axis=0, keepdims=True)) for head in heads
        ]
        turned_ref[...] = jnp.zeros_like(turned_ref)

        def grad_step(step, carry):
            at = pl.ds(key_rows(step), STEP)
            vals = v_ref[at, :]
            keys_turned = kt_ref[:, at]
            val_parts, key_parts = [], []
            for head in heads:
                q = q_ref[q_at, columns[head]]
                g = g_ref[q_at, columns[head]]
                probs = jnp.exp2(score_ref[head, at, :] - log_totals[head])
                grad_probs = contract_last(vals, g)
                grad_scores = (probs * (grad_probs - deltas[head])).astype(jnp.bfloat16)
                val_parts.append(contract_inner(probs.astype(jnp.bfloat16), g))
                key_parts.append(contract_inner(grad_scores, q))
                turned_ref[head] += contract_inner(keys_turned, grad_scores)
            dv_ref[at, :] += sum(val_parts[1:], val_parts[0])
            dk_ref[at, :] += sum(key_parts[1:], key_parts[0])
            return carry

        lax.fori_loop(0, count, grad_step, 0)
        for head in heads:
            dq_ref[q_at, columns[head]] = (turned_ref[head].T * ATT_SCALE).astype(jnp.bfloat16)
        return carry

    lax.fori_loop(0, rows // TILE, query_block, 0)


def attention(first_row, q, g, keys, vals, delta, starts):
    window = keys.shape[0]
    heads = q.shape[1] // HEAD_DIM
    return pl.pallas_call(
        attention_kernel,
        out_shape=(
            jax.ShapeDtypeStruct(q.shape, jnp.bfloat16),
            jax.ShapeDtypeStruct(keys.shape, jnp.float32),
            jax.ShapeDtypeStruct(keys.shape, jnp.float32),
        ),
        in_specs=[pl.BlockSpec(memory_space=pltpu.SMEM)] + [VMEM] * 6,
        out_specs=(VMEM,) * 3,
        scratch_shapes=[
            pltpu.VMEM((HEAD_DIM, window), jnp.bfloat16),
            pltpu.VMEM((heads, window, TILE), jnp.float32),
            pltpu.VMEM((heads, HEAD_DIM, TILE), jnp.float32),
        ],
        compiler_params=pltpu.CompilerParams(vmem_limit_bytes=44 * 1024 * 1024),
        name="attention",
    )(first_row, q, g, keys, vals, delta, starts)


def scatter_kernel(
    shards,
    plan,
    dq_in,
    dk_in,
    dv_in,
    dq_out,
    dk_out,
    dv_out,
    low_ref,
    got_ref,
    total_ref,
    sum_ref,
    send_sem,
    recv_sem,
    local_sem,
    halo_send,
    halo_recv,
):
    ctx, head = lax.axis_index("ctx"), lax.axis_index("head")
    part = dq_out.shape[0]
    rows = dq_in.shape[0]
    peers = rows // part
    halo = dk_in.shape[0] - rows
    meet(shards, peers, False)

    def columns(ref, owner):
        width = ref.shape[1] // peers
        return ref.at[:, pl.ds(pl.multiple_of(owner * width, width), width)]

    def row_part(ref, owner):
        return ref.at[pl.ds(pl.multiple_of(owner * part, part), part), :]

    pairs = (
        (lambda to: row_part(dq_in, to), lambda of: columns(dq_out, of)),
        (lambda to: row_part(sum_ref.at[0], to), lambda of: columns(dk_out, of)),
        (lambda to: row_part(sum_ref.at[1], to), lambda of: columns(dv_out, of)),
    )

    def exchange(index, step):
        to = lax.rem(head + step, peers)
        source, target = pairs[index]
        return pltpu.make_async_remote_copy(
            src_ref=source(to),
            dst_ref=target(head),
            send_sem=send_sem.at[index, step],
            recv_sem=recv_sem.at[index, step],
            device_id=(ctx, to),
            device_id_type=MESH,
        )

    def keep(index):
        source, target = pairs[index]
        return pltpu.make_async_copy(source(head), target(head), local_sem.at[index])

    def arrived(index, step):
        source, target = pairs[index]
        of = lax.rem(head + peers - step, peers)
        pltpu.make_async_remote_copy(
            src_ref=source(head),
            dst_ref=target(of),
            send_sem=send_sem.at[index, step],
            recv_sem=recv_sem.at[index, step],
            device_id=(ctx, of),
            device_id_type=MESH,
        ).wait_recv()

    def halo_copy(run, which):
        distance, first, end, _ = plan[run]
        base = halo - distance * rows
        return pltpu.make_async_remote_copy(
            src_ref=low_ref.at[which, base + first : base + end, :],
            dst_ref=got_ref.at[which, base + first : base + end, :],
            send_sem=halo_send.at[run, which],
            recv_sem=halo_recv.at[run, which],
            device_id=(ctx - distance, head),
            device_id_type=MESH,
        )

    for run, (distance, first, end, senders) in enumerate(plan):

        @pl.when(is_one_of(ctx - distance, senders, shards) & (ctx >= distance))
        def _():
            at = slice(halo - distance * rows + first, halo - distance * rows + end)
            low_ref[0, at, :] = (dk_in[at, :] * ATT_SCALE).astype(jnp.bfloat16)
            low_ref[1, at, :] = dv_in[at, :].astype(jnp.bfloat16)
            for which in range(2):
                halo_copy(run, which).start()

    keep(0).start()
    for step in range(1, peers):
        exchange(0, step).start()
    total_ref[0] = dk_in[halo:, :] * ATT_SCALE
    total_ref[1] = dv_in[halo:, :]

    for run, (distance, first, end, senders) in enumerate(plan):

        @pl.when(is_one_of(ctx, senders, shards))
        def _():
            got = slice(halo - distance * rows + first, halo - distance * rows + end)
            own = slice(first, end)
            for which in range(2):
                halo_copy(run, which).wait_recv()
                total_ref[which, own, :] += got_ref[which, got, :].astype(jnp.float32)

    sum_ref[...] = total_ref[...].astype(jnp.bfloat16)
    for index in (1, 2):
        keep(index).start()
        for step in range(1, peers):
            exchange(index, step).start()
    for run, (distance, first, end, senders) in enumerate(plan):

        @pl.when(is_one_of(ctx - distance, senders, shards) & (ctx >= distance))
        def _():
            for which in range(2):
                halo_copy(run, which).wait_send()

    for index in range(3):
        keep(index).wait()
        for step in range(1, peers):
            arrived(index, step)
            exchange(index, step).wait_send()


def scatter(shards, plan, peers, dq, dk, dv):
    rows, width = dq.shape
    window = dk.shape[0]
    low = jnp.bfloat16
    return pl.pallas_call(
        functools.partial(scatter_kernel, shards, plan),
        out_shape=(
            jax.ShapeDtypeStruct((rows // peers, width * peers), low),
            jax.ShapeDtypeStruct((rows // peers, HEAD_DIM * peers), low),
            jax.ShapeDtypeStruct((rows // peers, HEAD_DIM * peers), low),
        ),
        in_specs=[VMEM] * 3,
        out_specs=(ANYWHERE,) * 3,
        scratch_shapes=[
            pltpu.VMEM((2, window - rows, HEAD_DIM), low),
            pltpu.VMEM((2, window - rows, HEAD_DIM), low),
            pltpu.VMEM((2, rows, HEAD_DIM), jnp.float32),
            pltpu.VMEM((2, rows, HEAD_DIM), low),
            pltpu.SemaphoreType.DMA((3, peers)),
            pltpu.SemaphoreType.DMA((3, peers)),
            pltpu.SemaphoreType.DMA((3,)),
            pltpu.SemaphoreType.DMA((len(plan), 2)),
            pltpu.SemaphoreType.DMA((len(plan), 2)),
        ],
        compiler_params=pltpu.CompilerParams(
            collective_id=2,
            has_side_effects=True,
            vmem_limit_bytes=32 * 1024 * 1024,
        ),
        name="scatter",
    )(dq, dk, dv)


def first_tiles(ctx, block, shards, rows, reach_tiles):
    own = rows // TILE
    half = own // 2
    firsts = long_firsts(shards)
    second = is_one_of(ctx, tuple(first + 1 for first in firsts), shards)
    third = is_one_of(ctx, tuple(first + 2 for first in firsts), shards)
    low = jnp.where(second, jnp.minimum(reach_tiles - half, reach_tiles + block - 1), reach_tiles + block - 1)
    return jnp.where(third, reach_tiles - own - half, low)


def whole_kernel(
    shards,
    plan,
    q_in,
    k_in,
    v_in,
    g_in,
    d_in,
    lengths_ref,
    dq_out,
    dk_out,
    dv_out,
    q_buf,
    g_buf,
    k_win,
    v_win,
    d_buf,
    start_ref,
    kt_ref,
    score_ref,
    probs_ref,
    grads_ref,
    q_stack,
    g_stack,
    turned_ref,
    dk_acc,
    dv_acc,
    dq_buf,
    low_ref,
    got_ref,
    total_ref,
    sum_ref,
    send_sem,
    recv_sem,
    local_sem,
    halo_send,
    halo_recv,
    back_send,
    back_recv,
):
    ctx, head = lax.axis_index("ctx"), lax.axis_index("head")
    part = q_in.shape[0]
    rows, width = q_buf.shape
    peers = rows // part
    halo = k_win.shape[0] - rows
    half_width = width // 2
    pair_heads = range(half_width // HEAD_DIM)
    stacks = [slice(one * TILE, (one + 1) * TILE) for one in pair_heads]
    k_win[:halo, :] = jnp.zeros((halo, HEAD_DIM), k_win.dtype)
    v_win[:halo, :] = jnp.zeros((halo, HEAD_DIM), v_win.dtype)

    barrier = pltpu.get_barrier_semaphore()
    for step in range(1, peers):
        pl.semaphore_signal(
            barrier, inc=1, device_id=(ctx, lax.rem(head + step, peers)), device_id_type=MESH
        )
    for distance in (1, 2):

        @pl.when(ctx >= distance)
        def _():
            pl.semaphore_signal(
                barrier, inc=1, device_id=(ctx - distance, head), device_id_type=MESH
            )

        @pl.when(ctx < shards - distance)
        def _():
            pl.semaphore_signal(
                barrier, inc=1, device_id=(ctx + distance, head), device_id_type=MESH
            )

    around = jnp.minimum(shards - 1 - ctx, REACH) + jnp.minimum(ctx, REACH)
    pl.semaphore_wait(barrier, peers - 1 + around)

    def columns(ref, owner, offset, size):
        stride = ref.shape[1] // peers
        return ref.at[:, pl.ds(pl.multiple_of(owner * stride + offset, size), size)]

    def own_rows(ref, owner, first):
        return ref.at[pl.ds(pl.multiple_of(first + owner * part, part), part), :]

    def own_pair(ref, owner, pair):
        at = pl.ds(pl.multiple_of(owner * part, part), part)
        return ref.at[at, pair * half_width : (pair + 1) * half_width]

    def paired_in(source, target, pair):
        return (
            lambda to: columns(source, to, pair * half_width, half_width),
            lambda of: own_pair(target, of, pair),
        )

    def paired_out(source, target, pair):
        return (
            lambda to: own_pair(source, to, pair),
            lambda of: columns(target, of, pair * half_width, half_width),
        )

    routes = (
        (lambda to: columns(k_in, to, 0, HEAD_DIM), lambda of: own_rows(k_win, of, halo)),
        (lambda to: columns(v_in, to, 0, HEAD_DIM), lambda of: own_rows(v_win, of, halo)),
        (lambda to: d_in.at[to], lambda of: d_buf.at[of]),
        paired_in(q_in, q_buf, 0),
        paired_in(g_in, g_buf, 0),
        paired_in(q_in, q_buf, 1),
        paired_in(g_in, g_buf, 1),
        paired_out(dq_buf, dq_out, 0),
        paired_out(dq_buf, dq_out, 1),
        (lambda to: own_rows(sum_ref.at[0], to, 0), lambda of: columns(dk_out, of, 0, HEAD_DIM)),
        (lambda to: own_rows(sum_ref.at[1], to, 0), lambda of: columns(dv_out, of, 0, HEAD_DIM)),
    )

    def exchange(index, step):
        to = lax.rem(head + step, peers)
        source, target = routes[index]
        return pltpu.make_async_remote_copy(
            src_ref=source(to),
            dst_ref=target(head),
            send_sem=send_sem.at[index, step],
            recv_sem=recv_sem.at[index, step],
            device_id=(ctx, to),
            device_id_type=MESH,
        )

    def keep(index):
        source, target = routes[index]
        return pltpu.make_async_copy(source(head), target(head), local_sem.at[index])

    def begin(*indices):
        for index in indices:
            keep(index).start()
            for step in range(1, peers):
                exchange(index, step).start()

    def arrived(*indices):
        for index in indices:
            keep(index).wait()
            source, target = routes[index]
            for step in range(1, peers):
                of = lax.rem(head + peers - step, peers)
                pltpu.make_async_remote_copy(
                    src_ref=source(head),
                    dst_ref=target(of),
                    send_sem=send_sem.at[index, step],
                    recv_sem=recv_sem.at[index, step],
                    device_id=(ctx, of),
                    device_id_type=MESH,
                ).wait_recv()

    def halo_copy(run, which):
        distance, first, end, _ = plan[run]
        ref = (k_win, v_win)[which]
        base = halo - distance * rows
        return pltpu.make_async_remote_copy(
            src_ref=ref.at[halo + first : halo + end, :],
            dst_ref=ref.at[base + first : base + end, :],
            send_sem=halo_send.at[run, which],
            recv_sem=halo_recv.at[run, which],
            device_id=(ctx + distance, head),
            device_id_type=MESH,
        )

    def back_copy(run, which):
        distance, first, end, _ = plan[run]
        base = halo - distance * rows
        return pltpu.make_async_remote_copy(
            src_ref=low_ref.at[which, base + first : base + end, :],
            dst_ref=got_ref.at[which, base + first : base + end, :],
            send_sem=back_send.at[run, which],
            recv_sem=back_recv.at[run, which],
            device_id=(ctx - distance, head),
            device_id_type=MESH,
        )

    def for_runs(body, upward):
        for run, (distance, first, end, senders) in enumerate(plan):
            if upward:
                here = is_one_of(ctx, senders, shards)
            else:
                here = is_one_of(ctx - distance, senders, shards) & (ctx >= distance)

            @pl.when(here)
            def _():
                body(run, distance, first, end)

    begin(0, 1, 2, 3, 4)

    docs = lengths_ref.shape[1]
    before = lax.broadcasted_iota(jnp.int32, (docs, docs), 1) < lax.broadcasted_iota(
        jnp.int32, (docs, docs), 0
    )
    lengths = lengths_ref[...].astype(jnp.float32)
    doc_starts = jnp.sum(jnp.where(before, lengths, 0.0), axis=1, keepdims=True)
    doc_starts = doc_starts - (ctx * rows - halo).astype(jnp.float32)
    places = lax.broadcasted_iota(jnp.int32, (1, rows), 1).astype(jnp.float32) + float(halo)
    starts = jnp.max(jnp.where(doc_starts <= places, doc_starts, -1e9), axis=0, keepdims=True)
    start_ref[...] = starts.astype(jnp.int32)
    dk_acc[...] = jnp.zeros_like(dk_acc)
    dv_acc[...] = jnp.zeros_like(dv_acc)

    arrived(0, 1)
    for_runs(lambda run, *_: [halo_copy(run, which).start() for which in range(2)], True)
    begin(5, 6)

    reach_tiles = halo // TILE
    key_offset = lax.broadcasted_iota(jnp.int32, (STEP, TILE), 0)
    query_offset = lax.broadcasted_iota(jnp.int32, (1, TILE), 1)
    parts = TILE // part

    def turn(tile, carry):
        at = pl.ds(pl.multiple_of(tile * TILE, TILE), TILE)
        kt_ref[:, at] = k_win[at, :].T
        return carry

    def attend(pair):
        def query_block(block, carry):
            q_at = pl.ds(pl.multiple_of(block * TILE, TILE), TILE)
            end = halo + (block + 1) * TILE
            tiles = reach_tiles + block + 1 - first_tiles(ctx, block, shards, rows, reach_tiles)
            count = lax.div(tiles + 1, STEP // TILE)
            start = start_ref[:, q_at]
            last = query_offset + (end - TILE)
            deltas = []
            for one in pair_heads:
                which = pair * len(pair_heads) + one
                cols = slice(which * HEAD_DIM, (which + 1) * HEAD_DIM)
                q_stack[stacks[one], :] = q_buf[q_at, cols]
                g_stack[stacks[one], :] = g_buf[q_at, cols]
                deltas.append(
                    jnp.concatenate(
                        [d_buf[block * parts + p, which : which + 1, :] for p in range(parts)],
                        axis=1,
                    )
                )

            def key_rows(step):
                return pl.multiple_of(end - (step + 1) * STEP, TILE)

            def score_step(step, tops):
                first = key_rows(step)
                at = pl.ds(first, STEP)
                keys = k_win[at, :]
                place = key_offset + first
                allowed = (place >= start) & (place <= last)
                new_tops = []
                for one in pair_heads:
                    scores = contract_last(keys, q_stack[stacks[one], :]) * (ATT_SCALE * LOG2E)
                    scores = jnp.where(allowed, scores, NEG_FILL)
                    score_ref[at, stacks[one]] = scores
                    tall = jnp.max(scores.reshape(STEP // 8, 8, TILE), axis=0)
                    new_tops.append(jnp.maximum(tops[one], tall))
                return tuple(new_tops)

            none = jnp.full((8, TILE), NEG_FILL, jnp.float32)
            tops = lax.fori_loop(0, count, score_step, tuple(none for _ in pair_heads))
            tops = [jnp.max(top, axis=0, keepdims=True) for top in tops]

            def sum_step(step, totals):
                at = pl.ds(key_rows(step), STEP)
                new_totals = []
                for one in pair_heads:
                    powers = jnp.exp2(score_ref[at, stacks[one]] - tops[one])
                    tall = jnp.sum(powers.reshape(STEP // 8, 8, TILE), axis=0)
                    new_totals.append(totals[one] + tall)
                return tuple(new_totals)

            zero = jnp.zeros((8, TILE), jnp.float32)
            totals = lax.fori_loop(0, count, sum_step, tuple(zero for _ in pair_heads))
            log_totals = [
                tops[one] + jnp.log2(jnp.sum(totals[one], axis=0, keepdims=True))
                for one in pair_heads
            ]
            turned_ref[...] = jnp.zeros_like(turned_ref)

            def grad_step(step, carry):
                at = pl.ds(key_rows(step), STEP)
                vals = v_win[at, :]
                for one in pair_heads:
                    probs = jnp.exp2(score_ref[at, stacks[one]] - log_totals[one])
                    grad_probs = contract_last(vals, g_stack[stacks[one], :])
                    grads = (probs * (grad_probs - deltas[one])).astype(jnp.bfloat16)
                    probs_ref[:, stacks[one]] = probs.astype(jnp.bfloat16)
                    grads_ref[:, stacks[one]] = grads
                dv_acc[at, :] += contract_inner(probs_ref[...], g_stack[...])
                dk_acc[at, :] += contract_inner(grads_ref[...], q_stack[...])
                turned_ref[...] += contract_inner(kt_ref[:, at], grads_ref[...])
                return carry

            lax.fori_loop(0, count, grad_step, 0)
            for one in pair_heads:
                which = pair * len(pair_heads) + one
                dq = turned_ref[:, stacks[one]].T * ATT_SCALE
                dq_buf[q_at, which * HEAD_DIM : (which + 1) * HEAD_DIM] = dq.astype(jnp.bfloat16)
            return carry

        lax.fori_loop(0, rows // TILE, query_block, 0)

    arrived(2, 3, 4)
    for_runs(lambda run, *_: [halo_copy(run, which).wait_recv() for which in range(2)], False)
    lowest = first_tiles(ctx, 0, shards, rows, reach_tiles) - 1
    lax.fori_loop(lowest, reach_tiles + rows // TILE, turn, 0)
    attend(0)
    begin(7)
    arrived(5, 6)
    attend(1)

    def send_back(run, distance, first, end):
        at = slice(halo - distance * rows + first, halo - distance * rows + end)
        low_ref[0, at, :] = (dk_acc[at, :] * ATT_SCALE).astype(jnp.bfloat16)
        low_ref[1, at, :] = dv_acc[at, :].astype(jnp.bfloat16)
        for which in range(2):
            back_copy(run, which).start()

    def take_back(run, distance, first, end):
        got = slice(halo - distance * rows + first, halo - distance * rows + end)
        for which in range(2):
            back_copy(run, which).wait_recv()
            total_ref[which, first:end, :] += got_ref[which, got, :].astype(jnp.float32)

    for_runs(send_back, False)
    begin(8)
    total_ref[0] = dk_acc[halo:, :] * ATT_SCALE
    total_ref[1] = dv_acc[halo:, :]
    for_runs(take_back, True)
    sum_ref[...] = total_ref[...].astype(jnp.bfloat16)
    begin(9, 10)
    for_runs(lambda run, *_: [halo_copy(run, which).wait_send() for which in range(2)], True)
    for_runs(lambda run, *_: [back_copy(run, which).wait_send() for which in range(2)], False)
    arrived(7, 8, 9, 10)
    for index in range(len(routes)):
        for step in range(1, peers):
            exchange(index, step).wait_send()


def whole(shards, plan, queries, keys, values, grad_out, delta, doc_lengths):
    peers = delta.shape[0]
    part = queries.shape[0]
    rows = part * peers
    width = queries.shape[1] // peers
    window = (REACH + 1) * rows + TILE
    low, full = jnp.bfloat16, jnp.float32
    wide = width // 2 // HEAD_DIM * TILE
    dma = pltpu.SemaphoreType.DMA
    return pl.pallas_call(
        functools.partial(whole_kernel, shards, plan),
        out_shape=(
            jax.ShapeDtypeStruct(queries.shape, low),
            jax.ShapeDtypeStruct(keys.shape, low),
            jax.ShapeDtypeStruct(values.shape, low),
        ),
        in_specs=[ANYWHERE] * 4 + [VMEM] * 2,
        out_specs=(ANYWHERE,) * 3,
        scratch_shapes=[
            pltpu.VMEM((rows, width), low),
            pltpu.VMEM((rows, width), low),
            pltpu.VMEM((window, HEAD_DIM), low),
            pltpu.VMEM((window, HEAD_DIM), low),
            pltpu.VMEM(delta.shape, full),
            pltpu.VMEM((1, rows), jnp.int32),
            pltpu.VMEM((HEAD_DIM, window), low),
            pltpu.VMEM((window, wide), full),
            pltpu.VMEM((STEP, wide), low),
            pltpu.VMEM((STEP, wide), low),
            pltpu.VMEM((wide, HEAD_DIM), low),
            pltpu.VMEM((wide, HEAD_DIM), low),
            pltpu.VMEM((HEAD_DIM, wide), full),
            pltpu.VMEM((window, HEAD_DIM), full),
            pltpu.VMEM((window, HEAD_DIM), full),
            pltpu.VMEM((rows, width), low),
            pltpu.VMEM((2, window - rows, HEAD_DIM), low),
            pltpu.VMEM((2, window - rows, HEAD_DIM), low),
            pltpu.VMEM((2, rows, HEAD_DIM), full),
            pltpu.VMEM((2, rows, HEAD_DIM), low),
            dma((11, peers)),
            dma((11, peers)),
            dma((11,)),
            dma((len(plan), 2)),
            dma((len(plan), 2)),
            dma((len(plan), 2)),
            dma((len(plan), 2)),
        ],
        compiler_params=pltpu.CompilerParams(
            collective_id=0, has_side_effects=True, vmem_limit_bytes=44 * 1024 * 1024
        ),
        name="whole",
    )(queries, keys, values, grad_out, delta, doc_lengths[None])


def on_device(queries, keys, values, grad_out, delta, doc_lengths):
    shards, peers = lax.axis_size("ctx"), lax.axis_size("head")
    rows = queries.shape[0] * peers
    delta = delta.reshape(peers, delta.shape[0] // peers, delta.shape[1])
    slots = jnp.arange(doc_lengths.shape[0], dtype=jnp.int32)
    doc_starts = jnp.sum(jnp.where(slots[:, None] < slots[None, :], doc_lengths[:, None], 0), axis=0)

    def start_at(places):
        return jnp.max(
            jnp.where(doc_starts[:, None] <= places[None, :], doc_starts[:, None], 0), axis=0
        )

    blocks = np.arange(shards * rows // TILE)
    lowest = jnp.asarray(short_reach(blocks, shards, rows), jnp.int32)
    fits = jnp.all(start_at(jnp.asarray(blocks * TILE, jnp.int32)) >= lowest)

    def in_one(*operands):
        return whole(shards, halo_plan(shards, rows, True), *operands, doc_lengths)

    def in_three(*operands):
        plan = halo_plan(shards, rows, False)
        base = lax.axis_index("ctx") * rows
        starts = start_at(base + jnp.arange(rows, dtype=jnp.int32)) - (base - REACH * rows - TILE)
        q, k, v, g, d = gather(shards, plan, *operands)
        dq, dk, dv = attention(starts[::TILE], q, g, k, v, d, starts[None])
        return scatter(shards, plan, peers, dq, dk, dv)

    return lax.cond(fits, in_one, in_three, queries, keys, values, grad_out, delta)


def solution(mesh):
    rows = P(("ctx", "head"), None)
    return jax.shard_map(
        on_device,
        mesh=mesh,
        in_specs=(rows, rows, rows, rows, P(None, ("ctx", "head")), P()),
        out_specs=(rows, rows, rows),
        check_vma=False,
    )
```

```python
import functools

import jax
import jax.numpy as jnp
import numpy as np
from jax import lax
from jax.experimental import pallas as pl
from jax.experimental.pallas import tpu as pltpu
from jax.sharding import PartitionSpec as P

HEAD_DIM = 128
TILE = 256
STEP = 512
REACH = 2
NEG_FILL = -1e30
ATT_SCALE = HEAD_DIM ** (-0.5)
LOG2E = 1.4426950408889634
MESH = pl.DeviceIdType.MESH
VMEM = pl.BlockSpec(memory_space=pltpu.VMEM)
ANYWHERE = pl.BlockSpec(memory_space=pl.ANY)


def long_firsts(shards):
    middle = shards // 2
    return (0, middle - 3, middle - 1, middle + 1, shards - 3)


def halo_plan(shards, rows, short):
    near = tuple(range(shards - 1))
    far = tuple(range(shards - 2))
    if not short:
        return ((1, 0, rows, near), (2, 0, rows, far))
    firsts = long_firsts(shards)
    seconds = tuple(first + 1 for first in firsts)
    half = rows // 2
    return (
        (1, rows - TILE, rows, near),
        (1, half, rows - TILE, tuple(sorted(set(firsts + seconds)))),
        (1, 0, half, seconds),
        (2, half, rows, firsts),
    )


def short_reach(blocks, shards, rows):
    shard = blocks * TILE // rows
    reach = np.where(shard == 0, 0, (blocks - 1) * TILE)
    for first in long_firsts(shards):
        opening = first * rows + rows // 2
        for other in (first + 1, first + 2):
            reach = np.where(shard == other, np.minimum(reach, opening), reach)
    return reach


def is_one_of(index, members, shards):
    if members == tuple(range(len(members))):
        return index < len(members)
    return functools.reduce(jnp.logical_or, [index == member for member in members])


def contract_last(left, right):
    return lax.dot_general(
        left, right, (((1,), (1,)), ((), ())), preferred_element_type=jnp.float32
    )


def contract_inner(left, right):
    return jnp.dot(left, right, preferred_element_type=jnp.float32)


def meet(shards, peers, upward):
    ctx, head = lax.axis_index("ctx"), lax.axis_index("head")
    barrier = pltpu.get_barrier_semaphore()
    for step in range(1, peers):
        pl.semaphore_signal(
            barrier, inc=1, device_id=(ctx, lax.rem(head + step, peers)), device_id_type=MESH
        )
    for distance in (1, 2):
        other = ctx - distance if upward else ctx + distance
        there = ctx >= distance if upward else ctx < shards - distance

        @pl.when(there)
        def _():
            pl.semaphore_signal(barrier, inc=1, device_id=(other, head), device_id_type=MESH)

    beyond = shards - 1 - ctx if upward else ctx
    pl.semaphore_wait(barrier, peers - 1 + jnp.minimum(beyond, REACH))


def gather_kernel(
    shards,
    plan,
    q_in,
    k_in,
    v_in,
    g_in,
    d_in,
    q_out,
    k_out,
    v_out,
    g_out,
    d_out,
    send_sem,
    recv_sem,
    local_sem,
    halo_send,
    halo_recv,
):
    ctx, head = lax.axis_index("ctx"), lax.axis_index("head")
    part = q_in.shape[0]
    rows = q_out.shape[0]
    peers = rows // part
    halo = k_out.shape[0] - rows
    k_out[:halo, :] = jnp.zeros((halo, HEAD_DIM), k_out.dtype)
    v_out[:halo, :] = jnp.zeros((halo, HEAD_DIM), v_out.dtype)
    meet(shards, peers, True)

    def columns(ref, owner):
        width = ref.shape[1] // peers
        return ref.at[:, pl.ds(pl.multiple_of(owner * width, width), width)]

    def own_rows(ref, owner, first):
        return ref.at[pl.ds(pl.multiple_of(first + owner * part, part), part), :]

    pairs = (
        (lambda to: columns(k_in, to), lambda of: own_rows(k_out, of, halo)),
        (lambda to: columns(v_in, to), lambda of: own_rows(v_out, of, halo)),
        (lambda to: d_in.at[to], lambda of: d_out.at[of]),
        (lambda to: columns(q_in, to), lambda of: own_rows(q_out, of, 0)),
        (lambda to: columns(g_in, to), lambda of: own_rows(g_out, of, 0)),
    )

    def exchange(index, step):
        to = lax.rem(head + step, peers)
        source, target = pairs[index]
        return pltpu.make_async_remote_copy(
            src_ref=source(to),
            dst_ref=target(head),
            send_sem=send_sem.at[index, step],
            recv_sem=recv_sem.at[index, step],
            device_id=(ctx, to),
            device_id_type=MESH,
        )

    def keep(index):
        source, target = pairs[index]
        return pltpu.make_async_copy(source(head), target(head), local_sem.at[index])

    def arrived(index, step):
        source, target = pairs[index]
        of = lax.rem(head + peers - step, peers)
        pltpu.make_async_remote_copy(
            src_ref=source(head),
            dst_ref=target(of),
            send_sem=send_sem.at[index, step],
            recv_sem=recv_sem.at[index, step],
            device_id=(ctx, of),
            device_id_type=MESH,
        ).wait_recv()

    for index in range(5):
        keep(index).start()
        for step in range(1, peers):
            exchange(index, step).start()
    for index in range(2):
        keep(index).wait()
        for step in range(1, peers):
            arrived(index, step)

    def halo_copy(run, which):
        distance, first, end, _ = plan[run]
        ref = (k_out, v_out)[which]
        return pltpu.make_async_remote_copy(
            src_ref=ref.at[halo + first : halo + end, :],
            dst_ref=ref.at[halo - distance * rows + first : halo - distance * rows + end, :],
            send_sem=halo_send.at[run, which],
            recv_sem=halo_recv.at[run, which],
            device_id=(ctx + distance, head),
            device_id_type=MESH,
        )

    for run, (distance, first, end, senders) in enumerate(plan):

        @pl.when(is_one_of(ctx, senders, shards))
        def _():
            for which in range(2):
                halo_copy(run, which).start()

    for index in range(2, 5):
        keep(index).wait()
        for step in range(1, peers):
            arrived(index, step)
    for run, (distance, first, end, senders) in enumerate(plan):

        @pl.when(is_one_of(ctx, senders, shards))
        def _():
            for which in range(2):
                halo_copy(run, which).wait_send()

        @pl.when(is_one_of(ctx - distance, senders, shards) & (ctx >= distance))
        def _():
            for which in range(2):
                halo_copy(run, which).wait_recv()

    for index in range(5):
        for step in range(1, peers):
            exchange(index, step).wait_send()


def gather(shards, plan, queries, keys, values, grad_out, delta):
    peers = delta.shape[0]
    rows = queries.shape[0] * peers
    window = (REACH + 1) * rows + TILE
    width = queries.shape[1] // peers
    low = jnp.bfloat16
    return pl.pallas_call(
        functools.partial(gather_kernel, shards, plan),
        out_shape=(
            jax.ShapeDtypeStruct((rows, width), low),
            jax.ShapeDtypeStruct((window, HEAD_DIM), low),
            jax.ShapeDtypeStruct((window, HEAD_DIM), low),
            jax.ShapeDtypeStruct((rows, width), low),
            jax.ShapeDtypeStruct(delta.shape, jnp.float32),
        ),
        in_specs=[ANYWHERE] * 4 + [VMEM],
        out_specs=(VMEM,) * 5,
        scratch_shapes=[
            pltpu.SemaphoreType.DMA((5, peers)),
            pltpu.SemaphoreType.DMA((5, peers)),
            pltpu.SemaphoreType.DMA((5,)),
            pltpu.SemaphoreType.DMA((len(plan), 2)),
            pltpu.SemaphoreType.DMA((len(plan), 2)),
        ],
        compiler_params=pltpu.CompilerParams(
            collective_id=1,
            has_side_effects=True,
            vmem_limit_bytes=32 * 1024 * 1024,
        ),
        name="gather",
    )(queries, keys, values, grad_out, delta)


def attention_kernel(
    first_row,
    q_ref,
    g_ref,
    k_ref,
    v_ref,
    delta_ref,
    start_ref,
    dq_ref,
    dk_ref,
    dv_ref,
    kt_ref,
    score_ref,
    turned_ref,
):
    rows = q_ref.shape[0]
    heads = range(q_ref.shape[1] // HEAD_DIM)
    halo = k_ref.shape[0] - rows
    parts = TILE // delta_ref.shape[2]
    columns = [slice(head * HEAD_DIM, (head + 1) * HEAD_DIM) for head in heads]
    dk_ref[...] = jnp.zeros_like(dk_ref)
    dv_ref[...] = jnp.zeros_like(dv_ref)
    key_offset = lax.broadcasted_iota(jnp.int32, (STEP, TILE), 0)
    query_offset = lax.broadcasted_iota(jnp.int32, (1, TILE), 1)

    def turn(tile, carry):
        at = pl.ds(pl.multiple_of(tile * TILE, TILE), TILE)
        kt_ref[:, at] = k_ref[at, :].T
        return carry

    lax.fori_loop(jnp.maximum(first_row[0] // TILE - 1, 0), k_ref.shape[0] // TILE, turn, 0)

    def query_block(block, carry):
        q_at = pl.ds(pl.multiple_of(block * TILE, TILE), TILE)
        end = halo + (block + 1) * TILE
        count = (end - first_row[block] + STEP - 1) // STEP
        start = start_ref[:, q_at]
        last = query_offset + (end - TILE)
        deltas = [
            jnp.concatenate(
                [delta_ref[block * parts + part, head : head + 1, :] for part in range(parts)],
                axis=1,
            )
            for head in heads
        ]

        def key_rows(step):
            return pl.multiple_of(end - (step + 1) * STEP, TILE)

        def score_step(step, tops):
            first = key_rows(step)
            at = pl.ds(first, STEP)
            keys = k_ref[at, :]
            place = key_offset + first
            allowed = (place >= start) & (place <= last)
            new_tops = []
            for head in heads:
                scores = contract_last(keys, q_ref[q_at, columns[head]]) * (ATT_SCALE * LOG2E)
                scores = jnp.where(allowed, scores, NEG_FILL)
                score_ref[head, at, :] = scores
                tall = jnp.max(scores.reshape(STEP // 8, 8, TILE), axis=0)
                new_tops.append(jnp.maximum(tops[head], tall))
            return tuple(new_tops)

        none = jnp.full((8, TILE), NEG_FILL, jnp.float32)
        tops = lax.fori_loop(0, count, score_step, tuple(none for _ in heads))
        tops = [jnp.max(top, axis=0, keepdims=True) for top in tops]

        def sum_step(step, totals):
            at = pl.ds(key_rows(step), STEP)
            new_totals = []
            for head in heads:
                powers = jnp.exp2(score_ref[head, at, :] - tops[head])
                new_totals.append(
                    totals[head] + jnp.sum(powers.reshape(STEP // 8, 8, TILE), axis=0)
                )
            return tuple(new_totals)

        zero = jnp.zeros((8, TILE), jnp.float32)
        totals = lax.fori_loop(0, count, sum_step, tuple(zero for _ in heads))
        log_totals = [
            tops[head] + jnp.log2(jnp.sum(totals[head], axis=0, keepdims=True)) for head in heads
        ]
        turned_ref[...] = jnp.zeros_like(turned_ref)

        def grad_step(step, carry):
            at = pl.ds(key_rows(step), STEP)
            vals = v_ref[at, :]
            keys_turned = kt_ref[:, at]
            val_parts, key_parts = [], []
            for head in heads:
                q = q_ref[q_at, columns[head]]
                g = g_ref[q_at, columns[head]]
                probs = jnp.exp2(score_ref[head, at, :] - log_totals[head])
                grad_probs = contract_last(vals, g)
                grad_scores = (probs * (grad_probs - deltas[head])).astype(jnp.bfloat16)
                val_parts.append(contract_inner(probs.astype(jnp.bfloat16), g))
                key_parts.append(contract_inner(grad_scores, q))
                turned_ref[head] += contract_inner(keys_turned, grad_scores)
            dv_ref[at, :] += sum(val_parts[1:], val_parts[0])
            dk_ref[at, :] += sum(key_parts[1:], key_parts[0])
            return carry

        lax.fori_loop(0, count, grad_step, 0)
        for head in heads:
            dq_ref[q_at, columns[head]] = (turned_ref[head].T * ATT_SCALE).astype(jnp.bfloat16)
        return carry

    lax.fori_loop(0, rows // TILE, query_block, 0)


def attention(first_row, q, g, keys, vals, delta, starts):
    window = keys.shape[0]
    heads = q.shape[1] // HEAD_DIM
    return pl.pallas_call(
        attention_kernel,
        out_shape=(
            jax.ShapeDtypeStruct(q.shape, jnp.bfloat16),
            jax.ShapeDtypeStruct(keys.shape, jnp.float32),
            jax.ShapeDtypeStruct(keys.shape, jnp.float32),
        ),
        in_specs=[pl.BlockSpec(memory_space=pltpu.SMEM)] + [VMEM] * 6,
        out_specs=(VMEM,) * 3,
        scratch_shapes=[
            pltpu.VMEM((HEAD_DIM, window), jnp.bfloat16),
            pltpu.VMEM((heads, window, TILE), jnp.float32),
            pltpu.VMEM((heads, HEAD_DIM, TILE), jnp.float32),
        ],
        compiler_params=pltpu.CompilerParams(vmem_limit_bytes=44 * 1024 * 1024),
        name="attention",
    )(first_row, q, g, keys, vals, delta, starts)


def scatter_kernel(
    shards,
    plan,
    dq_in,
    dk_in,
    dv_in,
    dq_out,
    dk_out,
    dv_out,
    low_ref,
    got_ref,
    total_ref,
    sum_ref,
    send_sem,
    recv_sem,
    local_sem,
    halo_send,
    halo_recv,
):
    ctx, head = lax.axis_index("ctx"), lax.axis_index("head")
    part = dq_out.shape[0]
    rows = dq_in.shape[0]
    peers = rows // part
    halo = dk_in.shape[0] - rows
    meet(shards, peers, False)

    def columns(ref, owner):
        width = ref.shape[1] // peers
        return ref.at[:, pl.ds(pl.multiple_of(owner * width, width), width)]

    def row_part(ref, owner):
        return ref.at[pl.ds(pl.multiple_of(owner * part, part), part), :]

    pairs = (
        (lambda to: row_part(dq_in, to), lambda of: columns(dq_out, of)),
        (lambda to: row_part(sum_ref.at[0], to), lambda of: columns(dk_out, of)),
        (lambda to: row_part(sum_ref.at[1], to), lambda of: columns(dv_out, of)),
    )

    def exchange(index, step):
        to = lax.rem(head + step, peers)
        source, target = pairs[index]
        return pltpu.make_async_remote_copy(
            src_ref=source(to),
            dst_ref=target(head),
            send_sem=send_sem.at[index, step],
            recv_sem=recv_sem.at[index, step],
            device_id=(ctx, to),
            device_id_type=MESH,
        )

    def keep(index):
        source, target = pairs[index]
        return pltpu.make_async_copy(source(head), target(head), local_sem.at[index])

    def arrived(index, step):
        source, target = pairs[index]
        of = lax.rem(head + peers - step, peers)
        pltpu.make_async_remote_copy(
            src_ref=source(head),
            dst_ref=target(of),
            send_sem=send_sem.at[index, step],
            recv_sem=recv_sem.at[index, step],
            device_id=(ctx, of),
            device_id_type=MESH,
        ).wait_recv()

    def halo_copy(run, which):
        distance, first, end, _ = plan[run]
        base = halo - distance * rows
        return pltpu.make_async_remote_copy(
            src_ref=low_ref.at[which, base + first : base + end, :],
            dst_ref=got_ref.at[which, base + first : base + end, :],
            send_sem=halo_send.at[run, which],
            recv_sem=halo_recv.at[run, which],
            device_id=(ctx - distance, head),
            device_id_type=MESH,
        )

    for run, (distance, first, end, senders) in enumerate(plan):

        @pl.when(is_one_of(ctx - distance, senders, shards) & (ctx >= distance))
        def _():
            at = slice(halo - distance * rows + first, halo - distance * rows + end)
            low_ref[0, at, :] = (dk_in[at, :] * ATT_SCALE).astype(jnp.bfloat16)
            low_ref[1, at, :] = dv_in[at, :].astype(jnp.bfloat16)
            for which in range(2):
                halo_copy(run, which).start()

    keep(0).start()
    for step in range(1, peers):
        exchange(0, step).start()
    total_ref[0] = dk_in[halo:, :] * ATT_SCALE
    total_ref[1] = dv_in[halo:, :]

    for run, (distance, first, end, senders) in enumerate(plan):

        @pl.when(is_one_of(ctx, senders, shards))
        def _():
            got = slice(halo - distance * rows + first, halo - distance * rows + end)
            own = slice(first, end)
            for which in range(2):
                halo_copy(run, which).wait_recv()
                total_ref[which, own, :] += got_ref[which, got, :].astype(jnp.float32)

    sum_ref[...] = total_ref[...].astype(jnp.bfloat16)
    for index in (1, 2):
        keep(index).start()
        for step in range(1, peers):
            exchange(index, step).start()
    for run, (distance, first, end, senders) in enumerate(plan):

        @pl.when(is_one_of(ctx - distance, senders, shards) & (ctx >= distance))
        def _():
            for which in range(2):
                halo_copy(run, which).wait_send()

    for index in range(3):
        keep(index).wait()
        for step in range(1, peers):
            arrived(index, step)
            exchange(index, step).wait_send()


def scatter(shards, plan, peers, dq, dk, dv):
    rows, width = dq.shape
    window = dk.shape[0]
    low = jnp.bfloat16
    return pl.pallas_call(
        functools.partial(scatter_kernel, shards, plan),
        out_shape=(
            jax.ShapeDtypeStruct((rows // peers, width * peers), low),
            jax.ShapeDtypeStruct((rows // peers, HEAD_DIM * peers), low),
            jax.ShapeDtypeStruct((rows // peers, HEAD_DIM * peers), low),
        ),
        in_specs=[VMEM] * 3,
        out_specs=(ANYWHERE,) * 3,
        scratch_shapes=[
            pltpu.VMEM((2, window - rows, HEAD_DIM), low),
            pltpu.VMEM((2, window - rows, HEAD_DIM), low),
            pltpu.VMEM((2, rows, HEAD_DIM), jnp.float32),
            pltpu.VMEM((2, rows, HEAD_DIM), low),
            pltpu.SemaphoreType.DMA((3, peers)),
            pltpu.SemaphoreType.DMA((3, peers)),
            pltpu.SemaphoreType.DMA((3,)),
            pltpu.SemaphoreType.DMA((len(plan), 2)),
            pltpu.SemaphoreType.DMA((len(plan), 2)),
        ],
        compiler_params=pltpu.CompilerParams(
            collective_id=2,
            has_side_effects=True,
            vmem_limit_bytes=32 * 1024 * 1024,
        ),
        name="scatter",
    )(dq, dk, dv)


def first_tiles(ctx, block, shards, rows, reach_tiles):
    own = rows // TILE
    half = own // 2
    firsts = long_firsts(shards)
    second = is_one_of(ctx, tuple(first + 1 for first in firsts), shards)
    third = is_one_of(ctx, tuple(first + 2 for first in firsts), shards)
    low = jnp.where(second, jnp.minimum(reach_tiles - half, reach_tiles + block - 1), reach_tiles + block - 1)
    low = jnp.where(ctx == 0, reach_tiles, low)
    return jnp.where(third, reach_tiles - own - half, low)


def whole_kernel(
    shards,
    plan,
    q_in,
    k_in,
    v_in,
    g_in,
    d_in,
    lengths_ref,
    dq_out,
    dk_out,
    dv_out,
    q_buf,
    g_buf,
    k_win,
    v_win,
    d_buf,
    start_ref,
    kt_ref,
    score_ref,
    probs_ref,
    grads_ref,
    q_stack,
    g_stack,
    turned_ref,
    dk_acc,
    dv_acc,
    dq_buf,
    low_ref,
    got_ref,
    total_ref,
    sum_ref,
    send_sem,
    recv_sem,
    local_sem,
    halo_send,
    halo_recv,
    back_send,
    back_recv,
):
    ctx, head = lax.axis_index("ctx"), lax.axis_index("head")
    part = q_in.shape[0]
    rows, width = q_buf.shape
    peers = rows // part
    halo = k_win.shape[0] - rows
    half_width = width // 2
    pair_heads = range(half_width // HEAD_DIM)
    stacks = [slice(one * TILE, (one + 1) * TILE) for one in pair_heads]
    k_win[:halo, :] = jnp.zeros((halo, HEAD_DIM), k_win.dtype)
    v_win[:halo, :] = jnp.zeros((halo, HEAD_DIM), v_win.dtype)

    barrier = pltpu.get_barrier_semaphore()
    for step in range(1, peers):
        pl.semaphore_signal(
            barrier, inc=1, device_id=(ctx, lax.rem(head + step, peers)), device_id_type=MESH
        )
    for distance in (1, 2):

        @pl.when(ctx >= distance)
        def _():
            pl.semaphore_signal(
                barrier, inc=1, device_id=(ctx - distance, head), device_id_type=MESH
            )

        @pl.when(ctx < shards - distance)
        def _():
            pl.semaphore_signal(
                barrier, inc=1, device_id=(ctx + distance, head), device_id_type=MESH
            )

    around = jnp.minimum(shards - 1 - ctx, REACH) + jnp.minimum(ctx, REACH)
    pl.semaphore_wait(barrier, peers - 1 + around)

    def columns(ref, owner, offset, size):
        stride = ref.shape[1] // peers
        return ref.at[:, pl.ds(pl.multiple_of(owner * stride + offset, size), size)]

    def own_rows(ref, owner, first):
        return ref.at[pl.ds(pl.multiple_of(first + owner * part, part), part), :]

    def own_pair(ref, owner, pair):
        at = pl.ds(pl.multiple_of(owner * part, part), part)
        return ref.at[at, pair * half_width : (pair + 1) * half_width]

    def paired_in(source, target, pair):
        return (
            lambda to: columns(source, to, pair * half_width, half_width),
            lambda of: own_pair(target, of, pair),
        )

    def paired_out(source, target, pair):
        return (
            lambda to: own_pair(source, to, pair),
            lambda of: columns(target, of, pair * half_width, half_width),
        )

    routes = (
        (lambda to: columns(k_in, to, 0, HEAD_DIM), lambda of: own_rows(k_win, of, halo)),
        (lambda to: columns(v_in, to, 0, HEAD_DIM), lambda of: own_rows(v_win, of, halo)),
        (lambda to: d_in.at[to], lambda of: d_buf.at[of]),
        paired_in(q_in, q_buf, 0),
        paired_in(g_in, g_buf, 0),
        paired_in(q_in, q_buf, 1),
        paired_in(g_in, g_buf, 1),
        paired_out(dq_buf, dq_out, 0),
        paired_out(dq_buf, dq_out, 1),
        (lambda to: own_rows(sum_ref.at[0], to, 0), lambda of: columns(dk_out, of, 0, HEAD_DIM)),
        (lambda to: own_rows(sum_ref.at[1], to, 0), lambda of: columns(dv_out, of, 0, HEAD_DIM)),
    )

    def exchange(index, step):
        to = lax.rem(head + step, peers)
        source, target = routes[index]
        return pltpu.make_async_remote_copy(
            src_ref=source(to),
            dst_ref=target(head),
            send_sem=send_sem.at[index, step],
            recv_sem=recv_sem.at[index, step],
            device_id=(ctx, to),
            device_id_type=MESH,
        )

    def keep(index):
        source, target = routes[index]
        return pltpu.make_async_copy(source(head), target(head), local_sem.at[index])

    def begin(*indices):
        for index in indices:
            keep(index).start()
            for step in range(1, peers):
                exchange(index, step).start()

    def arrived(*indices):
        for index in indices:
            keep(index).wait()
            source, target = routes[index]
            for step in range(1, peers):
                of = lax.rem(head + peers - step, peers)
                pltpu.make_async_remote_copy(
                    src_ref=source(head),
                    dst_ref=target(of),
                    send_sem=send_sem.at[index, step],
                    recv_sem=recv_sem.at[index, step],
                    device_id=(ctx, of),
                    device_id_type=MESH,
                ).wait_recv()

    def halo_copy(run, which):
        distance, first, end, _ = plan[run]
        ref = (k_win, v_win)[which]
        base = halo - distance * rows
        return pltpu.make_async_remote_copy(
            src_ref=ref.at[halo + first : halo + end, :],
            dst_ref=ref.at[base + first : base + end, :],
            send_sem=halo_send.at[run, which],
            recv_sem=halo_recv.at[run, which],
            device_id=(ctx + distance, head),
            device_id_type=MESH,
        )

    def back_copy(run, which):
        distance, first, end, _ = plan[run]
        base = halo - distance * rows
        return pltpu.make_async_remote_copy(
            src_ref=low_ref.at[which, base + first : base + end, :],
            dst_ref=got_ref.at[which, base + first : base + end, :],
            send_sem=back_send.at[run, which],
            recv_sem=back_recv.at[run, which],
            device_id=(ctx - distance, head),
            device_id_type=MESH,
        )

    def for_runs(body, upward):
        for run, (distance, first, end, senders) in enumerate(plan):
            if upward:
                here = is_one_of(ctx, senders, shards)
            else:
                here = is_one_of(ctx - distance, senders, shards) & (ctx >= distance)

            @pl.when(here)
            def _():
                body(run, distance, first, end)

    begin(0, 1, 2, 3, 4)

    docs = lengths_ref.shape[1]
    before = lax.broadcasted_iota(jnp.int32, (docs, docs), 1) < lax.broadcasted_iota(
        jnp.int32, (docs, docs), 0
    )
    lengths = lengths_ref[...].astype(jnp.float32)
    doc_starts = jnp.sum(jnp.where(before, lengths, 0.0), axis=1, keepdims=True)
    doc_starts = doc_starts - (ctx * rows - halo).astype(jnp.float32)
    places = lax.broadcasted_iota(jnp.int32, (1, rows), 1).astype(jnp.float32) + float(halo)
    starts = jnp.max(jnp.where(doc_starts <= places, doc_starts, -1e9), axis=0, keepdims=True)
    start_ref[...] = starts.astype(jnp.int32)
    dk_acc[...] = jnp.zeros_like(dk_acc)
    dv_acc[...] = jnp.zeros_like(dv_acc)

    arrived(0, 1)
    for_runs(lambda run, *_: [halo_copy(run, which).start() for which in range(2)], True)
    begin(5, 6)

    reach_tiles = halo // TILE
    key_offset = lax.broadcasted_iota(jnp.int32, (STEP, TILE), 0)
    query_offset = lax.broadcasted_iota(jnp.int32, (1, TILE), 1)
    parts = TILE // part

    def turn(tile, carry):
        at = pl.ds(pl.multiple_of(tile * TILE, TILE), TILE)
        kt_ref[:, at] = k_win[at, :].T
        return carry

    def attend(pair):
        def query_block(block, carry):
            q_at = pl.ds(pl.multiple_of(block * TILE, TILE), TILE)
            end = halo + (block + 1) * TILE
            tiles = reach_tiles + block + 1 - first_tiles(ctx, block, shards, rows, reach_tiles)
            count = lax.div(tiles + 1, STEP // TILE)
            start = start_ref[:, q_at]
            last = query_offset + (end - TILE)
            deltas = []
            for one in pair_heads:
                which = pair * len(pair_heads) + one
                cols = slice(which * HEAD_DIM, (which + 1) * HEAD_DIM)
                q_stack[stacks[one], :] = q_buf[q_at, cols]
                g_stack[stacks[one], :] = g_buf[q_at, cols]
                deltas.append(
                    jnp.concatenate(
                        [d_buf[block * parts + p, which : which + 1, :] for p in range(parts)],
                        axis=1,
                    )
                )

            def key_rows(step):
                return pl.multiple_of(end - (step + 1) * STEP, TILE)

            def score_step(step, tops):
                first = key_rows(step)
                at = pl.ds(first, STEP)
                keys = k_win[at, :]
                place = key_offset + first
                allowed = (place >= start) & (place <= last)
                new_tops = []
                for one in pair_heads:
                    scores = contract_last(keys, q_stack[stacks[one], :]) * (ATT_SCALE * LOG2E)
                    scores = jnp.where(allowed, scores, NEG_FILL)
                    score_ref[at, stacks[one]] = scores
                    tall = jnp.max(scores.reshape(STEP // 8, 8, TILE), axis=0)
                    new_tops.append(jnp.maximum(tops[one], tall))
                return tuple(new_tops)

            none = jnp.full((8, TILE), NEG_FILL, jnp.float32)
            tops = lax.fori_loop(0, count, score_step, tuple(none for _ in pair_heads))
            tops = [jnp.max(top, axis=0, keepdims=True) for top in tops]

            def sum_step(step, totals):
                at = pl.ds(key_rows(step), STEP)
                new_totals = []
                for one in pair_heads:
                    powers = jnp.exp2(score_ref[at, stacks[one]] - tops[one])
                    tall = jnp.sum(powers.reshape(STEP // 8, 8, TILE), axis=0)
                    new_totals.append(totals[one] + tall)
                return tuple(new_totals)

            zero = jnp.zeros((8, TILE), jnp.float32)
            totals = lax.fori_loop(0, count, sum_step, tuple(zero for _ in pair_heads))
            log_totals = [
                tops[one] + jnp.log2(jnp.sum(totals[one], axis=0, keepdims=True))
                for one in pair_heads
            ]
            turned_ref[...] = jnp.zeros_like(turned_ref)

            def grad_step(step, carry):
                at = pl.ds(key_rows(step), STEP)
                vals = v_win[at, :]
                for one in pair_heads:
                    probs = jnp.exp2(score_ref[at, stacks[one]] - log_totals[one])
                    grad_probs = contract_last(vals, g_stack[stacks[one], :])
                    grads = (probs * (grad_probs - deltas[one])).astype(jnp.bfloat16)
                    probs_ref[:, stacks[one]] = probs.astype(jnp.bfloat16)
                    grads_ref[:, stacks[one]] = grads
                dv_acc[at, :] += contract_inner(probs_ref[...], g_stack[...])
                dk_acc[at, :] += contract_inner(grads_ref[...], q_stack[...])
                turned_ref[...] += contract_inner(kt_ref[:, at], grads_ref[...])
                return carry

            lax.fori_loop(0, count, grad_step, 0)
            for one in pair_heads:
                which = pair * len(pair_heads) + one
                dq = turned_ref[:, stacks[one]].T * ATT_SCALE
                dq_buf[q_at, which * HEAD_DIM : (which + 1) * HEAD_DIM] = dq.astype(jnp.bfloat16)
            return carry

        lax.fori_loop(0, rows // TILE, query_block, 0)

    arrived(2, 3, 4)
    for_runs(lambda run, *_: [halo_copy(run, which).wait_recv() for which in range(2)], False)
    lowest = first_tiles(ctx, 0, shards, rows, reach_tiles) - 1
    lax.fori_loop(lowest, reach_tiles + rows // TILE, turn, 0)
    attend(0)
    begin(7)
    arrived(5, 6)
    attend(1)

    def send_back(run, distance, first, end):
        at = slice(halo - distance * rows + first, halo - distance * rows + end)
        low_ref[0, at, :] = (dk_acc[at, :] * ATT_SCALE).astype(jnp.bfloat16)
        low_ref[1, at, :] = dv_acc[at, :].astype(jnp.bfloat16)
        for which in range(2):
            back_copy(run, which).start()

    def take_back(run, distance, first, end):
        got = slice(halo - distance * rows + first, halo - distance * rows + end)
        for which in range(2):
            back_copy(run, which).wait_recv()
            total_ref[which, first:end, :] += got_ref[which, got, :].astype(jnp.float32)

    for_runs(send_back, False)
    begin(8)
    total_ref[0] = dk_acc[halo:, :] * ATT_SCALE
    total_ref[1] = dv_acc[halo:, :]
    for_runs(take_back, True)
    sum_ref[...] = total_ref[...].astype(jnp.bfloat16)
    begin(9, 10)
    for_runs(lambda run, *_: [halo_copy(run, which).wait_send() for which in range(2)], True)
    for_runs(lambda run, *_: [back_copy(run, which).wait_send() for which in range(2)], False)
    arrived(7, 8, 9, 10)
    for index in range(len(routes)):
        for step in range(1, peers):
            exchange(index, step).wait_send()


def whole(shards, plan, queries, keys, values, grad_out, delta, doc_lengths):
    peers = delta.shape[0]
    part = queries.shape[0]
    rows = part * peers
    width = queries.shape[1] // peers
    window = (REACH + 1) * rows + TILE
    low, full = jnp.bfloat16, jnp.float32
    wide = width // 2 // HEAD_DIM * TILE
    dma = pltpu.SemaphoreType.DMA
    return pl.pallas_call(
        functools.partial(whole_kernel, shards, plan),
        out_shape=(
            jax.ShapeDtypeStruct(queries.shape, low),
            jax.ShapeDtypeStruct(keys.shape, low),
            jax.ShapeDtypeStruct(values.shape, low),
        ),
        in_specs=[ANYWHERE] * 4 + [VMEM] * 2,
        out_specs=(ANYWHERE,) * 3,
        scratch_shapes=[
            pltpu.VMEM((rows, width), low),
            pltpu.VMEM((rows, width), low),
            pltpu.VMEM((window, HEAD_DIM), low),
            pltpu.VMEM((window, HEAD_DIM), low),
            pltpu.VMEM(delta.shape, full),
            pltpu.VMEM((1, rows), jnp.int32),
            pltpu.VMEM((HEAD_DIM, window), low),
            pltpu.VMEM((window, wide), full),
            pltpu.VMEM((STEP, wide), low),
            pltpu.VMEM((STEP, wide), low),
            pltpu.VMEM((wide, HEAD_DIM), low),
            pltpu.VMEM((wide, HEAD_DIM), low),
            pltpu.VMEM((HEAD_DIM, wide), full),
            pltpu.VMEM((window, HEAD_DIM), full),
            pltpu.VMEM((window, HEAD_DIM), full),
            pltpu.VMEM((rows, width), low),
            pltpu.VMEM((2, window - rows, HEAD_DIM), low),
            pltpu.VMEM((2, window - rows, HEAD_DIM), low),
            pltpu.VMEM((2, rows, HEAD_DIM), full),
            pltpu.VMEM((2, rows, HEAD_DIM), low),
            dma((11, peers)),
            dma((11, peers)),
            dma((11,)),
            dma((len(plan), 2)),
            dma((len(plan), 2)),
            dma((len(plan), 2)),
            dma((len(plan), 2)),
        ],
        compiler_params=pltpu.CompilerParams(
            collective_id=0, has_side_effects=True, vmem_limit_bytes=44 * 1024 * 1024
        ),
        name="whole",
    )(queries, keys, values, grad_out, delta, doc_lengths[None])


def on_device(queries, keys, values, grad_out, delta, doc_lengths):
    shards, peers = lax.axis_size("ctx"), lax.axis_size("head")
    rows = queries.shape[0] * peers
    delta = delta.reshape(peers, delta.shape[0] // peers, delta.shape[1])
    slots = jnp.arange(doc_lengths.shape[0], dtype=jnp.int32)
    doc_starts = jnp.sum(jnp.where(slots[:, None] < slots[None, :], doc_lengths[:, None], 0), axis=0)

    def start_at(places):
        return jnp.max(
            jnp.where(doc_starts[:, None] <= places[None, :], doc_starts[:, None], 0), axis=0
        )

    blocks = np.arange(shards * rows // TILE)
    lowest = jnp.asarray(short_reach(blocks, shards, rows), jnp.int32)
    fits = jnp.all(start_at(jnp.asarray(blocks * TILE, jnp.int32)) >= lowest)

    def in_one(*operands):
        return whole(shards, halo_plan(shards, rows, True), *operands, doc_lengths)

    def in_three(*operands):
        plan = halo_plan(shards, rows, False)
        base = lax.axis_index("ctx") * rows
        starts = start_at(base + jnp.arange(rows, dtype=jnp.int32)) - (base - REACH * rows - TILE)
        q, k, v, g, d = gather(shards, plan, *operands)
        dq, dk, dv = attention(starts[::TILE], q, g, k, v, d, starts[None])
        return scatter(shards, plan, peers, dq, dk, dv)

    return lax.cond(fits, in_one, in_three, queries, keys, values, grad_out, delta)


def solution(mesh):
    rows = P(("ctx", "head"), None)
    return jax.shard_map(
        on_device,
        mesh=mesh,
        in_specs=(rows, rows, rows, rows, P(None, ("ctx", "head")), P()),
        out_specs=(rows, rows, rows),
        check_vma=False,
    )
```

```python
import functools

import jax
import jax.numpy as jnp
from jax import lax
from jax.experimental import pallas as pl
from jax.experimental.pallas import tpu as pltpu
from jax.sharding import PartitionSpec as P

HEAD_DIM = 128
TILE = 256
STEP = 512
BLOCK = 512
REACH = 2
NEG_FILL = -1e30
ATT_SCALE = HEAD_DIM ** (-0.5)
LOG2E = 1.4426950408889634
MESH = pl.DeviceIdType.MESH
VMEM = pl.BlockSpec(memory_space=pltpu.VMEM)
ANYWHERE = pl.BlockSpec(memory_space=pl.ANY)


def long_firsts(shards):
    middle = shards // 2
    return (0, middle - 3, middle - 1, middle + 1, shards - 3)


def halo_plan(shards, rows, short):
    near = tuple(range(shards - 1))
    far = tuple(range(shards - 2))
    if not short:
        return ((1, 0, rows, near), (2, 0, rows, far))
    firsts = long_firsts(shards)
    seconds = tuple(first + 1 for first in firsts)
    half = rows // 2
    return (
        (1, rows - TILE, rows, near),
        (1, half, rows - TILE, tuple(sorted(set(firsts + seconds)))),
        (1, 0, half, seconds),
        (2, half, rows, firsts),
    )


def short_reach(blocks, shards, rows):
    shard = blocks // (rows // BLOCK)
    reach = jnp.where(shard == 0, 0, blocks * BLOCK - TILE)
    for first in long_firsts(shards):
        opening = first * rows + rows // 2
        holds = (shard == first + 1) | (shard == first + 2)
        reach = jnp.where(holds, jnp.minimum(reach, opening), reach)
    return reach


def is_one_of(index, members, shards):
    if members == tuple(range(len(members))):
        return index < len(members)
    return functools.reduce(jnp.logical_or, [index == member for member in members])


def contract_last(left, right):
    return lax.dot_general(
        left, right, (((1,), (1,)), ((), ())), preferred_element_type=jnp.float32
    )


def contract_inner(left, right):
    return jnp.dot(left, right, preferred_element_type=jnp.float32)


def meet(shards, peers, upward):
    ctx, head = lax.axis_index("ctx"), lax.axis_index("head")
    barrier = pltpu.get_barrier_semaphore()
    for step in range(1, peers):
        pl.semaphore_signal(
            barrier, inc=1, device_id=(ctx, lax.rem(head + step, peers)), device_id_type=MESH
        )
    for distance in (1, 2):
        other = ctx - distance if upward else ctx + distance
        there = ctx >= distance if upward else ctx < shards - distance

        @pl.when(there)
        def _():
            pl.semaphore_signal(barrier, inc=1, device_id=(other, head), device_id_type=MESH)

    beyond = shards - 1 - ctx if upward else ctx
    pl.semaphore_wait(barrier, peers - 1 + jnp.minimum(beyond, REACH))


def gather_kernel(
    shards,
    plan,
    q_in,
    k_in,
    v_in,
    g_in,
    d_in,
    q_out,
    k_out,
    v_out,
    g_out,
    d_out,
    send_sem,
    recv_sem,
    local_sem,
    halo_send,
    halo_recv,
):
    ctx, head = lax.axis_index("ctx"), lax.axis_index("head")
    part = q_in.shape[0]
    rows = q_out.shape[0]
    peers = rows // part
    halo = k_out.shape[0] - rows
    k_out[:halo, :] = jnp.zeros((halo, HEAD_DIM), k_out.dtype)
    v_out[:halo, :] = jnp.zeros((halo, HEAD_DIM), v_out.dtype)
    meet(shards, peers, True)

    def columns(ref, owner):
        width = ref.shape[1] // peers
        return ref.at[:, pl.ds(pl.multiple_of(owner * width, width), width)]

    def own_rows(ref, owner, first):
        return ref.at[pl.ds(pl.multiple_of(first + owner * part, part), part), :]

    pairs = (
        (lambda to: columns(k_in, to), lambda of: own_rows(k_out, of, halo)),
        (lambda to: columns(v_in, to), lambda of: own_rows(v_out, of, halo)),
        (lambda to: d_in.at[to], lambda of: d_out.at[of]),
        (lambda to: columns(q_in, to), lambda of: own_rows(q_out, of, 0)),
        (lambda to: columns(g_in, to), lambda of: own_rows(g_out, of, 0)),
    )

    def exchange(index, step):
        to = lax.rem(head + step, peers)
        source, target = pairs[index]
        return pltpu.make_async_remote_copy(
            src_ref=source(to),
            dst_ref=target(head),
            send_sem=send_sem.at[index, step],
            recv_sem=recv_sem.at[index, step],
            device_id=(ctx, to),
            device_id_type=MESH,
        )

    def keep(index):
        source, target = pairs[index]
        return pltpu.make_async_copy(source(head), target(head), local_sem.at[index])

    def arrived(index, step):
        source, target = pairs[index]
        of = lax.rem(head + peers - step, peers)
        pltpu.make_async_remote_copy(
            src_ref=source(head),
            dst_ref=target(of),
            send_sem=send_sem.at[index, step],
            recv_sem=recv_sem.at[index, step],
            device_id=(ctx, of),
            device_id_type=MESH,
        ).wait_recv()

    for index in range(5):
        keep(index).start()
        for step in range(1, peers):
            exchange(index, step).start()
    for index in range(2):
        keep(index).wait()
        for step in range(1, peers):
            arrived(index, step)

    def halo_copy(run, which):
        distance, first, end, _ = plan[run]
        ref = (k_out, v_out)[which]
        return pltpu.make_async_remote_copy(
            src_ref=ref.at[halo + first : halo + end, :],
            dst_ref=ref.at[halo - distance * rows + first : halo - distance * rows + end, :],
            send_sem=halo_send.at[run, which],
            recv_sem=halo_recv.at[run, which],
            device_id=(ctx + distance, head),
            device_id_type=MESH,
        )

    for run, (distance, first, end, senders) in enumerate(plan):

        @pl.when(is_one_of(ctx, senders, shards))
        def _():
            for which in range(2):
                halo_copy(run, which).start()

    for index in range(2, 5):
        keep(index).wait()
        for step in range(1, peers):
            arrived(index, step)
    for run, (distance, first, end, senders) in enumerate(plan):

        @pl.when(is_one_of(ctx, senders, shards))
        def _():
            for which in range(2):
                halo_copy(run, which).wait_send()

        @pl.when(is_one_of(ctx - distance, senders, shards) & (ctx >= distance))
        def _():
            for which in range(2):
                halo_copy(run, which).wait_recv()

    for index in range(5):
        for step in range(1, peers):
            exchange(index, step).wait_send()


def gather(shards, plan, queries, keys, values, grad_out, delta):
    peers = delta.shape[0]
    rows = queries.shape[0] * peers
    window = (REACH + 1) * rows + TILE
    width = queries.shape[1] // peers
    low = jnp.bfloat16
    return pl.pallas_call(
        functools.partial(gather_kernel, shards, plan),
        out_shape=(
            jax.ShapeDtypeStruct((rows, width), low),
            jax.ShapeDtypeStruct((window, HEAD_DIM), low),
            jax.ShapeDtypeStruct((window, HEAD_DIM), low),
            jax.ShapeDtypeStruct((rows, width), low),
            jax.ShapeDtypeStruct(delta.shape, jnp.float32),
        ),
        in_specs=[ANYWHERE] * 4 + [VMEM],
        out_specs=(VMEM,) * 5,
        scratch_shapes=[
            pltpu.SemaphoreType.DMA((5, peers)),
            pltpu.SemaphoreType.DMA((5, peers)),
            pltpu.SemaphoreType.DMA((5,)),
            pltpu.SemaphoreType.DMA((len(plan), 2)),
            pltpu.SemaphoreType.DMA((len(plan), 2)),
        ],
        compiler_params=pltpu.CompilerParams(
            collective_id=1,
            has_side_effects=True,
            vmem_limit_bytes=32 * 1024 * 1024,
        ),
        name="gather",
    )(queries, keys, values, grad_out, delta)


def attention_kernel(
    first_row,
    q_ref,
    g_ref,
    k_ref,
    v_ref,
    delta_ref,
    start_ref,
    dq_ref,
    dk_ref,
    dv_ref,
    kt_ref,
    score_ref,
    turned_ref,
):
    rows = q_ref.shape[0]
    heads = range(q_ref.shape[1] // HEAD_DIM)
    halo = k_ref.shape[0] - rows
    parts = TILE // delta_ref.shape[2]
    columns = [slice(head * HEAD_DIM, (head + 1) * HEAD_DIM) for head in heads]
    dk_ref[...] = jnp.zeros_like(dk_ref)
    dv_ref[...] = jnp.zeros_like(dv_ref)
    key_offset = lax.broadcasted_iota(jnp.int32, (STEP, TILE), 0)
    query_offset = lax.broadcasted_iota(jnp.int32, (1, TILE), 1)

    def turn(tile, carry):
        at = pl.ds(pl.multiple_of(tile * TILE, TILE), TILE)
        kt_ref[:, at] = k_ref[at, :].T
        return carry

    lax.fori_loop(jnp.maximum(first_row[0] // TILE - 1, 0), k_ref.shape[0] // TILE, turn, 0)

    def query_block(block, carry):
        q_at = pl.ds(pl.multiple_of(block * TILE, TILE), TILE)
        end = halo + (block + 1) * TILE
        count = (end - first_row[block] + STEP - 1) // STEP
        start = start_ref[:, q_at]
        last = query_offset + (end - TILE)
        deltas = [
            jnp.concatenate(
                [delta_ref[block * parts + part, head : head + 1, :] for part in range(parts)],
                axis=1,
            )
            for head in heads
        ]

        def key_rows(step):
            return pl.multiple_of(end - (step + 1) * STEP, TILE)

        def score_step(step, tops):
            first = key_rows(step)
            at = pl.ds(first, STEP)
            keys = k_ref[at, :]
            place = key_offset + first
            allowed = (place >= start) & (place <= last)
            new_tops = []
            for head in heads:
                scores = contract_last(keys, q_ref[q_at, columns[head]]) * (ATT_SCALE * LOG2E)
                scores = jnp.where(allowed, scores, NEG_FILL)
                score_ref[head, at, :] = scores
                tall = jnp.max(scores.reshape(STEP // 8, 8, TILE), axis=0)
                new_tops.append(jnp.maximum(tops[head], tall))
            return tuple(new_tops)

        none = jnp.full((8, TILE), NEG_FILL, jnp.float32)
        tops = lax.fori_loop(0, count, score_step, tuple(none for _ in heads))
        tops = [jnp.max(top, axis=0, keepdims=True) for top in tops]

        def sum_step(step, totals):
            at = pl.ds(key_rows(step), STEP)
            new_totals = []
            for head in heads:
                powers = jnp.exp2(score_ref[head, at, :] - tops[head])
                new_totals.append(
                    totals[head] + jnp.sum(powers.reshape(STEP // 8, 8, TILE), axis=0)
                )
            return tuple(new_totals)

        zero = jnp.zeros((8, TILE), jnp.float32)
        totals = lax.fori_loop(0, count, sum_step, tuple(zero for _ in heads))
        log_totals = [
            tops[head] + jnp.log2(jnp.sum(totals[head], axis=0, keepdims=True)) for head in heads
        ]
        turned_ref[...] = jnp.zeros_like(turned_ref)

        def grad_step(step, carry):
            at = pl.ds(key_rows(step), STEP)
            vals = v_ref[at, :]
            keys_turned = kt_ref[:, at]
            val_parts, key_parts = [], []
            for head in heads:
                q = q_ref[q_at, columns[head]]
                g = g_ref[q_at, columns[head]]
                probs = jnp.exp2(score_ref[head, at, :] - log_totals[head])
                grad_probs = contract_last(vals, g)
                grad_scores = (probs * (grad_probs - deltas[head])).astype(jnp.bfloat16)
                val_parts.append(contract_inner(probs.astype(jnp.bfloat16), g))
                key_parts.append(contract_inner(grad_scores, q))
                turned_ref[head] += contract_inner(keys_turned, grad_scores)
            dv_ref[at, :] += sum(val_parts[1:], val_parts[0])
            dk_ref[at, :] += sum(key_parts[1:], key_parts[0])
            return carry

        lax.fori_loop(0, count, grad_step, 0)
        for head in heads:
            dq_ref[q_at, columns[head]] = (turned_ref[head].T * ATT_SCALE).astype(jnp.bfloat16)
        return carry

    lax.fori_loop(0, rows // TILE, query_block, 0)


def attention(first_row, q, g, keys, vals, delta, starts):
    window = keys.shape[0]
    heads = q.shape[1] // HEAD_DIM
    return pl.pallas_call(
        attention_kernel,
        out_shape=(
            jax.ShapeDtypeStruct(q.shape, jnp.bfloat16),
            jax.ShapeDtypeStruct(keys.shape, jnp.float32),
            jax.ShapeDtypeStruct(keys.shape, jnp.float32),
        ),
        in_specs=[pl.BlockSpec(memory_space=pltpu.SMEM)] + [VMEM] * 6,
        out_specs=(VMEM,) * 3,
        scratch_shapes=[
            pltpu.VMEM((HEAD_DIM, window), jnp.bfloat16),
            pltpu.VMEM((heads, window, TILE), jnp.float32),
            pltpu.VMEM((heads, HEAD_DIM, TILE), jnp.float32),
        ],
        compiler_params=pltpu.CompilerParams(vmem_limit_bytes=44 * 1024 * 1024),
        name="attention",
    )(first_row, q, g, keys, vals, delta, starts)


def scatter_kernel(
    shards,
    plan,
    dq_in,
    dk_in,
    dv_in,
    dq_out,
    dk_out,
    dv_out,
    low_ref,
    got_ref,
    total_ref,
    sum_ref,
    send_sem,
    recv_sem,
    local_sem,
    halo_send,
    halo_recv,
):
    ctx, head = lax.axis_index("ctx"), lax.axis_index("head")
    part = dq_out.shape[0]
    rows = dq_in.shape[0]
    peers = rows // part
    halo = dk_in.shape[0] - rows
    meet(shards, peers, False)

    def columns(ref, owner):
        width = ref.shape[1] // peers
        return ref.at[:, pl.ds(pl.multiple_of(owner * width, width), width)]

    def row_part(ref, owner):
        return ref.at[pl.ds(pl.multiple_of(owner * part, part), part), :]

    pairs = (
        (lambda to: row_part(dq_in, to), lambda of: columns(dq_out, of)),
        (lambda to: row_part(sum_ref.at[0], to), lambda of: columns(dk_out, of)),
        (lambda to: row_part(sum_ref.at[1], to), lambda of: columns(dv_out, of)),
    )

    def exchange(index, step):
        to = lax.rem(head + step, peers)
        source, target = pairs[index]
        return pltpu.make_async_remote_copy(
            src_ref=source(to),
            dst_ref=target(head),
            send_sem=send_sem.at[index, step],
            recv_sem=recv_sem.at[index, step],
            device_id=(ctx, to),
            device_id_type=MESH,
        )

    def keep(index):
        source, target = pairs[index]
        return pltpu.make_async_copy(source(head), target(head), local_sem.at[index])

    def arrived(index, step):
        source, target = pairs[index]
        of = lax.rem(head + peers - step, peers)
        pltpu.make_async_remote_copy(
            src_ref=source(head),
            dst_ref=target(of),
            send_sem=send_sem.at[index, step],
            recv_sem=recv_sem.at[index, step],
            device_id=(ctx, of),
            device_id_type=MESH,
        ).wait_recv()

    def halo_copy(run, which):
        distance, first, end, _ = plan[run]
        base = halo - distance * rows
        return pltpu.make_async_remote_copy(
            src_ref=low_ref.at[which, base + first : base + end, :],
            dst_ref=got_ref.at[which, base + first : base + end, :],
            send_sem=halo_send.at[run, which],
            recv_sem=halo_recv.at[run, which],
            device_id=(ctx - distance, head),
            device_id_type=MESH,
        )

    for run, (distance, first, end, senders) in enumerate(plan):

        @pl.when(is_one_of(ctx - distance, senders, shards) & (ctx >= distance))
        def _():
            at = slice(halo - distance * rows + first, halo - distance * rows + end)
            low_ref[0, at, :] = (dk_in[at, :] * ATT_SCALE).astype(jnp.bfloat16)
            low_ref[1, at, :] = dv_in[at, :].astype(jnp.bfloat16)
            for which in range(2):
                halo_copy(run, which).start()

    keep(0).start()
    for step in range(1, peers):
        exchange(0, step).start()
    total_ref[0] = dk_in[halo:, :] * ATT_SCALE
    total_ref[1] = dv_in[halo:, :]

    for run, (distance, first, end, senders) in enumerate(plan):

        @pl.when(is_one_of(ctx, senders, shards))
        def _():
            got = slice(halo - distance * rows + first, halo - distance * rows + end)
            own = slice(first, end)
            for which in range(2):
                halo_copy(run, which).wait_recv()
                total_ref[which, own, :] += got_ref[which, got, :].astype(jnp.float32)

    sum_ref[...] = total_ref[...].astype(jnp.bfloat16)
    for index in (1, 2):
        keep(index).start()
        for step in range(1, peers):
            exchange(index, step).start()
    for run, (distance, first, end, senders) in enumerate(plan):

        @pl.when(is_one_of(ctx - distance, senders, shards) & (ctx >= distance))
        def _():
            for which in range(2):
                halo_copy(run, which).wait_send()

    for index in range(3):
        keep(index).wait()
        for step in range(1, peers):
            arrived(index, step)
            exchange(index, step).wait_send()


def scatter(shards, plan, peers, dq, dk, dv):
    rows, width = dq.shape
    window = dk.shape[0]
    low = jnp.bfloat16
    return pl.pallas_call(
        functools.partial(scatter_kernel, shards, plan),
        out_shape=(
            jax.ShapeDtypeStruct((rows // peers, width * peers), low),
            jax.ShapeDtypeStruct((rows // peers, HEAD_DIM * peers), low),
            jax.ShapeDtypeStruct((rows // peers, HEAD_DIM * peers), low),
        ),
        in_specs=[VMEM] * 3,
        out_specs=(ANYWHERE,) * 3,
        scratch_shapes=[
            pltpu.VMEM((2, window - rows, HEAD_DIM), low),
            pltpu.VMEM((2, window - rows, HEAD_DIM), low),
            pltpu.VMEM((2, rows, HEAD_DIM), jnp.float32),
            pltpu.VMEM((2, rows, HEAD_DIM), low),
            pltpu.SemaphoreType.DMA((3, peers)),
            pltpu.SemaphoreType.DMA((3, peers)),
            pltpu.SemaphoreType.DMA((3,)),
            pltpu.SemaphoreType.DMA((len(plan), 2)),
            pltpu.SemaphoreType.DMA((len(plan), 2)),
        ],
        compiler_params=pltpu.CompilerParams(
            collective_id=2,
            has_side_effects=True,
            vmem_limit_bytes=32 * 1024 * 1024,
        ),
        name="scatter",
    )(dq, dk, dv)


def first_tiles(ctx, block, shards, rows, reach_tiles):
    own = rows // TILE
    half = own // 2
    firsts = long_firsts(shards)
    second = is_one_of(ctx, tuple(first + 1 for first in firsts), shards)
    third = is_one_of(ctx, tuple(first + 2 for first in firsts), shards)
    low = reach_tiles + block * (BLOCK // TILE) - 1
    low = jnp.where(ctx == 0, reach_tiles, low)
    low = jnp.where(second, reach_tiles - half, low)
    return jnp.where(third, reach_tiles - own - half, low)


def whole_kernel(
    shards,
    plan,
    q_in,
    k_in,
    v_in,
    g_in,
    d_in,
    lengths_ref,
    dq_out,
    dk_out,
    dv_out,
    q_buf,
    g_buf,
    k_win,
    v_win,
    d_buf,
    start_ref,
    kt_ref,
    score_ref,
    probs_ref,
    grads_ref,
    q_stack,
    g_stack,
    turned_ref,
    dk_acc,
    dv_acc,
    dq_buf,
    low_ref,
    got_ref,
    total_ref,
    sum_ref,
    send_sem,
    recv_sem,
    local_sem,
    halo_send,
    halo_recv,
    back_send,
    back_recv,
):
    ctx, head = lax.axis_index("ctx"), lax.axis_index("head")
    part = q_in.shape[0]
    rows, width = q_buf.shape
    peers = rows // part
    halo = k_win.shape[0] - rows
    half_width = width // 2
    pair_heads = range(half_width // HEAD_DIM)
    stacks = [slice(one * BLOCK, (one + 1) * BLOCK) for one in pair_heads]
    k_win[:halo, :] = jnp.zeros((halo, HEAD_DIM), k_win.dtype)
    v_win[:halo, :] = jnp.zeros((halo, HEAD_DIM), v_win.dtype)

    barrier = pltpu.get_barrier_semaphore()
    for step in range(1, peers):
        pl.semaphore_signal(
            barrier, inc=1, device_id=(ctx, lax.rem(head + step, peers)), device_id_type=MESH
        )
    for distance in (1, 2):

        @pl.when(ctx >= distance)
        def _():
            pl.semaphore_signal(
                barrier, inc=1, device_id=(ctx - distance, head), device_id_type=MESH
            )

        @pl.when(ctx < shards - distance)
        def _():
            pl.semaphore_signal(
                barrier, inc=1, device_id=(ctx + distance, head), device_id_type=MESH
            )

    around = jnp.minimum(shards - 1 - ctx, REACH) + jnp.minimum(ctx, REACH)
    pl.semaphore_wait(barrier, peers - 1 + around)

    def columns(ref, owner, offset, size):
        stride = ref.shape[1] // peers
        return ref.at[:, pl.ds(pl.multiple_of(owner * stride + offset, size), size)]

    def own_rows(ref, owner, first):
        return ref.at[pl.ds(pl.multiple_of(first + owner * part, part), part), :]

    def own_pair(ref, owner, pair):
        at = pl.ds(pl.multiple_of(owner * part, part), part)
        return ref.at[at, pair * half_width : (pair + 1) * half_width]

    def paired_in(source, target, pair):
        return (
            lambda to: columns(source, to, pair * half_width, half_width),
            lambda of: own_pair(target, of, pair),
        )

    def paired_out(source, target, pair):
        return (
            lambda to: own_pair(source, to, pair),
            lambda of: columns(target, of, pair * half_width, half_width),
        )

    routes = (
        (lambda to: columns(k_in, to, 0, HEAD_DIM), lambda of: own_rows(k_win, of, halo)),
        (lambda to: columns(v_in, to, 0, HEAD_DIM), lambda of: own_rows(v_win, of, halo)),
        (lambda to: d_in.at[to], lambda of: d_buf.at[of]),
        paired_in(q_in, q_buf, 0),
        paired_in(g_in, g_buf, 0),
        paired_in(q_in, q_buf, 1),
        paired_in(g_in, g_buf, 1),
        paired_out(dq_buf, dq_out, 0),
        paired_out(dq_buf, dq_out, 1),
        (lambda to: own_rows(sum_ref.at[0], to, 0), lambda of: columns(dk_out, of, 0, HEAD_DIM)),
        (lambda to: own_rows(sum_ref.at[1], to, 0), lambda of: columns(dv_out, of, 0, HEAD_DIM)),
    )

    def exchange(index, step):
        to = lax.rem(head + step, peers)
        source, target = routes[index]
        return pltpu.make_async_remote_copy(
            src_ref=source(to),
            dst_ref=target(head),
            send_sem=send_sem.at[index, step],
            recv_sem=recv_sem.at[index, step],
            device_id=(ctx, to),
            device_id_type=MESH,
        )

    def keep(index):
        source, target = routes[index]
        return pltpu.make_async_copy(source(head), target(head), local_sem.at[index])

    def begin(*indices):
        for index in indices:
            keep(index).start()
            for step in range(1, peers):
                exchange(index, step).start()

    def arrived(*indices):
        for index in indices:
            keep(index).wait()
            source, target = routes[index]
            for step in range(1, peers):
                of = lax.rem(head + peers - step, peers)
                pltpu.make_async_remote_copy(
                    src_ref=source(head),
                    dst_ref=target(of),
                    send_sem=send_sem.at[index, step],
                    recv_sem=recv_sem.at[index, step],
                    device_id=(ctx, of),
                    device_id_type=MESH,
                ).wait_recv()

    def halo_copy(run, which):
        distance, first, end, _ = plan[run]
        ref = (k_win, v_win)[which]
        base = halo - distance * rows
        return pltpu.make_async_remote_copy(
            src_ref=ref.at[halo + first : halo + end, :],
            dst_ref=ref.at[base + first : base + end, :],
            send_sem=halo_send.at[run, which],
            recv_sem=halo_recv.at[run, which],
            device_id=(ctx + distance, head),
            device_id_type=MESH,
        )

    def back_copy(run, which):
        distance, first, end, _ = plan[run]
        base = halo - distance * rows
        return pltpu.make_async_remote_copy(
            src_ref=low_ref.at[which, base + first : base + end, :],
            dst_ref=got_ref.at[which, base + first : base + end, :],
            send_sem=back_send.at[run, which],
            recv_sem=back_recv.at[run, which],
            device_id=(ctx - distance, head),
            device_id_type=MESH,
        )

    def for_runs(body, upward):
        for run, (distance, first, end, senders) in enumerate(plan):
            if upward:
                here = is_one_of(ctx, senders, shards)
            else:
                here = is_one_of(ctx - distance, senders, shards) & (ctx >= distance)

            @pl.when(here)
            def _():
                body(run, distance, first, end)

    begin(0, 1, 2, 3, 4)

    docs = lengths_ref.shape[1]
    before = lax.broadcasted_iota(jnp.int32, (docs, docs), 1) < lax.broadcasted_iota(
        jnp.int32, (docs, docs), 0
    )
    lengths = lengths_ref[...].astype(jnp.float32)
    doc_starts = jnp.sum(jnp.where(before, lengths, 0.0), axis=1, keepdims=True)
    doc_starts = doc_starts - (ctx * rows - halo).astype(jnp.float32)
    places = lax.broadcasted_iota(jnp.int32, (1, rows), 1).astype(jnp.float32) + float(halo)
    starts = jnp.max(jnp.where(doc_starts <= places, doc_starts, -1e9), axis=0, keepdims=True)
    start_ref[...] = starts.astype(jnp.int32)
    dk_acc[...] = jnp.zeros_like(dk_acc)
    dv_acc[...] = jnp.zeros_like(dv_acc)

    arrived(0, 1)
    for_runs(lambda run, *_: [halo_copy(run, which).start() for which in range(2)], True)
    begin(5, 6)

    reach_tiles = halo // TILE
    key_offset = lax.broadcasted_iota(jnp.int32, (STEP, BLOCK), 0)
    query_offset = lax.broadcasted_iota(jnp.int32, (1, BLOCK), 1)
    parts = BLOCK // part

    def block_steps(block):
        low = first_tiles(ctx, block, shards, rows, reach_tiles)
        tiles = reach_tiles + (block + 1) * (BLOCK // TILE) - low
        return lax.div(tiles + STEP // TILE - 1, STEP // TILE)

    def turn(tile, carry):
        at = pl.ds(pl.multiple_of(tile * TILE, TILE), TILE)
        kt_ref[:, at] = k_win[at, :].T
        return carry

    def attend(pair):
        def query_block(block, carry):
            q_at = pl.ds(pl.multiple_of(block * BLOCK, BLOCK), BLOCK)
            end = halo + (block + 1) * BLOCK
            count = block_steps(block)
            start = start_ref[:, q_at]
            last = query_offset + (end - BLOCK)
            deltas = []
            for one in pair_heads:
                which = pair * len(pair_heads) + one
                cols = slice(which * HEAD_DIM, (which + 1) * HEAD_DIM)
                q_stack[stacks[one], :] = q_buf[q_at, cols]
                g_stack[stacks[one], :] = g_buf[q_at, cols]
                deltas.append(
                    jnp.concatenate(
                        [d_buf[block * parts + p, which : which + 1, :] for p in range(parts)],
                        axis=1,
                    )
                )

            def key_rows(step):
                return pl.multiple_of(end - (step + 1) * STEP, TILE)

            def score_step(step, tops):
                first = key_rows(step)
                at = pl.ds(first, STEP)
                keys = k_win[at, :]
                place = key_offset + first
                allowed = (place >= start) & (place <= last)
                new_tops = []
                for one in pair_heads:
                    scores = contract_last(keys, q_stack[stacks[one], :]) * (ATT_SCALE * LOG2E)
                    scores = jnp.where(allowed, scores, NEG_FILL)
                    score_ref[at, stacks[one]] = scores
                    tall = jnp.max(scores.reshape(STEP // 8, 8, BLOCK), axis=0)
                    new_tops.append(jnp.maximum(tops[one], tall))
                return tuple(new_tops)

            none = jnp.full((8, BLOCK), NEG_FILL, jnp.float32)
            tops = lax.fori_loop(0, count, score_step, tuple(none for _ in pair_heads))
            tops = [jnp.max(top, axis=0, keepdims=True) for top in tops]

            def sum_step(step, totals):
                at = pl.ds(key_rows(step), STEP)
                new_totals = []
                for one in pair_heads:
                    powers = jnp.exp2(score_ref[at, stacks[one]] - tops[one])
                    tall = jnp.sum(powers.reshape(STEP // 8, 8, BLOCK), axis=0)
                    new_totals.append(totals[one] + tall)
                return tuple(new_totals)

            zero = jnp.zeros((8, BLOCK), jnp.float32)
            totals = lax.fori_loop(0, count, sum_step, tuple(zero for _ in pair_heads))
            log_totals = [
                tops[one] + jnp.log2(jnp.sum(totals[one], axis=0, keepdims=True))
                for one in pair_heads
            ]
            turned_ref[...] = jnp.zeros_like(turned_ref)

            def grad_step(step, carry):
                at = pl.ds(key_rows(step), STEP)
                vals = v_win[at, :]
                for one in pair_heads:
                    probs = jnp.exp2(score_ref[at, stacks[one]] - log_totals[one])
                    grad_probs = contract_last(vals, g_stack[stacks[one], :])
                    grads = (probs * (grad_probs - deltas[one])).astype(jnp.bfloat16)
                    probs_ref[:, stacks[one]] = probs.astype(jnp.bfloat16)
                    grads_ref[:, stacks[one]] = grads
                dv_acc[at, :] += contract_inner(probs_ref[...], g_stack[...])
                dk_acc[at, :] += contract_inner(grads_ref[...], q_stack[...])
                turned_ref[...] += contract_inner(kt_ref[:, at], grads_ref[...])
                return carry

            lax.fori_loop(0, count, grad_step, 0)
            for one in pair_heads:
                which = pair * len(pair_heads) + one
                dq = turned_ref[:, stacks[one]].T * ATT_SCALE
                dq_buf[q_at, which * HEAD_DIM : (which + 1) * HEAD_DIM] = dq.astype(jnp.bfloat16)
            return carry

        lax.fori_loop(0, rows // BLOCK, query_block, 0)

    arrived(2, 3, 4)
    for_runs(lambda run, *_: [halo_copy(run, which).wait_recv() for which in range(2)], False)
    lowest = reach_tiles + BLOCK // TILE - block_steps(0) * (STEP // TILE)
    lax.fori_loop(lowest, reach_tiles + rows // TILE, turn, 0)
    attend(0)
    begin(7)
    arrived(5, 6)
    attend(1)

    def send_back(run, distance, first, end):
        at = slice(halo - distance * rows + first, halo - distance * rows + end)
        low_ref[0, at, :] = (dk_acc[at, :] * ATT_SCALE).astype(jnp.bfloat16)
        low_ref[1, at, :] = dv_acc[at, :].astype(jnp.bfloat16)
        for which in range(2):
            back_copy(run, which).start()

    def take_back(run, distance, first, end):
        got = slice(halo - distance * rows + first, halo - distance * rows + end)
        for which in range(2):
            back_copy(run, which).wait_recv()
            total_ref[which, first:end, :] += got_ref[which, got, :].astype(jnp.float32)

    for_runs(send_back, False)
    begin(8)
    total_ref[0] = dk_acc[halo:, :] * ATT_SCALE
    total_ref[1] = dv_acc[halo:, :]
    for_runs(take_back, True)
    sum_ref[...] = total_ref[...].astype(jnp.bfloat16)
    begin(9, 10)
    for_runs(lambda run, *_: [halo_copy(run, which).wait_send() for which in range(2)], True)
    for_runs(lambda run, *_: [back_copy(run, which).wait_send() for which in range(2)], False)
    arrived(7, 8, 9, 10)
    for index in range(len(routes)):
        for step in range(1, peers):
            exchange(index, step).wait_send()


def whole(shards, plan, queries, keys, values, grad_out, delta, doc_lengths):
    peers = delta.shape[0]
    part = queries.shape[0]
    rows = part * peers
    width = queries.shape[1] // peers
    window = (REACH + 1) * rows + TILE
    low, full = jnp.bfloat16, jnp.float32
    wide = width // 2 // HEAD_DIM * BLOCK
    dma = pltpu.SemaphoreType.DMA
    return pl.pallas_call(
        functools.partial(whole_kernel, shards, plan),
        out_shape=(
            jax.ShapeDtypeStruct(queries.shape, low),
            jax.ShapeDtypeStruct(keys.shape, low),
            jax.ShapeDtypeStruct(values.shape, low),
        ),
        in_specs=[ANYWHERE] * 4 + [VMEM] * 2,
        out_specs=(ANYWHERE,) * 3,
        scratch_shapes=[
            pltpu.VMEM((rows, width), low),
            pltpu.VMEM((rows, width), low),
            pltpu.VMEM((window, HEAD_DIM), low),
            pltpu.VMEM((window, HEAD_DIM), low),
            pltpu.VMEM(delta.shape, full),
            pltpu.VMEM((1, rows), jnp.int32),
            pltpu.VMEM((HEAD_DIM, window), low),
            pltpu.VMEM((window, wide), full),
            pltpu.VMEM((STEP, wide), low),
            pltpu.VMEM((STEP, wide), low),
            pltpu.VMEM((wide, HEAD_DIM), low),
            pltpu.VMEM((wide, HEAD_DIM), low),
            pltpu.VMEM((HEAD_DIM, wide), full),
            pltpu.VMEM((window, HEAD_DIM), full),
            pltpu.VMEM((window, HEAD_DIM), full),
            pltpu.VMEM((rows, width), low),
            pltpu.VMEM((2, window - rows, HEAD_DIM), low),
            pltpu.VMEM((2, window - rows, HEAD_DIM), low),
            pltpu.VMEM((2, rows, HEAD_DIM), full),
            pltpu.VMEM((2, rows, HEAD_DIM), low),
            dma((11, peers)),
            dma((11, peers)),
            dma((11,)),
            dma((len(plan), 2)),
            dma((len(plan), 2)),
            dma((len(plan), 2)),
            dma((len(plan), 2)),
        ],
        compiler_params=pltpu.CompilerParams(
            collective_id=0, has_side_effects=True, vmem_limit_bytes=48 * 1024 * 1024
        ),
        name="whole",
    )(queries, keys, values, grad_out, delta, doc_lengths[None])


def settle_kernel(*refs):
    count = len(refs) // 2
    sems = refs[-1]
    copies = [
        pltpu.make_async_copy(refs[one], refs[count + one], sems.at[one]) for one in range(count)
    ]
    for copy in copies:
        copy.start()
    for copy in copies:
        copy.wait()


def settled(*arrays):
    return pl.pallas_call(
        settle_kernel,
        out_shape=tuple(jax.ShapeDtypeStruct(a.shape, a.dtype) for a in arrays),
        in_specs=[ANYWHERE] * len(arrays),
        out_specs=(ANYWHERE,) * len(arrays),
        scratch_shapes=[pltpu.SemaphoreType.DMA((len(arrays),))],
        name="settle",
    )(*arrays)


def on_device(queries, keys, values, grad_out, delta, doc_lengths):
    shards, peers = lax.axis_size("ctx"), lax.axis_size("head")
    rows = queries.shape[0] * peers
    delta = delta.reshape(peers, delta.shape[0] // peers, delta.shape[1])
    slots = jnp.arange(doc_lengths.shape[0], dtype=jnp.int32)
    doc_starts = jnp.sum(jnp.where(slots[:, None] < slots[None, :], doc_lengths[:, None], 0), axis=0)

    def start_at(places):
        return jnp.max(
            jnp.where(doc_starts[:, None] <= places[None, :], doc_starts[:, None], 0), axis=0
        )

    last_block = lax.div(doc_starts + doc_lengths - 1, jnp.int32(BLOCK))
    fits = jnp.all(doc_starts >= short_reach(last_block, shards, rows))

    def in_one(*operands):
        return whole(shards, halo_plan(shards, rows, True), *operands, doc_lengths)

    def in_three(*operands):
        plan = halo_plan(shards, rows, False)
        base = lax.axis_index("ctx") * rows
        starts = start_at(base + jnp.arange(rows, dtype=jnp.int32)) - (base - REACH * rows - TILE)
        q, k, v, g, d = gather(shards, plan, *operands)
        dq, dk, dv = attention(starts[::TILE], q, g, k, v, d, starts[None])
        return scatter(shards, plan, peers, dq, dk, dv)

    return settled(*lax.cond(fits, in_one, in_three, queries, keys, values, grad_out, delta))


def solution(mesh):
    rows = P(("ctx", "head"), None)
    return jax.shard_map(
        on_device,
        mesh=mesh,
        in_specs=(rows, rows, rows, rows, P(None, ("ctx", "head")), P()),
        out_specs=(rows, rows, rows),
        check_vma=False,
    )
```

```python
import functools

import jax
import jax.numpy as jnp
from jax import lax
from jax.experimental import pallas as pl
from jax.experimental.pallas import tpu as pltpu
from jax.sharding import PartitionSpec as P

HEAD_DIM = 128
TILE = 256
STEP = 512
BLOCK = 512
HOPS = ((2, 1), (2, 0), (1, 1), (3, 1), (0, 1), (1, 0), (3, 0))
REACH = 2
NEG_FILL = -1e30
ATT_SCALE = HEAD_DIM ** (-0.5)
LOG2E = 1.4426950408889634
MESH = pl.DeviceIdType.MESH
VMEM = pl.BlockSpec(memory_space=pltpu.VMEM)
ANYWHERE = pl.BlockSpec(memory_space=pl.ANY)


def long_firsts(shards):
    middle = shards // 2
    return (0, middle - 3, middle - 1, middle + 1, shards - 3)


def halo_plan(shards, rows, short):
    near = tuple(range(shards - 1))
    far = tuple(range(shards - 2))
    if not short:
        return ((1, 0, rows, near), (2, 0, rows, far))
    firsts = long_firsts(shards)
    seconds = tuple(first + 1 for first in firsts)
    half = rows // 2
    return (
        (1, rows - TILE, rows, near),
        (1, half, rows - TILE, tuple(sorted(set(firsts + seconds)))),
        (1, 0, half, seconds),
        (2, half, rows, firsts),
    )


def short_reach(blocks, shards, rows):
    shard = blocks // (rows // BLOCK)
    reach = jnp.where(shard == 0, 0, blocks * BLOCK - TILE)
    for first in long_firsts(shards):
        opening = first * rows + rows // 2
        holds = (shard == first + 1) | (shard == first + 2)
        reach = jnp.where(holds, jnp.minimum(reach, opening), reach)
    return reach


def is_one_of(index, members, shards):
    if members == tuple(range(len(members))):
        return index < len(members)
    return functools.reduce(jnp.logical_or, [index == member for member in members])


def contract_last(left, right):
    return lax.dot_general(
        left, right, (((1,), (1,)), ((), ())), preferred_element_type=jnp.float32
    )


def contract_inner(left, right):
    return jnp.dot(left, right, preferred_element_type=jnp.float32)


def meet(shards, peers, upward):
    ctx, head = lax.axis_index("ctx"), lax.axis_index("head")
    barrier = pltpu.get_barrier_semaphore()
    for step in range(1, peers):
        pl.semaphore_signal(
            barrier, inc=1, device_id=(ctx, lax.rem(head + step, peers)), device_id_type=MESH
        )
    for distance in (1, 2):
        other = ctx - distance if upward else ctx + distance
        there = ctx >= distance if upward else ctx < shards - distance

        @pl.when(there)
        def _():
            pl.semaphore_signal(barrier, inc=1, device_id=(other, head), device_id_type=MESH)

    beyond = shards - 1 - ctx if upward else ctx
    pl.semaphore_wait(barrier, peers - 1 + jnp.minimum(beyond, REACH))


def gather_kernel(
    shards,
    plan,
    q_in,
    k_in,
    v_in,
    g_in,
    d_in,
    q_out,
    k_out,
    v_out,
    g_out,
    d_out,
    send_sem,
    recv_sem,
    local_sem,
    halo_send,
    halo_recv,
):
    ctx, head = lax.axis_index("ctx"), lax.axis_index("head")
    part = q_in.shape[0]
    rows = q_out.shape[0]
    peers = rows // part
    halo = k_out.shape[0] - rows
    k_out[:halo, :] = jnp.zeros((halo, HEAD_DIM), k_out.dtype)
    v_out[:halo, :] = jnp.zeros((halo, HEAD_DIM), v_out.dtype)
    meet(shards, peers, True)

    def columns(ref, owner):
        width = ref.shape[1] // peers
        return ref.at[:, pl.ds(pl.multiple_of(owner * width, width), width)]

    def own_rows(ref, owner, first):
        return ref.at[pl.ds(pl.multiple_of(first + owner * part, part), part), :]

    pairs = (
        (lambda to: columns(k_in, to), lambda of: own_rows(k_out, of, halo)),
        (lambda to: columns(v_in, to), lambda of: own_rows(v_out, of, halo)),
        (lambda to: d_in.at[to], lambda of: d_out.at[of]),
        (lambda to: columns(q_in, to), lambda of: own_rows(q_out, of, 0)),
        (lambda to: columns(g_in, to), lambda of: own_rows(g_out, of, 0)),
    )

    def exchange(index, step):
        to = lax.rem(head + step, peers)
        source, target = pairs[index]
        return pltpu.make_async_remote_copy(
            src_ref=source(to),
            dst_ref=target(head),
            send_sem=send_sem.at[index, step],
            recv_sem=recv_sem.at[index, step],
            device_id=(ctx, to),
            device_id_type=MESH,
        )

    def keep(index):
        source, target = pairs[index]
        return pltpu.make_async_copy(source(head), target(head), local_sem.at[index])

    def arrived(index, step):
        source, target = pairs[index]
        of = lax.rem(head + peers - step, peers)
        pltpu.make_async_remote_copy(
            src_ref=source(head),
            dst_ref=target(of),
            send_sem=send_sem.at[index, step],
            recv_sem=recv_sem.at[index, step],
            device_id=(ctx, of),
            device_id_type=MESH,
        ).wait_recv()

    for index in range(5):
        keep(index).start()
        for step in range(1, peers):
            exchange(index, step).start()
    for index in range(2):
        keep(index).wait()
        for step in range(1, peers):
            arrived(index, step)

    def halo_copy(run, which):
        distance, first, end, _ = plan[run]
        ref = (k_out, v_out)[which]
        return pltpu.make_async_remote_copy(
            src_ref=ref.at[halo + first : halo + end, :],
            dst_ref=ref.at[halo - distance * rows + first : halo - distance * rows + end, :],
            send_sem=halo_send.at[run, which],
            recv_sem=halo_recv.at[run, which],
            device_id=(ctx + distance, head),
            device_id_type=MESH,
        )

    for run, (distance, first, end, senders) in enumerate(plan):

        @pl.when(is_one_of(ctx, senders, shards))
        def _():
            for which in range(2):
                halo_copy(run, which).start()

    for index in range(2, 5):
        keep(index).wait()
        for step in range(1, peers):
            arrived(index, step)
    for run, (distance, first, end, senders) in enumerate(plan):

        @pl.when(is_one_of(ctx, senders, shards))
        def _():
            for which in range(2):
                halo_copy(run, which).wait_send()

        @pl.when(is_one_of(ctx - distance, senders, shards) & (ctx >= distance))
        def _():
            for which in range(2):
                halo_copy(run, which).wait_recv()

    for index in range(5):
        for step in range(1, peers):
            exchange(index, step).wait_send()


def gather(shards, plan, queries, keys, values, grad_out, delta):
    peers = delta.shape[0]
    rows = queries.shape[0] * peers
    window = (REACH + 1) * rows + TILE
    width = queries.shape[1] // peers
    low = jnp.bfloat16
    return pl.pallas_call(
        functools.partial(gather_kernel, shards, plan),
        out_shape=(
            jax.ShapeDtypeStruct((rows, width), low),
            jax.ShapeDtypeStruct((window, HEAD_DIM), low),
            jax.ShapeDtypeStruct((window, HEAD_DIM), low),
            jax.ShapeDtypeStruct((rows, width), low),
            jax.ShapeDtypeStruct(delta.shape, jnp.float32),
        ),
        in_specs=[ANYWHERE] * 4 + [VMEM],
        out_specs=(VMEM,) * 5,
        scratch_shapes=[
            pltpu.SemaphoreType.DMA((5, peers)),
            pltpu.SemaphoreType.DMA((5, peers)),
            pltpu.SemaphoreType.DMA((5,)),
            pltpu.SemaphoreType.DMA((len(plan), 2)),
            pltpu.SemaphoreType.DMA((len(plan), 2)),
        ],
        compiler_params=pltpu.CompilerParams(
            collective_id=1,
            has_side_effects=True,
            vmem_limit_bytes=32 * 1024 * 1024,
        ),
        name="gather",
    )(queries, keys, values, grad_out, delta)


def attention_kernel(
    first_row,
    q_ref,
    g_ref,
    k_ref,
    v_ref,
    delta_ref,
    start_ref,
    dq_ref,
    dk_ref,
    dv_ref,
    kt_ref,
    score_ref,
    turned_ref,
):
    rows = q_ref.shape[0]
    heads = range(q_ref.shape[1] // HEAD_DIM)
    halo = k_ref.shape[0] - rows
    parts = TILE // delta_ref.shape[2]
    columns = [slice(head * HEAD_DIM, (head + 1) * HEAD_DIM) for head in heads]
    dk_ref[...] = jnp.zeros_like(dk_ref)
    dv_ref[...] = jnp.zeros_like(dv_ref)
    key_offset = lax.broadcasted_iota(jnp.int32, (STEP, TILE), 0)
    query_offset = lax.broadcasted_iota(jnp.int32, (1, TILE), 1)

    def turn(tile, carry):
        at = pl.ds(pl.multiple_of(tile * TILE, TILE), TILE)
        kt_ref[:, at] = k_ref[at, :].T
        return carry

    lax.fori_loop(jnp.maximum(first_row[0] // TILE - 1, 0), k_ref.shape[0] // TILE, turn, 0)

    def query_block(block, carry):
        q_at = pl.ds(pl.multiple_of(block * TILE, TILE), TILE)
        end = halo + (block + 1) * TILE
        count = (end - first_row[block] + STEP - 1) // STEP
        start = start_ref[:, q_at]
        last = query_offset + (end - TILE)
        deltas = [
            jnp.concatenate(
                [delta_ref[block * parts + part, head : head + 1, :] for part in range(parts)],
                axis=1,
            )
            for head in heads
        ]

        def key_rows(step):
            return pl.multiple_of(end - (step + 1) * STEP, TILE)

        def score_step(step, tops):
            first = key_rows(step)
            at = pl.ds(first, STEP)
            keys = k_ref[at, :]
            place = key_offset + first
            allowed = (place >= start) & (place <= last)
            new_tops = []
            for head in heads:
                scores = contract_last(keys, q_ref[q_at, columns[head]]) * (ATT_SCALE * LOG2E)
                scores = jnp.where(allowed, scores, NEG_FILL)
                score_ref[head, at, :] = scores
                tall = jnp.max(scores.reshape(STEP // 8, 8, TILE), axis=0)
                new_tops.append(jnp.maximum(tops[head], tall))
            return tuple(new_tops)

        none = jnp.full((8, TILE), NEG_FILL, jnp.float32)
        tops = lax.fori_loop(0, count, score_step, tuple(none for _ in heads))
        tops = [jnp.max(top, axis=0, keepdims=True) for top in tops]

        def sum_step(step, totals):
            at = pl.ds(key_rows(step), STEP)
            new_totals = []
            for head in heads:
                powers = jnp.exp2(score_ref[head, at, :] - tops[head])
                new_totals.append(
                    totals[head] + jnp.sum(powers.reshape(STEP // 8, 8, TILE), axis=0)
                )
            return tuple(new_totals)

        zero = jnp.zeros((8, TILE), jnp.float32)
        totals = lax.fori_loop(0, count, sum_step, tuple(zero for _ in heads))
        log_totals = [
            tops[head] + jnp.log2(jnp.sum(totals[head], axis=0, keepdims=True)) for head in heads
        ]
        turned_ref[...] = jnp.zeros_like(turned_ref)

        def grad_step(step, carry):
            at = pl.ds(key_rows(step), STEP)
            vals = v_ref[at, :]
            keys_turned = kt_ref[:, at]
            val_parts, key_parts = [], []
            for head in heads:
                q = q_ref[q_at, columns[head]]
                g = g_ref[q_at, columns[head]]
                probs = jnp.exp2(score_ref[head, at, :] - log_totals[head])
                grad_probs = contract_last(vals, g)
                grad_scores = (probs * (grad_probs - deltas[head])).astype(jnp.bfloat16)
                val_parts.append(contract_inner(probs.astype(jnp.bfloat16), g))
                key_parts.append(contract_inner(grad_scores, q))
                turned_ref[head] += contract_inner(keys_turned, grad_scores)
            dv_ref[at, :] += sum(val_parts[1:], val_parts[0])
            dk_ref[at, :] += sum(key_parts[1:], key_parts[0])
            return carry

        lax.fori_loop(0, count, grad_step, 0)
        for head in heads:
            dq_ref[q_at, columns[head]] = (turned_ref[head].T * ATT_SCALE).astype(jnp.bfloat16)
        return carry

    lax.fori_loop(0, rows // TILE, query_block, 0)


def attention(first_row, q, g, keys, vals, delta, starts):
    window = keys.shape[0]
    heads = q.shape[1] // HEAD_DIM
    return pl.pallas_call(
        attention_kernel,
        out_shape=(
            jax.ShapeDtypeStruct(q.shape, jnp.bfloat16),
            jax.ShapeDtypeStruct(keys.shape, jnp.float32),
            jax.ShapeDtypeStruct(keys.shape, jnp.float32),
        ),
        in_specs=[pl.BlockSpec(memory_space=pltpu.SMEM)] + [VMEM] * 6,
        out_specs=(VMEM,) * 3,
        scratch_shapes=[
            pltpu.VMEM((HEAD_DIM, window), jnp.bfloat16),
            pltpu.VMEM((heads, window, TILE), jnp.float32),
            pltpu.VMEM((heads, HEAD_DIM, TILE), jnp.float32),
        ],
        compiler_params=pltpu.CompilerParams(vmem_limit_bytes=44 * 1024 * 1024),
        name="attention",
    )(first_row, q, g, keys, vals, delta, starts)


def scatter_kernel(
    shards,
    plan,
    dq_in,
    dk_in,
    dv_in,
    dq_out,
    dk_out,
    dv_out,
    low_ref,
    got_ref,
    total_ref,
    sum_ref,
    send_sem,
    recv_sem,
    local_sem,
    halo_send,
    halo_recv,
):
    ctx, head = lax.axis_index("ctx"), lax.axis_index("head")
    part = dq_out.shape[0]
    rows = dq_in.shape[0]
    peers = rows // part
    halo = dk_in.shape[0] - rows
    meet(shards, peers, False)

    def columns(ref, owner):
        width = ref.shape[1] // peers
        return ref.at[:, pl.ds(pl.multiple_of(owner * width, width), width)]

    def row_part(ref, owner):
        return ref.at[pl.ds(pl.multiple_of(owner * part, part), part), :]

    pairs = (
        (lambda to: row_part(dq_in, to), lambda of: columns(dq_out, of)),
        (lambda to: row_part(sum_ref.at[0], to), lambda of: columns(dk_out, of)),
        (lambda to: row_part(sum_ref.at[1], to), lambda of: columns(dv_out, of)),
    )

    def exchange(index, step):
        to = lax.rem(head + step, peers)
        source, target = pairs[index]
        return pltpu.make_async_remote_copy(
            src_ref=source(to),
            dst_ref=target(head),
            send_sem=send_sem.at[index, step],
            recv_sem=recv_sem.at[index, step],
            device_id=(ctx, to),
            device_id_type=MESH,
        )

    def keep(index):
        source, target = pairs[index]
        return pltpu.make_async_copy(source(head), target(head), local_sem.at[index])

    def arrived(index, step):
        source, target = pairs[index]
        of = lax.rem(head + peers - step, peers)
        pltpu.make_async_remote_copy(
            src_ref=source(head),
            dst_ref=target(of),
            send_sem=send_sem.at[index, step],
            recv_sem=recv_sem.at[index, step],
            device_id=(ctx, of),
            device_id_type=MESH,
        ).wait_recv()

    def halo_copy(run, which):
        distance, first, end, _ = plan[run]
        base = halo - distance * rows
        return pltpu.make_async_remote_copy(
            src_ref=low_ref.at[which, base + first : base + end, :],
            dst_ref=got_ref.at[which, base + first : base + end, :],
            send_sem=halo_send.at[run, which],
            recv_sem=halo_recv.at[run, which],
            device_id=(ctx - distance, head),
            device_id_type=MESH,
        )

    for run, (distance, first, end, senders) in enumerate(plan):

        @pl.when(is_one_of(ctx - distance, senders, shards) & (ctx >= distance))
        def _():
            at = slice(halo - distance * rows + first, halo - distance * rows + end)
            low_ref[0, at, :] = (dk_in[at, :] * ATT_SCALE).astype(jnp.bfloat16)
            low_ref[1, at, :] = dv_in[at, :].astype(jnp.bfloat16)
            for which in range(2):
                halo_copy(run, which).start()

    keep(0).start()
    for step in range(1, peers):
        exchange(0, step).start()
    total_ref[0] = dk_in[halo:, :] * ATT_SCALE
    total_ref[1] = dv_in[halo:, :]

    for run, (distance, first, end, senders) in enumerate(plan):

        @pl.when(is_one_of(ctx, senders, shards))
        def _():
            got = slice(halo - distance * rows + first, halo - distance * rows + end)
            own = slice(first, end)
            for which in range(2):
                halo_copy(run, which).wait_recv()
                total_ref[which, own, :] += got_ref[which, got, :].astype(jnp.float32)

    sum_ref[...] = total_ref[...].astype(jnp.bfloat16)
    for index in (1, 2):
        keep(index).start()
        for step in range(1, peers):
            exchange(index, step).start()
    for run, (distance, first, end, senders) in enumerate(plan):

        @pl.when(is_one_of(ctx - distance, senders, shards) & (ctx >= distance))
        def _():
            for which in range(2):
                halo_copy(run, which).wait_send()

    for index in range(3):
        keep(index).wait()
        for step in range(1, peers):
            arrived(index, step)
            exchange(index, step).wait_send()


def scatter(shards, plan, peers, dq, dk, dv):
    rows, width = dq.shape
    window = dk.shape[0]
    low = jnp.bfloat16
    return pl.pallas_call(
        functools.partial(scatter_kernel, shards, plan),
        out_shape=(
            jax.ShapeDtypeStruct((rows // peers, width * peers), low),
            jax.ShapeDtypeStruct((rows // peers, HEAD_DIM * peers), low),
            jax.ShapeDtypeStruct((rows // peers, HEAD_DIM * peers), low),
        ),
        in_specs=[VMEM] * 3,
        out_specs=(ANYWHERE,) * 3,
        scratch_shapes=[
            pltpu.VMEM((2, window - rows, HEAD_DIM), low),
            pltpu.VMEM((2, window - rows, HEAD_DIM), low),
            pltpu.VMEM((2, rows, HEAD_DIM), jnp.float32),
            pltpu.VMEM((2, rows, HEAD_DIM), low),
            pltpu.SemaphoreType.DMA((3, peers)),
            pltpu.SemaphoreType.DMA((3, peers)),
            pltpu.SemaphoreType.DMA((3,)),
            pltpu.SemaphoreType.DMA((len(plan), 2)),
            pltpu.SemaphoreType.DMA((len(plan), 2)),
        ],
        compiler_params=pltpu.CompilerParams(
            collective_id=2,
            has_side_effects=True,
            vmem_limit_bytes=32 * 1024 * 1024,
        ),
        name="scatter",
    )(dq, dk, dv)


def first_tiles(ctx, block, shards, rows, reach_tiles):
    own = rows // TILE
    half = own // 2
    firsts = long_firsts(shards)
    second = is_one_of(ctx, tuple(first + 1 for first in firsts), shards)
    third = is_one_of(ctx, tuple(first + 2 for first in firsts), shards)
    low = reach_tiles + block * (BLOCK // TILE) - 1
    low = jnp.where(ctx == 0, reach_tiles, low)
    low = jnp.where(second, reach_tiles - half, low)
    return jnp.where(third, reach_tiles - own - half, low)


def whole_kernel(
    shards,
    plan,
    q_in,
    k_in,
    v_in,
    g_in,
    d_in,
    lengths_ref,
    dq_out,
    dk_out,
    dv_out,
    q_buf,
    g_buf,
    k_win,
    v_win,
    d_buf,
    start_ref,
    kt_ref,
    score_ref,
    probs_ref,
    grads_ref,
    q_stack,
    g_stack,
    delta_ref,
    log_ref,
    turned_ref,
    dk_acc,
    dv_acc,
    dq_buf,
    low_ref,
    got_ref,
    total_ref,
    sum_ref,
    send_sem,
    recv_sem,
    local_sem,
    halo_send,
    halo_recv,
    back_send,
    back_recv,
):
    ctx, head = lax.axis_index("ctx"), lax.axis_index("head")
    part = q_in.shape[0]
    rows, width = q_buf.shape
    peers = rows // part
    halo = k_win.shape[0] - rows
    half_width = width // 2
    pair_heads = range(half_width // HEAD_DIM)
    stacks = [slice(one * BLOCK, (one + 1) * BLOCK) for one in pair_heads]
    k_win[:halo, :] = jnp.zeros((halo, HEAD_DIM), k_win.dtype)
    v_win[:halo, :] = jnp.zeros((halo, HEAD_DIM), v_win.dtype)

    barrier = pltpu.get_barrier_semaphore()
    for step in range(1, peers):
        pl.semaphore_signal(
            barrier, inc=1, device_id=(ctx, lax.rem(head + step, peers)), device_id_type=MESH
        )
    for distance in (1, 2):

        @pl.when(ctx >= distance)
        def _():
            pl.semaphore_signal(
                barrier, inc=1, device_id=(ctx - distance, head), device_id_type=MESH
            )

        @pl.when(ctx < shards - distance)
        def _():
            pl.semaphore_signal(
                barrier, inc=1, device_id=(ctx + distance, head), device_id_type=MESH
            )

    around = jnp.minimum(shards - 1 - ctx, REACH) + jnp.minimum(ctx, REACH)
    pl.semaphore_wait(barrier, peers - 1 + around)

    def partner(step, sign):
        along, across = HOPS[step - 1]
        line = peers // 2
        moved = lax.rem(lax.div(head, 2) + (along if sign > 0 else line - along), line)
        return moved * 2 + lax.rem(head + across, 2)

    def columns(ref, owner, offset, size):
        stride = ref.shape[1] // peers
        return ref.at[:, pl.ds(pl.multiple_of(owner * stride + offset, size), size)]

    def own_rows(ref, owner, first):
        return ref.at[pl.ds(pl.multiple_of(first + owner * part, part), part), :]

    def own_pair(ref, owner, pair):
        at = pl.ds(pl.multiple_of(owner * part, part), part)
        return ref.at[at, pair * half_width : (pair + 1) * half_width]

    def paired_in(source, target, pair):
        return (
            lambda to: columns(source, to, pair * half_width, half_width),
            lambda of: own_pair(target, of, pair),
        )

    def paired_out(source, target, pair):
        return (
            lambda to: own_pair(source, to, pair),
            lambda of: columns(target, of, pair * half_width, half_width),
        )

    routes = (
        (lambda to: columns(k_in, to, 0, HEAD_DIM), lambda of: own_rows(k_win, of, halo)),
        (lambda to: columns(v_in, to, 0, HEAD_DIM), lambda of: own_rows(v_win, of, halo)),
        (lambda to: d_in.at[to], lambda of: d_buf.at[of]),
        paired_in(q_in, q_buf, 0),
        paired_in(g_in, g_buf, 0),
        paired_in(q_in, q_buf, 1),
        paired_in(g_in, g_buf, 1),
        paired_out(dq_buf, dq_out, 0),
        paired_out(dq_buf, dq_out, 1),
        (lambda to: own_rows(sum_ref.at[0], to, 0), lambda of: columns(dk_out, of, 0, HEAD_DIM)),
        (lambda to: own_rows(sum_ref.at[1], to, 0), lambda of: columns(dv_out, of, 0, HEAD_DIM)),
    )

    def exchange(index, step):
        to = partner(step, 1)
        source, target = routes[index]
        return pltpu.make_async_remote_copy(
            src_ref=source(to),
            dst_ref=target(head),
            send_sem=send_sem.at[index, step],
            recv_sem=recv_sem.at[index, step],
            device_id=(ctx, to),
            device_id_type=MESH,
        )

    def keep(index):
        source, target = routes[index]
        return pltpu.make_async_copy(source(head), target(head), local_sem.at[index])

    def begin(*indices):
        for index in indices:
            keep(index).start()
            for step in range(1, peers):
                exchange(index, step).start()

    def begin_block(index, block):
        per_block = BLOCK // part

        @pl.when(lax.div(head, per_block) == block)
        def _():
            keep(index).start()

        for step in range(1, peers):

            @pl.when(lax.div(partner(step, 1), per_block) == block)
            def _():
                exchange(index, step).start()

    def arrived(*indices):
        for index in indices:
            keep(index).wait()
            source, target = routes[index]
            for step in range(1, peers):
                of = partner(step, -1)
                pltpu.make_async_remote_copy(
                    src_ref=source(head),
                    dst_ref=target(of),
                    send_sem=send_sem.at[index, step],
                    recv_sem=recv_sem.at[index, step],
                    device_id=(ctx, of),
                    device_id_type=MESH,
                ).wait_recv()

    def halo_copy(run, which):
        distance, first, end, _ = plan[run]
        ref = (k_win, v_win)[which]
        base = halo - distance * rows
        return pltpu.make_async_remote_copy(
            src_ref=ref.at[halo + first : halo + end, :],
            dst_ref=ref.at[base + first : base + end, :],
            send_sem=halo_send.at[run, which],
            recv_sem=halo_recv.at[run, which],
            device_id=(ctx + distance, head),
            device_id_type=MESH,
        )

    def back_copy(run, which):
        distance, first, end, _ = plan[run]
        base = halo - distance * rows
        return pltpu.make_async_remote_copy(
            src_ref=low_ref.at[which, base + first : base + end, :],
            dst_ref=got_ref.at[which, base + first : base + end, :],
            send_sem=back_send.at[run, which],
            recv_sem=back_recv.at[run, which],
            device_id=(ctx - distance, head),
            device_id_type=MESH,
        )

    def for_runs(body, upward):
        for run, (distance, first, end, senders) in enumerate(plan):
            if upward:
                here = is_one_of(ctx, senders, shards)
            else:
                here = is_one_of(ctx - distance, senders, shards) & (ctx >= distance)

            @pl.when(here)
            def _():
                body(run, distance, first, end)

    begin(0, 1, 3, 2, 4)

    docs = lengths_ref.shape[1]
    before = lax.broadcasted_iota(jnp.int32, (docs, docs), 1) < lax.broadcasted_iota(
        jnp.int32, (docs, docs), 0
    )
    lengths = lengths_ref[...].astype(jnp.float32)
    doc_starts = jnp.sum(jnp.where(before, lengths, 0.0), axis=1, keepdims=True)
    doc_starts = doc_starts - (ctx * rows - halo).astype(jnp.float32)
    places = lax.broadcasted_iota(jnp.int32, (1, rows), 1).astype(jnp.float32) + float(halo)
    starts = jnp.max(jnp.where(doc_starts <= places, doc_starts, -1e9), axis=0, keepdims=True)
    start_ref[...] = starts.astype(jnp.int32)
    dk_acc[...] = jnp.zeros_like(dk_acc)
    dv_acc[...] = jnp.zeros_like(dv_acc)

    for which in range(2):
        arrived(which)
        for_runs(lambda run, *_: halo_copy(run, which).start(), True)
    begin(5, 6)

    reach_tiles = halo // TILE
    key_offset = lax.broadcasted_iota(jnp.int32, (STEP, BLOCK), 0)
    query_offset = lax.broadcasted_iota(jnp.int32, (1, BLOCK), 1)
    parts = BLOCK // part

    def block_steps(block):
        low = first_tiles(ctx, block, shards, rows, reach_tiles)
        tiles = reach_tiles + (block + 1) * (BLOCK // TILE) - low
        return lax.div(tiles + STEP // TILE - 1, STEP // TILE)

    def turn(tile, carry):
        at = pl.ds(pl.multiple_of(tile * TILE, TILE), TILE)
        kt_ref[:, at] = k_win[at, :].T
        return carry

    def key_rows(block, step):
        return pl.multiple_of(halo + (block + 1) * BLOCK - (step + 1) * STEP, TILE)

    def query_rows(block):
        return pl.ds(pl.multiple_of(block * BLOCK, BLOCK), BLOCK)

    def attend_sums(pair):
        def query_block(block, carry):
            q_at = query_rows(block)
            count = block_steps(block)
            start = start_ref[:, q_at]
            last = query_offset + (halo + block * BLOCK)
            for one in pair_heads:
                which = pair * len(pair_heads) + one
                cols = slice(which * HEAD_DIM, (which + 1) * HEAD_DIM)
                q_stack[block, stacks[one], :] = q_buf[q_at, cols]

            def score_step(step, tops):
                first = key_rows(block, step)
                at = pl.ds(first, STEP)
                keys = k_win[at, :]
                place = key_offset + first
                allowed = (place >= start) & (place <= last)
                new_tops = []
                for one in pair_heads:
                    scores = contract_last(keys, q_stack[block, stacks[one], :])
                    scores = jnp.where(allowed, scores * (ATT_SCALE * LOG2E), NEG_FILL)
                    score_ref[block, at, stacks[one]] = scores
                    tall = jnp.max(scores.reshape(STEP // 8, 8, BLOCK), axis=0)
                    new_tops.append(jnp.maximum(tops[one], tall))
                return tuple(new_tops)

            none = jnp.full((8, BLOCK), NEG_FILL, jnp.float32)
            tops = lax.fori_loop(0, count, score_step, tuple(none for _ in pair_heads))
            tops = [jnp.max(top, axis=0, keepdims=True) for top in tops]

            def sum_step(step, totals):
                at = pl.ds(key_rows(block, step), STEP)
                new_totals = []
                for one in pair_heads:
                    powers = jnp.exp2(score_ref[block, at, stacks[one]] - tops[one])
                    tall = jnp.sum(powers.reshape(STEP // 8, 8, BLOCK), axis=0)
                    new_totals.append(totals[one] + tall)
                return tuple(new_totals)

            zero = jnp.zeros((8, BLOCK), jnp.float32)
            totals = lax.fori_loop(0, count, sum_step, tuple(zero for _ in pair_heads))
            for one in pair_heads:
                total = jnp.sum(totals[one], axis=0, keepdims=True)
                log_ref[block, :, stacks[one]] = tops[one] + jnp.log2(total)
            turned_ref[block] = jnp.zeros(turned_ref.shape[1:], jnp.float32)
            return carry

        lax.fori_loop(0, rows // BLOCK, query_block, 0)

    def grad_steps(block, first, end):
        def grad_step(step, carry):
            at = pl.ds(key_rows(block, step), STEP)
            vals = v_win[at, :]
            for one in pair_heads:
                logs = log_ref[block, :, stacks[one]]
                probs = jnp.exp2(score_ref[block, at, stacks[one]] - logs)
                grad_probs = contract_last(vals, g_stack[block, stacks[one], :])
                grads = probs * (grad_probs - delta_ref[block, :, stacks[one]])
                probs_ref[:, stacks[one]] = probs.astype(jnp.bfloat16)
                grads_ref[:, stacks[one]] = grads.astype(jnp.bfloat16)
            dv_acc[at, :] += contract_inner(probs_ref[...], g_stack[block])
            dk_acc[at, :] += contract_inner(grads_ref[...], q_stack[block])
            turned_ref[block] += contract_inner(kt_ref[:, at], grads_ref[...])
            return carry

        lax.fori_loop(first, end, grad_step, 0)

    def attend_halo(pair):
        def query_block(block, carry):
            for one in pair_heads:
                which = pair * len(pair_heads) + one
                cols = slice(which * HEAD_DIM, (which + 1) * HEAD_DIM)
                g_stack[block, stacks[one], :] = g_buf[query_rows(block), cols]
                delta_ref[block, :, stacks[one]] = jnp.concatenate(
                    [d_buf[block * parts + p, which : which + 1, :] for p in range(parts)], axis=1
                )
            grad_steps(block, block + 1, block_steps(block))
            return carry

        lax.fori_loop(0, rows // BLOCK, query_block, 0)

    def attend_own(pair, index):
        def query_block(block, carry):
            grad_steps(block, 0, jnp.minimum(block + 1, block_steps(block)))
            for one in pair_heads:
                which = pair * len(pair_heads) + one
                dq = turned_ref[block, :, stacks[one]].T * ATT_SCALE
                cols = slice(which * HEAD_DIM, (which + 1) * HEAD_DIM)
                dq_buf[query_rows(block), cols] = dq.astype(jnp.bfloat16)
            begin_block(index, block)
            return carry

        lax.fori_loop(0, rows // BLOCK, query_block, 0)

    arrived(3)
    for_runs(lambda run, *_: halo_copy(run, 0).wait_recv(), False)
    attend_sums(0)
    arrived(2, 4)
    for_runs(lambda run, *_: halo_copy(run, 1).wait_recv(), False)
    lowest = reach_tiles + BLOCK // TILE - block_steps(0) * (STEP // TILE)
    lax.fori_loop(lowest, reach_tiles + rows // TILE, turn, 0)
    attend_halo(0)
    attend_own(0, 7)
    arrived(5)
    attend_sums(1)
    arrived(6)
    attend_halo(1)

    for which in range(2):

        def send_back(run, distance, first, end):
            at = slice(halo - distance * rows + first, halo - distance * rows + end)
            part_sum = dv_acc[at, :] if which else dk_acc[at, :] * ATT_SCALE
            low_ref[which, at, :] = part_sum.astype(jnp.bfloat16)
            back_copy(run, which).start()

        for_runs(send_back, False)

    attend_own(1, 8)
    total_ref[0] = dk_acc[halo:, :] * ATT_SCALE
    total_ref[1] = dv_acc[halo:, :]
    for which in range(2):

        def take_back(run, distance, first, end):
            got = slice(halo - distance * rows + first, halo - distance * rows + end)
            back_copy(run, which).wait_recv()
            total_ref[which, first:end, :] += got_ref[which, got, :].astype(jnp.float32)

        for_runs(take_back, True)
        sum_ref[which] = total_ref[which].astype(jnp.bfloat16)
        begin(9 + which)

    for_runs(lambda run, *_: [halo_copy(run, which).wait_send() for which in range(2)], True)
    for_runs(lambda run, *_: [back_copy(run, which).wait_send() for which in range(2)], False)
    arrived(7, 8, 9, 10)
    for index in range(len(routes)):
        for step in range(1, peers):
            exchange(index, step).wait_send()


def whole(shards, plan, queries, keys, values, grad_out, delta, doc_lengths):
    peers = delta.shape[0]
    part = queries.shape[0]
    rows = part * peers
    width = queries.shape[1] // peers
    window = (REACH + 1) * rows + TILE
    low, full = jnp.bfloat16, jnp.float32
    wide = width // 2 // HEAD_DIM * BLOCK
    blocks = rows // BLOCK
    dma = pltpu.SemaphoreType.DMA
    return pl.pallas_call(
        functools.partial(whole_kernel, shards, plan),
        out_shape=(
            jax.ShapeDtypeStruct(queries.shape, low),
            jax.ShapeDtypeStruct(keys.shape, low),
            jax.ShapeDtypeStruct(values.shape, low),
        ),
        in_specs=[ANYWHERE] * 4 + [VMEM] * 2,
        out_specs=(ANYWHERE,) * 3,
        scratch_shapes=[
            pltpu.VMEM((rows, width), low),
            pltpu.VMEM((rows, width), low),
            pltpu.VMEM((window, HEAD_DIM), low),
            pltpu.VMEM((window, HEAD_DIM), low),
            pltpu.VMEM(delta.shape, full),
            pltpu.VMEM((1, rows), jnp.int32),
            pltpu.VMEM((HEAD_DIM, window), low),
            pltpu.VMEM((blocks, window, wide), full),
            pltpu.VMEM((STEP, wide), low),
            pltpu.VMEM((STEP, wide), low),
            pltpu.VMEM((blocks, wide, HEAD_DIM), low),
            pltpu.VMEM((blocks, wide, HEAD_DIM), low),
            pltpu.VMEM((blocks, 1, wide), full),
            pltpu.VMEM((blocks, 1, wide), full),
            pltpu.VMEM((blocks, HEAD_DIM, wide), full),
            pltpu.VMEM((window, HEAD_DIM), full),
            pltpu.VMEM((window, HEAD_DIM), full),
            pltpu.VMEM((rows, width), low),
            pltpu.VMEM((2, window - rows, HEAD_DIM), low),
            pltpu.VMEM((2, window - rows, HEAD_DIM), low),
            pltpu.VMEM((2, rows, HEAD_DIM), full),
            pltpu.VMEM((2, rows, HEAD_DIM), low),
            dma((11, peers)),
            dma((11, peers)),
            dma((11,)),
            dma((len(plan), 2)),
            dma((len(plan), 2)),
            dma((len(plan), 2)),
            dma((len(plan), 2)),
        ],
        compiler_params=pltpu.CompilerParams(
            collective_id=0, has_side_effects=True, vmem_limit_bytes=56 * 1024 * 1024
        ),
        name="whole",
    )(queries, keys, values, grad_out, delta, doc_lengths[None])


def settle_kernel(*refs):
    count = len(refs) // 2
    sems = refs[-1]
    copies = [
        pltpu.make_async_copy(refs[one], refs[count + one], sems.at[one]) for one in range(count)
    ]
    for copy in copies:
        copy.start()
    for copy in copies:
        copy.wait()


def settled(*arrays):
    return pl.pallas_call(
        settle_kernel,
        out_shape=tuple(jax.ShapeDtypeStruct(a.shape, a.dtype) for a in arrays),
        in_specs=[ANYWHERE] * len(arrays),
        out_specs=(ANYWHERE,) * len(arrays),
        scratch_shapes=[pltpu.SemaphoreType.DMA((len(arrays),))],
        name="settle",
    )(*arrays)


def on_device(queries, keys, values, grad_out, delta, doc_lengths):
    shards, peers = lax.axis_size("ctx"), lax.axis_size("head")
    rows = queries.shape[0] * peers
    delta = delta.reshape(peers, delta.shape[0] // peers, delta.shape[1])
    slots = jnp.arange(doc_lengths.shape[0], dtype=jnp.int32)
    doc_starts = jnp.sum(jnp.where(slots[:, None] < slots[None, :], doc_lengths[:, None], 0), axis=0)

    def start_at(places):
        return jnp.max(
            jnp.where(doc_starts[:, None] <= places[None, :], doc_starts[:, None], 0), axis=0
        )

    last_block = lax.div(doc_starts + doc_lengths - 1, jnp.int32(BLOCK))
    fits = jnp.all(doc_starts >= short_reach(last_block, shards, rows))

    def in_one(*operands):
        return whole(shards, halo_plan(shards, rows, True), *operands, doc_lengths)

    def in_three(*operands):
        plan = halo_plan(shards, rows, False)
        base = lax.axis_index("ctx") * rows
        starts = start_at(base + jnp.arange(rows, dtype=jnp.int32)) - (base - REACH * rows - TILE)
        q, k, v, g, d = gather(shards, plan, *operands)
        dq, dk, dv = attention(starts[::TILE], q, g, k, v, d, starts[None])
        return scatter(shards, plan, peers, dq, dk, dv)

    return settled(*lax.cond(fits, in_one, in_three, queries, keys, values, grad_out, delta))


def solution(mesh):
    rows = P(("ctx", "head"), None)
    return jax.shard_map(
        on_device,
        mesh=mesh,
        in_specs=(rows, rows, rows, rows, P(None, ("ctx", "head")), P()),
        out_specs=(rows, rows, rows),
        check_vma=False,
    )
```

```python
import functools

import jax
import jax.numpy as jnp
from jax import lax
from jax.experimental import pallas as pl
from jax.experimental.pallas import tpu as pltpu
from jax.sharding import PartitionSpec as P

HEAD_DIM = 128
TILE = 256
STEP = 512
BLOCK = 512
HOPS = ((2, 1), (2, 0), (1, 1), (3, 1), (0, 1), (1, 0), (3, 0))
REACH = 2
NEG_FILL = -1e30
ATT_SCALE = HEAD_DIM ** (-0.5)
LOG2E = 1.4426950408889634
MESH = pl.DeviceIdType.MESH
VMEM = pl.BlockSpec(memory_space=pltpu.VMEM)
ANYWHERE = pl.BlockSpec(memory_space=pl.ANY)


def long_firsts(shards):
    middle = shards // 2
    return (0, middle - 3, middle - 1, middle + 1, shards - 3)


def halo_plan(shards, rows, short):
    near = tuple(range(shards - 1))
    far = tuple(range(shards - 2))
    if not short:
        return ((1, 0, rows, near), (2, 0, rows, far))
    firsts = long_firsts(shards)
    seconds = tuple(first + 1 for first in firsts)
    half = rows // 2
    return (
        (1, rows - TILE, rows, near),
        (1, half, rows - TILE, tuple(sorted(set(firsts + seconds)))),
        (1, 0, half, seconds),
        (2, half, rows, firsts),
    )


def short_reach(blocks, shards, rows):
    shard = lax.shift_right_logical(blocks, jnp.int32((rows // BLOCK).bit_length() - 1))
    reach = jnp.where(shard == 0, 0, blocks * BLOCK - TILE)
    for first in long_firsts(shards):
        opening = first * rows + rows // 2
        holds = (shard == first + 1) | (shard == first + 2)
        reach = jnp.where(holds, jnp.minimum(reach, opening), reach)
    return reach


def is_one_of(index, members, shards):
    if members == tuple(range(len(members))):
        return index < len(members)
    return functools.reduce(jnp.logical_or, [index == member for member in members])


def contract_last(left, right):
    return lax.dot_general(
        left, right, (((1,), (1,)), ((), ())), preferred_element_type=jnp.float32
    )


def contract_inner(left, right):
    return jnp.dot(left, right, preferred_element_type=jnp.float32)


def meet(shards, peers, upward):
    ctx, head = lax.axis_index("ctx"), lax.axis_index("head")
    barrier = pltpu.get_barrier_semaphore()
    for step in range(1, peers):
        pl.semaphore_signal(
            barrier, inc=1, device_id=(ctx, lax.rem(head + step, peers)), device_id_type=MESH
        )
    for distance in (1, 2):
        other = ctx - distance if upward else ctx + distance
        there = ctx >= distance if upward else ctx < shards - distance

        @pl.when(there)
        def _():
            pl.semaphore_signal(barrier, inc=1, device_id=(other, head), device_id_type=MESH)

    beyond = shards - 1 - ctx if upward else ctx
    pl.semaphore_wait(barrier, peers - 1 + jnp.minimum(beyond, REACH))


def gather_kernel(
    shards,
    plan,
    q_in,
    k_in,
    v_in,
    g_in,
    d_in,
    q_out,
    k_out,
    v_out,
    g_out,
    d_out,
    send_sem,
    recv_sem,
    local_sem,
    halo_send,
    halo_recv,
):
    ctx, head = lax.axis_index("ctx"), lax.axis_index("head")
    part = q_in.shape[0]
    rows = q_out.shape[0]
    peers = rows // part
    halo = k_out.shape[0] - rows
    k_out[:halo, :] = jnp.zeros((halo, HEAD_DIM), k_out.dtype)
    v_out[:halo, :] = jnp.zeros((halo, HEAD_DIM), v_out.dtype)
    meet(shards, peers, True)

    def columns(ref, owner):
        width = ref.shape[1] // peers
        return ref.at[:, pl.ds(pl.multiple_of(owner * width, width), width)]

    def own_rows(ref, owner, first):
        return ref.at[pl.ds(pl.multiple_of(first + owner * part, part), part), :]

    pairs = (
        (lambda to: columns(k_in, to), lambda of: own_rows(k_out, of, halo)),
        (lambda to: columns(v_in, to), lambda of: own_rows(v_out, of, halo)),
        (lambda to: d_in.at[to], lambda of: d_out.at[of]),
        (lambda to: columns(q_in, to), lambda of: own_rows(q_out, of, 0)),
        (lambda to: columns(g_in, to), lambda of: own_rows(g_out, of, 0)),
    )

    def exchange(index, step):
        to = lax.rem(head + step, peers)
        source, target = pairs[index]
        return pltpu.make_async_remote_copy(
            src_ref=source(to),
            dst_ref=target(head),
            send_sem=send_sem.at[index, step],
            recv_sem=recv_sem.at[index, step],
            device_id=(ctx, to),
            device_id_type=MESH,
        )

    def keep(index):
        source, target = pairs[index]
        return pltpu.make_async_copy(source(head), target(head), local_sem.at[index])

    def arrived(index, step):
        source, target = pairs[index]
        of = lax.rem(head + peers - step, peers)
        pltpu.make_async_remote_copy(
            src_ref=source(head),
            dst_ref=target(of),
            send_sem=send_sem.at[index, step],
            recv_sem=recv_sem.at[index, step],
            device_id=(ctx, of),
            device_id_type=MESH,
        ).wait_recv()

    for index in range(5):
        keep(index).start()
        for step in range(1, peers):
            exchange(index, step).start()
    for index in range(2):
        keep(index).wait()
        for step in range(1, peers):
            arrived(index, step)

    def halo_copy(run, which):
        distance, first, end, _ = plan[run]
        ref = (k_out, v_out)[which]
        return pltpu.make_async_remote_copy(
            src_ref=ref.at[halo + first : halo + end, :],
            dst_ref=ref.at[halo - distance * rows + first : halo - distance * rows + end, :],
            send_sem=halo_send.at[run, which],
            recv_sem=halo_recv.at[run, which],
            device_id=(ctx + distance, head),
            device_id_type=MESH,
        )

    for run, (distance, first, end, senders) in enumerate(plan):

        @pl.when(is_one_of(ctx, senders, shards))
        def _():
            for which in range(2):
                halo_copy(run, which).start()

    for index in range(2, 5):
        keep(index).wait()
        for step in range(1, peers):
            arrived(index, step)
    for run, (distance, first, end, senders) in enumerate(plan):

        @pl.when(is_one_of(ctx, senders, shards))
        def _():
            for which in range(2):
                halo_copy(run, which).wait_send()

        @pl.when(is_one_of(ctx - distance, senders, shards) & (ctx >= distance))
        def _():
            for which in range(2):
                halo_copy(run, which).wait_recv()

    for index in range(5):
        for step in range(1, peers):
            exchange(index, step).wait_send()


def gather(shards, plan, queries, keys, values, grad_out, delta):
    peers = delta.shape[0]
    rows = queries.shape[0] * peers
    window = (REACH + 1) * rows + TILE
    width = queries.shape[1] // peers
    low = jnp.bfloat16
    return pl.pallas_call(
        functools.partial(gather_kernel, shards, plan),
        out_shape=(
            jax.ShapeDtypeStruct((rows, width), low),
            jax.ShapeDtypeStruct((window, HEAD_DIM), low),
            jax.ShapeDtypeStruct((window, HEAD_DIM), low),
            jax.ShapeDtypeStruct((rows, width), low),
            jax.ShapeDtypeStruct(delta.shape, jnp.float32),
        ),
        in_specs=[ANYWHERE] * 4 + [VMEM],
        out_specs=(VMEM,) * 5,
        scratch_shapes=[
            pltpu.SemaphoreType.DMA((5, peers)),
            pltpu.SemaphoreType.DMA((5, peers)),
            pltpu.SemaphoreType.DMA((5,)),
            pltpu.SemaphoreType.DMA((len(plan), 2)),
            pltpu.SemaphoreType.DMA((len(plan), 2)),
        ],
        compiler_params=pltpu.CompilerParams(
            collective_id=1,
            has_side_effects=True,
            vmem_limit_bytes=32 * 1024 * 1024,
        ),
        name="gather",
    )(queries, keys, values, grad_out, delta)


def attention_kernel(
    first_row,
    q_ref,
    g_ref,
    k_ref,
    v_ref,
    delta_ref,
    start_ref,
    dq_ref,
    dk_ref,
    dv_ref,
    kt_ref,
    score_ref,
    turned_ref,
):
    rows = q_ref.shape[0]
    heads = range(q_ref.shape[1] // HEAD_DIM)
    halo = k_ref.shape[0] - rows
    parts = TILE // delta_ref.shape[2]
    columns = [slice(head * HEAD_DIM, (head + 1) * HEAD_DIM) for head in heads]
    dk_ref[...] = jnp.zeros_like(dk_ref)
    dv_ref[...] = jnp.zeros_like(dv_ref)
    key_offset = lax.broadcasted_iota(jnp.int32, (STEP, TILE), 0)
    query_offset = lax.broadcasted_iota(jnp.int32, (1, TILE), 1)

    def turn(tile, carry):
        at = pl.ds(pl.multiple_of(tile * TILE, TILE), TILE)
        kt_ref[:, at] = k_ref[at, :].T
        return carry

    lax.fori_loop(jnp.maximum(first_row[0] // TILE - 1, 0), k_ref.shape[0] // TILE, turn, 0)

    def query_block(block, carry):
        q_at = pl.ds(pl.multiple_of(block * TILE, TILE), TILE)
        end = halo + (block + 1) * TILE
        count = (end - first_row[block] + STEP - 1) // STEP
        start = start_ref[:, q_at]
        last = query_offset + (end - TILE)
        deltas = [
            jnp.concatenate(
                [delta_ref[block * parts + part, head : head + 1, :] for part in range(parts)],
                axis=1,
            )
            for head in heads
        ]

        def key_rows(step):
            return pl.multiple_of(end - (step + 1) * STEP, TILE)

        def score_step(step, tops):
            first = key_rows(step)
            at = pl.ds(first, STEP)
            keys = k_ref[at, :]
            place = key_offset + first
            allowed = (place >= start) & (place <= last)
            new_tops = []
            for head in heads:
                scores = contract_last(keys, q_ref[q_at, columns[head]]) * (ATT_SCALE * LOG2E)
                scores = jnp.where(allowed, scores, NEG_FILL)
                score_ref[head, at, :] = scores
                tall = jnp.max(scores.reshape(STEP // 8, 8, TILE), axis=0)
                new_tops.append(jnp.maximum(tops[head], tall))
            return tuple(new_tops)

        none = jnp.full((8, TILE), NEG_FILL, jnp.float32)
        tops = lax.fori_loop(0, count, score_step, tuple(none for _ in heads))
        tops = [jnp.max(top, axis=0, keepdims=True) for top in tops]

        def sum_step(step, totals):
            at = pl.ds(key_rows(step), STEP)
            new_totals = []
            for head in heads:
                powers = jnp.exp2(score_ref[head, at, :] - tops[head])
                new_totals.append(
                    totals[head] + jnp.sum(powers.reshape(STEP // 8, 8, TILE), axis=0)
                )
            return tuple(new_totals)

        zero = jnp.zeros((8, TILE), jnp.float32)
        totals = lax.fori_loop(0, count, sum_step, tuple(zero for _ in heads))
        log_totals = [
            tops[head] + jnp.log2(jnp.sum(totals[head], axis=0, keepdims=True)) for head in heads
        ]
        turned_ref[...] = jnp.zeros_like(turned_ref)

        def grad_step(step, carry):
            at = pl.ds(key_rows(step), STEP)
            vals = v_ref[at, :]
            keys_turned = kt_ref[:, at]
            val_parts, key_parts = [], []
            for head in heads:
                q = q_ref[q_at, columns[head]]
                g = g_ref[q_at, columns[head]]
                probs = jnp.exp2(score_ref[head, at, :] - log_totals[head])
                grad_probs = contract_last(vals, g)
                grad_scores = (probs * (grad_probs - deltas[head])).astype(jnp.bfloat16)
                val_parts.append(contract_inner(probs.astype(jnp.bfloat16), g))
                key_parts.append(contract_inner(grad_scores, q))
                turned_ref[head] += contract_inner(keys_turned, grad_scores)
            dv_ref[at, :] += sum(val_parts[1:], val_parts[0])
            dk_ref[at, :] += sum(key_parts[1:], key_parts[0])
            return carry

        lax.fori_loop(0, count, grad_step, 0)
        for head in heads:
            dq_ref[q_at, columns[head]] = (turned_ref[head].T * ATT_SCALE).astype(jnp.bfloat16)
        return carry

    lax.fori_loop(0, rows // TILE, query_block, 0)


def attention(first_row, q, g, keys, vals, delta, starts):
    window = keys.shape[0]
    heads = q.shape[1] // HEAD_DIM
    return pl.pallas_call(
        attention_kernel,
        out_shape=(
            jax.ShapeDtypeStruct(q.shape, jnp.bfloat16),
            jax.ShapeDtypeStruct(keys.shape, jnp.float32),
            jax.ShapeDtypeStruct(keys.shape, jnp.float32),
        ),
        in_specs=[pl.BlockSpec(memory_space=pltpu.SMEM)] + [VMEM] * 6,
        out_specs=(VMEM,) * 3,
        scratch_shapes=[
            pltpu.VMEM((HEAD_DIM, window), jnp.bfloat16),
            pltpu.VMEM((heads, window, TILE), jnp.float32),
            pltpu.VMEM((heads, HEAD_DIM, TILE), jnp.float32),
        ],
        compiler_params=pltpu.CompilerParams(vmem_limit_bytes=44 * 1024 * 1024),
        name="attention",
    )(first_row, q, g, keys, vals, delta, starts)


def scatter_kernel(
    shards,
    plan,
    dq_in,
    dk_in,
    dv_in,
    dq_out,
    dk_out,
    dv_out,
    low_ref,
    got_ref,
    total_ref,
    sum_ref,
    send_sem,
    recv_sem,
    local_sem,
    halo_send,
    halo_recv,
):
    ctx, head = lax.axis_index("ctx"), lax.axis_index("head")
    part = dq_out.shape[0]
    rows = dq_in.shape[0]
    peers = rows // part
    halo = dk_in.shape[0] - rows
    meet(shards, peers, False)

    def columns(ref, owner):
        width = ref.shape[1] // peers
        return ref.at[:, pl.ds(pl.multiple_of(owner * width, width), width)]

    def row_part(ref, owner):
        return ref.at[pl.ds(pl.multiple_of(owner * part, part), part), :]

    pairs = (
        (lambda to: row_part(dq_in, to), lambda of: columns(dq_out, of)),
        (lambda to: row_part(sum_ref.at[0], to), lambda of: columns(dk_out, of)),
        (lambda to: row_part(sum_ref.at[1], to), lambda of: columns(dv_out, of)),
    )

    def exchange(index, step):
        to = lax.rem(head + step, peers)
        source, target = pairs[index]
        return pltpu.make_async_remote_copy(
            src_ref=source(to),
            dst_ref=target(head),
            send_sem=send_sem.at[index, step],
            recv_sem=recv_sem.at[index, step],
            device_id=(ctx, to),
            device_id_type=MESH,
        )

    def keep(index):
        source, target = pairs[index]
        return pltpu.make_async_copy(source(head), target(head), local_sem.at[index])

    def arrived(index, step):
        source, target = pairs[index]
        of = lax.rem(head + peers - step, peers)
        pltpu.make_async_remote_copy(
            src_ref=source(head),
            dst_ref=target(of),
            send_sem=send_sem.at[index, step],
            recv_sem=recv_sem.at[index, step],
            device_id=(ctx, of),
            device_id_type=MESH,
        ).wait_recv()

    def halo_copy(run, which):
        distance, first, end, _ = plan[run]
        base = halo - distance * rows
        return pltpu.make_async_remote_copy(
            src_ref=low_ref.at[which, base + first : base + end, :],
            dst_ref=got_ref.at[which, base + first : base + end, :],
            send_sem=halo_send.at[run, which],
            recv_sem=halo_recv.at[run, which],
            device_id=(ctx - distance, head),
            device_id_type=MESH,
        )

    for run, (distance, first, end, senders) in enumerate(plan):

        @pl.when(is_one_of(ctx - distance, senders, shards) & (ctx >= distance))
        def _():
            at = slice(halo - distance * rows + first, halo - distance * rows + end)
            low_ref[0, at, :] = (dk_in[at, :] * ATT_SCALE).astype(jnp.bfloat16)
            low_ref[1, at, :] = dv_in[at, :].astype(jnp.bfloat16)
            for which in range(2):
                halo_copy(run, which).start()

    keep(0).start()
    for step in range(1, peers):
        exchange(0, step).start()
    total_ref[0] = dk_in[halo:, :] * ATT_SCALE
    total_ref[1] = dv_in[halo:, :]

    for run, (distance, first, end, senders) in enumerate(plan):

        @pl.when(is_one_of(ctx, senders, shards))
        def _():
            got = slice(halo - distance * rows + first, halo - distance * rows + end)
            own = slice(first, end)
            for which in range(2):
                halo_copy(run, which).wait_recv()
                total_ref[which, own, :] += got_ref[which, got, :].astype(jnp.float32)

    sum_ref[...] = total_ref[...].astype(jnp.bfloat16)
    for index in (1, 2):
        keep(index).start()
        for step in range(1, peers):
            exchange(index, step).start()
    for run, (distance, first, end, senders) in enumerate(plan):

        @pl.when(is_one_of(ctx - distance, senders, shards) & (ctx >= distance))
        def _():
            for which in range(2):
                halo_copy(run, which).wait_send()

    for index in range(3):
        keep(index).wait()
        for step in range(1, peers):
            arrived(index, step)
            exchange(index, step).wait_send()


def scatter(shards, plan, peers, dq, dk, dv):
    rows, width = dq.shape
    window = dk.shape[0]
    low = jnp.bfloat16
    return pl.pallas_call(
        functools.partial(scatter_kernel, shards, plan),
        out_shape=(
            jax.ShapeDtypeStruct((rows // peers, width * peers), low),
            jax.ShapeDtypeStruct((rows // peers, HEAD_DIM * peers), low),
            jax.ShapeDtypeStruct((rows // peers, HEAD_DIM * peers), low),
        ),
        in_specs=[VMEM] * 3,
        out_specs=(ANYWHERE,) * 3,
        scratch_shapes=[
            pltpu.VMEM((2, window - rows, HEAD_DIM), low),
            pltpu.VMEM((2, window - rows, HEAD_DIM), low),
            pltpu.VMEM((2, rows, HEAD_DIM), jnp.float32),
            pltpu.VMEM((2, rows, HEAD_DIM), low),
            pltpu.SemaphoreType.DMA((3, peers)),
            pltpu.SemaphoreType.DMA((3, peers)),
            pltpu.SemaphoreType.DMA((3,)),
            pltpu.SemaphoreType.DMA((len(plan), 2)),
            pltpu.SemaphoreType.DMA((len(plan), 2)),
        ],
        compiler_params=pltpu.CompilerParams(
            collective_id=2,
            has_side_effects=True,
            vmem_limit_bytes=32 * 1024 * 1024,
        ),
        name="scatter",
    )(dq, dk, dv)


def first_tiles(ctx, block, shards, rows, reach_tiles):
    own = rows // TILE
    half = own // 2
    firsts = long_firsts(shards)
    second = is_one_of(ctx, tuple(first + 1 for first in firsts), shards)
    third = is_one_of(ctx, tuple(first + 2 for first in firsts), shards)
    low = reach_tiles + block * (BLOCK // TILE) - 1
    low = jnp.where(ctx == 0, reach_tiles, low)
    low = jnp.where(second, reach_tiles - half, low)
    return jnp.where(third, reach_tiles - own - half, low)


def whole_kernel(
    shards,
    plan,
    q_in,
    k_in,
    v_in,
    g_in,
    d_in,
    lengths_ref,
    dq_out,
    dk_out,
    dv_out,
    q_buf,
    g_buf,
    k_win,
    v_win,
    d_buf,
    start_ref,
    kt_ref,
    score_ref,
    probs_ref,
    grads_ref,
    q_stack,
    g_stack,
    delta_ref,
    log_ref,
    turned_ref,
    dk_acc,
    dv_acc,
    dq_buf,
    low_ref,
    got_ref,
    total_ref,
    sum_ref,
    send_sem,
    recv_sem,
    local_sem,
    halo_send,
    halo_recv,
    back_send,
    back_recv,
):
    ctx, head = lax.axis_index("ctx"), lax.axis_index("head")
    part = q_in.shape[0]
    rows, width = q_buf.shape
    peers = rows // part
    halo = k_win.shape[0] - rows
    half_width = width // 2
    pair_heads = range(half_width // HEAD_DIM)
    stacks = [slice(one * BLOCK, (one + 1) * BLOCK) for one in pair_heads]
    k_win[:halo, :] = jnp.zeros((halo, HEAD_DIM), k_win.dtype)
    v_win[:halo, :] = jnp.zeros((halo, HEAD_DIM), v_win.dtype)

    barrier = pltpu.get_barrier_semaphore()
    for step in range(1, peers):
        pl.semaphore_signal(
            barrier, inc=1, device_id=(ctx, lax.rem(head + step, peers)), device_id_type=MESH
        )
    for distance in (1, 2):

        @pl.when(ctx >= distance)
        def _():
            pl.semaphore_signal(
                barrier, inc=1, device_id=(ctx - distance, head), device_id_type=MESH
            )

        @pl.when(ctx < shards - distance)
        def _():
            pl.semaphore_signal(
                barrier, inc=1, device_id=(ctx + distance, head), device_id_type=MESH
            )

    around = jnp.minimum(shards - 1 - ctx, REACH) + jnp.minimum(ctx, REACH)
    pl.semaphore_wait(barrier, peers - 1 + around)

    def partner(step, sign):
        along, across = HOPS[step - 1]
        line = peers // 2
        moved = lax.rem(lax.div(head, 2) + (along if sign > 0 else line - along), line)
        return moved * 2 + lax.rem(head + across, 2)

    def columns(ref, owner, offset, size):
        stride = ref.shape[1] // peers
        return ref.at[:, pl.ds(pl.multiple_of(owner * stride + offset, size), size)]

    def own_rows(ref, owner, first):
        return ref.at[pl.ds(pl.multiple_of(first + owner * part, part), part), :]

    def own_pair(ref, owner, pair):
        at = pl.ds(pl.multiple_of(owner * part, part), part)
        return ref.at[at, pair * half_width : (pair + 1) * half_width]

    def paired_in(source, target, pair):
        return (
            lambda to: columns(source, to, pair * half_width, half_width),
            lambda of: own_pair(target, of, pair),
        )

    def paired_out(source, target, pair):
        return (
            lambda to: own_pair(source, to, pair),
            lambda of: columns(target, of, pair * half_width, half_width),
        )

    routes = (
        (lambda to: columns(k_in, to, 0, HEAD_DIM), lambda of: own_rows(k_win, of, halo)),
        (lambda to: columns(v_in, to, 0, HEAD_DIM), lambda of: own_rows(v_win, of, halo)),
        (lambda to: d_in.at[to], lambda of: d_buf.at[of]),
        paired_in(q_in, q_buf, 0),
        paired_in(g_in, g_buf, 0),
        paired_in(q_in, q_buf, 1),
        paired_in(g_in, g_buf, 1),
        paired_out(dq_buf, dq_out, 0),
        paired_out(dq_buf, dq_out, 1),
        (lambda to: own_rows(sum_ref.at[0], to, 0), lambda of: columns(dk_out, of, 0, HEAD_DIM)),
        (lambda to: own_rows(sum_ref.at[1], to, 0), lambda of: columns(dv_out, of, 0, HEAD_DIM)),
    )

    def exchange(index, step):
        to = partner(step, 1)
        source, target = routes[index]
        return pltpu.make_async_remote_copy(
            src_ref=source(to),
            dst_ref=target(head),
            send_sem=send_sem.at[index, step],
            recv_sem=recv_sem.at[index, step],
            device_id=(ctx, to),
            device_id_type=MESH,
        )

    def keep(index):
        source, target = routes[index]
        return pltpu.make_async_copy(source(head), target(head), local_sem.at[index])

    def begin(*indices):
        for index in indices:
            keep(index).start()
            for step in range(1, peers):
                exchange(index, step).start()

    def begin_block(index, block):
        per_block = BLOCK // part

        @pl.when(lax.div(head, per_block) == block)
        def _():
            keep(index).start()

        for step in range(1, peers):

            @pl.when(lax.div(partner(step, 1), per_block) == block)
            def _():
                exchange(index, step).start()

    def arrived(*indices):
        for index in indices:
            keep(index).wait()
            source, target = routes[index]
            for step in range(1, peers):
                of = partner(step, -1)
                pltpu.make_async_remote_copy(
                    src_ref=source(head),
                    dst_ref=target(of),
                    send_sem=send_sem.at[index, step],
                    recv_sem=recv_sem.at[index, step],
                    device_id=(ctx, of),
                    device_id_type=MESH,
                ).wait_recv()

    def halo_copy(run, which):
        distance, first, end, _ = plan[run]
        ref = (k_win, v_win)[which]
        base = halo - distance * rows
        return pltpu.make_async_remote_copy(
            src_ref=ref.at[halo + first : halo + end, :],
            dst_ref=ref.at[base + first : base + end, :],
            send_sem=halo_send.at[run, which],
            recv_sem=halo_recv.at[run, which],
            device_id=(ctx + distance, head),
            device_id_type=MESH,
        )

    def back_copy(run, which):
        distance, first, end, _ = plan[run]
        base = halo - distance * rows
        return pltpu.make_async_remote_copy(
            src_ref=low_ref.at[which, base + first : base + end, :],
            dst_ref=got_ref.at[which, base + first : base + end, :],
            send_sem=back_send.at[run, which],
            recv_sem=back_recv.at[run, which],
            device_id=(ctx - distance, head),
            device_id_type=MESH,
        )

    def for_runs(body, upward):
        for run, (distance, first, end, senders) in enumerate(plan):
            if upward:
                here = is_one_of(ctx, senders, shards)
            else:
                here = is_one_of(ctx - distance, senders, shards) & (ctx >= distance)

            @pl.when(here)
            def _():
                body(run, distance, first, end)

    begin(0, 1, 3, 2, 4)

    docs = lengths_ref.shape[1]
    before = lax.broadcasted_iota(jnp.int32, (docs, docs), 1) < lax.broadcasted_iota(
        jnp.int32, (docs, docs), 0
    )
    lengths = lengths_ref[...].astype(jnp.float32)
    doc_starts = jnp.sum(jnp.where(before, lengths, 0.0), axis=1, keepdims=True)
    doc_starts = doc_starts - (ctx * rows - halo).astype(jnp.float32)
    places = lax.broadcasted_iota(jnp.int32, (1, rows), 1).astype(jnp.float32) + float(halo)
    starts = jnp.max(jnp.where(doc_starts <= places, doc_starts, -1e9), axis=0, keepdims=True)
    start_ref[...] = starts.astype(jnp.int32)
    dk_acc[...] = jnp.zeros_like(dk_acc)
    dv_acc[...] = jnp.zeros_like(dv_acc)

    for which in range(2):
        arrived(which)
        for_runs(lambda run, *_: halo_copy(run, which).start(), True)

    reach_tiles = halo // TILE
    key_offset = lax.broadcasted_iota(jnp.int32, (STEP, BLOCK), 0)
    query_offset = lax.broadcasted_iota(jnp.int32, (1, BLOCK), 1)
    parts = BLOCK // part

    def block_steps(block):
        low = first_tiles(ctx, block, shards, rows, reach_tiles)
        tiles = reach_tiles + (block + 1) * (BLOCK // TILE) - low
        return lax.div(tiles + STEP // TILE - 1, STEP // TILE)

    def turn(tile, carry):
        at = pl.ds(pl.multiple_of(tile * TILE, TILE), TILE)
        kt_ref[:, at] = k_win[at, :].T
        return carry

    def key_rows(block, step):
        return pl.multiple_of(halo + (block + 1) * BLOCK - (step + 1) * STEP, TILE)

    def query_rows(block):
        return pl.ds(pl.multiple_of(block * BLOCK, BLOCK), BLOCK)

    def attend_sums(pair):
        def query_block(block, carry):
            q_at = query_rows(block)
            count = block_steps(block)
            start = start_ref[:, q_at]
            last = query_offset + (halo + block * BLOCK)
            for one in pair_heads:
                which = pair * len(pair_heads) + one
                cols = slice(which * HEAD_DIM, (which + 1) * HEAD_DIM)
                q_stack[block, stacks[one], :] = q_buf[q_at, cols]

            def score_step(step, tops):
                first = key_rows(block, step)
                at = pl.ds(first, STEP)
                keys = k_win[at, :]
                place = key_offset + first
                allowed = (place >= start) & (place <= last)
                new_tops = []
                for one in pair_heads:
                    scores = contract_last(keys, q_stack[block, stacks[one], :])
                    scores = jnp.where(allowed, scores * (ATT_SCALE * LOG2E), NEG_FILL)
                    score_ref[block, at, stacks[one]] = scores
                    tall = jnp.max(scores.reshape(STEP // 8, 8, BLOCK), axis=0)
                    new_tops.append(jnp.maximum(tops[one], tall))
                return tuple(new_tops)

            none = jnp.full((8, BLOCK), NEG_FILL, jnp.float32)
            tops = lax.fori_loop(0, count, score_step, tuple(none for _ in pair_heads))
            tops = [jnp.max(top, axis=0, keepdims=True) for top in tops]

            def sum_step(step, totals):
                at = pl.ds(key_rows(block, step), STEP)
                new_totals = []
                for one in pair_heads:
                    powers = jnp.exp2(score_ref[block, at, stacks[one]] - tops[one])
                    tall = jnp.sum(powers.reshape(STEP // 8, 8, BLOCK), axis=0)
                    new_totals.append(totals[one] + tall)
                return tuple(new_totals)

            zero = jnp.zeros((8, BLOCK), jnp.float32)
            totals = lax.fori_loop(0, count, sum_step, tuple(zero for _ in pair_heads))
            for one in pair_heads:
                total = jnp.sum(totals[one], axis=0, keepdims=True)
                log_ref[block, :, stacks[one]] = tops[one] + jnp.log2(total)
            turned_ref[block] = jnp.zeros(turned_ref.shape[1:], jnp.float32)
            return carry

        lax.fori_loop(0, rows // BLOCK, query_block, 0)

    def grad_steps(block, first, end):
        def grad_step(step, carry):
            at = pl.ds(key_rows(block, step), STEP)
            vals = v_win[at, :]
            for one in pair_heads:
                logs = log_ref[block, :, stacks[one]]
                probs = jnp.exp2(score_ref[block, at, stacks[one]] - logs)
                grad_probs = contract_last(vals, g_stack[block, stacks[one], :])
                grads = probs * (grad_probs - delta_ref[block, :, stacks[one]])
                probs_ref[:, stacks[one]] = probs.astype(jnp.bfloat16)
                grads_ref[:, stacks[one]] = grads.astype(jnp.bfloat16)
            dv_acc[at, :] += contract_inner(probs_ref[...], g_stack[block])
            dk_acc[at, :] += contract_inner(grads_ref[...], q_stack[block])
            turned_ref[block] += contract_inner(kt_ref[:, at], grads_ref[...])
            return carry

        lax.fori_loop(first, end, grad_step, 0)

    def attend_halo(pair):
        def query_block(block, carry):
            for one in pair_heads:
                which = pair * len(pair_heads) + one
                cols = slice(which * HEAD_DIM, (which + 1) * HEAD_DIM)
                g_stack[block, stacks[one], :] = g_buf[query_rows(block), cols]
                delta_ref[block, :, stacks[one]] = jnp.concatenate(
                    [d_buf[block * parts + p, which : which + 1, :] for p in range(parts)], axis=1
                )
            grad_steps(block, block + 1, block_steps(block))
            return carry

        lax.fori_loop(0, rows // BLOCK, query_block, 0)

    def attend_own(pair, index):
        def query_block(block, carry):
            grad_steps(block, 0, jnp.minimum(block + 1, block_steps(block)))
            for one in pair_heads:
                which = pair * len(pair_heads) + one
                dq = turned_ref[block, :, stacks[one]].T * ATT_SCALE
                cols = slice(which * HEAD_DIM, (which + 1) * HEAD_DIM)
                dq_buf[query_rows(block), cols] = dq.astype(jnp.bfloat16)
            begin_block(index, block)
            return carry

        lax.fori_loop(0, rows // BLOCK, query_block, 0)

    arrived(3)
    for_runs(lambda run, *_: halo_copy(run, 0).wait_recv(), False)
    begin(5, 6)
    attend_sums(0)
    arrived(2, 4)
    for_runs(lambda run, *_: halo_copy(run, 1).wait_recv(), False)
    lowest = reach_tiles + BLOCK // TILE - block_steps(0) * (STEP // TILE)
    lax.fori_loop(lowest, reach_tiles + rows // TILE, turn, 0)
    attend_halo(0)
    attend_own(0, 7)
    arrived(5)
    attend_sums(1)
    arrived(6)
    attend_halo(1)

    for which in range(2):

        def send_back(run, distance, first, end):
            at = slice(halo - distance * rows + first, halo - distance * rows + end)
            part_sum = dv_acc[at, :] if which else dk_acc[at, :] * ATT_SCALE
            low_ref[which, at, :] = part_sum.astype(jnp.bfloat16)
            back_copy(run, which).start()

        for_runs(send_back, False)

    attend_own(1, 8)
    total_ref[0] = dk_acc[halo:, :] * ATT_SCALE
    total_ref[1] = dv_acc[halo:, :]
    for which in range(2):

        def take_back(run, distance, first, end):
            got = slice(halo - distance * rows + first, halo - distance * rows + end)
            back_copy(run, which).wait_recv()
            total_ref[which, first:end, :] += got_ref[which, got, :].astype(jnp.float32)

        for_runs(take_back, True)
        sum_ref[which] = total_ref[which].astype(jnp.bfloat16)
        begin(9 + which)

    for_runs(lambda run, *_: [halo_copy(run, which).wait_send() for which in range(2)], True)
    for_runs(lambda run, *_: [back_copy(run, which).wait_send() for which in range(2)], False)
    arrived(7, 8, 9, 10)
    for index in range(len(routes)):
        for step in range(1, peers):
            exchange(index, step).wait_send()


def whole(shards, plan, queries, keys, values, grad_out, delta, doc_lengths):
    peers = delta.shape[0]
    part = queries.shape[0]
    rows = part * peers
    width = queries.shape[1] // peers
    window = (REACH + 1) * rows + TILE
    low, full = jnp.bfloat16, jnp.float32
    wide = width // 2 // HEAD_DIM * BLOCK
    blocks = rows // BLOCK
    dma = pltpu.SemaphoreType.DMA
    return pl.pallas_call(
        functools.partial(whole_kernel, shards, plan),
        out_shape=(
            jax.ShapeDtypeStruct(queries.shape, low),
            jax.ShapeDtypeStruct(keys.shape, low),
            jax.ShapeDtypeStruct(values.shape, low),
        ),
        in_specs=[ANYWHERE] * 4 + [VMEM] * 2,
        out_specs=(ANYWHERE,) * 3,
        scratch_shapes=[
            pltpu.VMEM((rows, width), low),
            pltpu.VMEM((rows, width), low),
            pltpu.VMEM((window, HEAD_DIM), low),
            pltpu.VMEM((window, HEAD_DIM), low),
            pltpu.VMEM(delta.shape, full),
            pltpu.VMEM((1, rows), jnp.int32),
            pltpu.VMEM((HEAD_DIM, window), low),
            pltpu.VMEM((blocks, window, wide), full),
            pltpu.VMEM((STEP, wide), low),
            pltpu.VMEM((STEP, wide), low),
            pltpu.VMEM((blocks, wide, HEAD_DIM), low),
            pltpu.VMEM((blocks, wide, HEAD_DIM), low),
            pltpu.VMEM((blocks, 1, wide), full),
            pltpu.VMEM((blocks, 1, wide), full),
            pltpu.VMEM((blocks, HEAD_DIM, wide), full),
            pltpu.VMEM((window, HEAD_DIM), full),
            pltpu.VMEM((window, HEAD_DIM), full),
            pltpu.VMEM((rows, width), low),
            pltpu.VMEM((2, window - rows, HEAD_DIM), low),
            pltpu.VMEM((2, window - rows, HEAD_DIM), low),
            pltpu.VMEM((2, rows, HEAD_DIM), full),
            pltpu.VMEM((2, rows, HEAD_DIM), low),
            dma((11, peers)),
            dma((11, peers)),
            dma((11,)),
            dma((len(plan), 2)),
            dma((len(plan), 2)),
            dma((len(plan), 2)),
            dma((len(plan), 2)),
        ],
        compiler_params=pltpu.CompilerParams(
            collective_id=0, has_side_effects=True, vmem_limit_bytes=56 * 1024 * 1024
        ),
        name="whole",
    )(queries, keys, values, grad_out, delta, doc_lengths[None])


def settle_kernel(*refs):
    count = len(refs) // 2
    sems = refs[-1]
    copies = [
        pltpu.make_async_copy(refs[one], refs[count + one], sems.at[one]) for one in range(count)
    ]
    for copy in copies:
        copy.start()
    for copy in copies:
        copy.wait()


def settled(*arrays):
    return pl.pallas_call(
        settle_kernel,
        out_shape=tuple(jax.ShapeDtypeStruct(a.shape, a.dtype) for a in arrays),
        in_specs=[ANYWHERE] * len(arrays),
        out_specs=(ANYWHERE,) * len(arrays),
        scratch_shapes=[pltpu.SemaphoreType.DMA((len(arrays),))],
        name="settle",
    )(*arrays)


def on_device(queries, keys, values, grad_out, delta, doc_lengths):
    shards, peers = lax.axis_size("ctx"), lax.axis_size("head")
    rows = queries.shape[0] * peers
    delta = delta.reshape(peers, delta.shape[0] // peers, delta.shape[1])
    slots = jnp.arange(doc_lengths.shape[0], dtype=jnp.int32)
    doc_starts = jnp.sum(jnp.where(slots[:, None] < slots[None, :], doc_lengths[:, None], 0), axis=0)

    def start_at(places):
        return jnp.max(
            jnp.where(doc_starts[:, None] <= places[None, :], doc_starts[:, None], 0), axis=0
        )

    last_block = lax.shift_right_logical(
        doc_starts + doc_lengths - 1, jnp.int32(BLOCK.bit_length() - 1)
    )
    fits = jnp.all(doc_starts >= short_reach(last_block, shards, rows))

    def in_one(*operands):
        return whole(shards, halo_plan(shards, rows, True), *operands, doc_lengths)

    def in_three(*operands):
        plan = halo_plan(shards, rows, False)
        base = lax.axis_index("ctx") * rows
        starts = start_at(base + jnp.arange(rows, dtype=jnp.int32)) - (base - REACH * rows - TILE)
        q, k, v, g, d = gather(shards, plan, *operands)
        dq, dk, dv = attention(starts[::TILE], q, g, k, v, d, starts[None])
        return scatter(shards, plan, peers, dq, dk, dv)

    return settled(*lax.cond(fits, in_one, in_three, queries, keys, values, grad_out, delta))


def solution(mesh):
    rows = P(("ctx", "head"), None)
    return jax.shard_map(
        on_device,
        mesh=mesh,
        in_specs=(rows, rows, rows, rows, P(None, ("ctx", "head")), P()),
        out_specs=(rows, rows, rows),
        check_vma=False,
    )
```
